32 devices in a mesh: gx: 4 (over z), gy: 8 (over y, x, core).
Axes of the slice: x: 2, y: 2, z: 4, core: 2. Of those that a mesh axis runs over, the one named last changes fastest.
Arguments:
- patches: bfloat16 [39168, 768], P(('gx', 'gy')), may hold values from -6 to 6
- lengths: int32 [32], P(('gx', 'gy')), may hold values from 122 to 1224, as said below
- cotangent: bfloat16 [39168, 768], P(('gx', 'gy')), may hold values from -6 to 6
- w_qkv: bfloat16 [768, 2304], P('gx', 'gy'), may hold values from -0.21875 to 0.21875
- w_out: bfloat16 [768, 768], P('gx', 'gy'), may hold values from -4 to 4
- w_up: bfloat16 [768, 3072], P('gx', 'gy'), may hold values from -0.21875 to 0.21875
- w_down: bfloat16 [3072, 768], P('gx', 'gy'), may hold values from -0.109375 to 0.109375
- bias_q: bfloat16 [768], P(('gx', 'gy')), may hold values from -3 to 3
- bias_v: bfloat16 [768], P(('gx', 'gy')), may hold values from -3 to 3
- bias_o: bfloat16 [768], P(('gx', 'gy')), may hold values from -1.75 to 1.75
- bias_up: bfloat16 [3072], P(('gx', 'gy')), may hold values from -3 to 3
- bias_down: bfloat16 [768], P(('gx', 'gy')), may hold values from -1.75 to 1.75
- gain_one: bfloat16 [768], P(('gx', 'gy')), may hold values from 0.5 to 1.5
- shift_one: bfloat16 [768], P(('gx', 'gy')), may hold values from -1.75 to 1.75
- gain_two: bfloat16 [768], P(('gx', 'gy')), may hold values from 0.5 to 1.5
- shift_two: bfloat16 [768], P(('gx', 'gy')), may hold values from -1.75 to 1.75
Outputs:
- out_rows: bfloat16 [39168, 768], P(('gx', 'gy'))
- grad_rows: float32 [39168, 768], P(('gx', 'gy'))
- grad_w_qkv: float32 [768, 2304], P('gx', 'gy')
- grad_w_out: float32 [768, 768], P('gx', 'gy')
- grad_w_up: float32 [768, 3072], P('gx', 'gy')
- grad_w_down: float32 [3072, 768], P('gx', 'gy')
- grad_bias_q: float32 [768], P(('gx', 'gy'))
- grad_bias_v: float32 [768], P(('gx', 'gy'))
- grad_bias_o: float32 [768], P(('gx', 'gy'))
- grad_bias_up: float32 [3072], P(('gx', 'gy'))
- grad_bias_down: float32 [768], P(('gx', 'gy'))
- grad_gain_one: float32 [768], P(('gx', 'gy'))
- grad_shift_one: float32 [768], P(('gx', 'gy'))
- grad_gain_two: float32 [768], P(('gx', 'gy'))
- grad_shift_two: float32 [768], P(('gx', 'gy'))
The draws below stay inside these ranges and needn't reach their ends.
Inputs may be any that keep to these rules, and one draw needn't show every extreme that they name: `lengths`: each clip's true patch count; some clip fills all 1224 slots and some clip has 122 patches in every draw.
All inputs are finite; a program needn't handle non-finite values.
Results may differ from the reference program's by a relative error of at most 0.02.
Values may be sent and summed in bfloat16 or wider, within the bound.
No kernel may reach another device: no remote copies, remote signals or barrier semaphores. Data moves between devices by JAX's collectives and lax.ppermute only.
A program may use at most 192 MiB of HBM per device.

```python
import jax
import jax.numpy as jnp
from jax import lax

HEADS = 12
HEAD_DIM = 64
FF = 3072
D = 768
SLOTS = 1224
CLIPS = 32
TOKENS = 39168


def draw_lengths(key, part):
    base_len = jax.random.randint(jax.random.fold_in(key, 11), (CLIPS,), SLOTS // 10, SLOTS + 1)
    full_pick = jax.random.randint(jax.random.fold_in(key, 12), (), 0, CLIPS)
    short_step = jax.random.randint(jax.random.fold_in(key, 13), (), 1, CLIPS)
    short_pick = (full_pick + short_step) % CLIPS
    positions = jnp.arange(CLIPS)
    result = jnp.where(positions == full_pick, SLOTS, base_len)
    result = jnp.where(positions == short_pick, SLOTS // 10, result)
    return result.astype(jnp.int32)


def strengthened(values, stream_key, source, target, parts, factor):
    owner, partner = [(jnp.arange(values.shape[dim]) // (values.shape[dim] // parts)).reshape([-1 if axis == dim else 1 for axis in range(values.ndim)]) for dim in (source, target)]
    chosen = jax.random.permutation(stream_key, parts)[partner]
    strong = (owner == chosen) | (owner == (partner + parts // 2) % parts)
    return jnp.where(strong, factor * values, values)


def steps_of(rng, shape, shards, low, largest):
    gain = 1.0
    for axis_at, blocks in shards:
        steps = jax.random.uniform(jax.random.fold_in(jax.random.fold_in(rng, 6), axis_at), (blocks,), jnp.float32, low / len(shards), largest / len(shards))
        gain = gain * jnp.repeat(jnp.exp(steps), shape[axis_at] // blocks).reshape((-1,) + (1,) * (len(shape) - 1 - axis_at))
    return gain


def noise(rng, shape, scale, limit, split=(), held_as=jnp.bfloat16):
    entries = jax.random.normal(rng, shape, jnp.float32) * scale
    if len(split) > 0:
        entries = steps_of(rng, shape, split, -0.22, 0.18) * entries
    return jnp.clip(entries, min=-limit, max=limit).astype(held_as)


def heavy_noise(stream_key, extent, scale, bound, cuts, heavy, dtype=jnp.bfloat16):
    values = scale * jax.random.normal(stream_key, extent, jnp.float32)
    if cuts:
        values = values * steps_of(stream_key, extent, cuts, -0.22, 0.18)
    return jnp.clip(strengthened(values, jax.random.fold_in(stream_key, 3), *heavy), -bound, bound).astype(dtype)


def setup_inputs(seed: int = 0) -> dict:
    seeds = jax.random.split(jax.random.key(seed), 17)
    return {
        "patches": noise(seeds[0], (TOKENS, D), 1.0, 6.0, ((0, 32),)),
        "lengths": draw_lengths(jax.random.fold_in(seeds[16], 71), 0),
        "cotangent": heavy_noise(seeds[2], (TOKENS, D), 1.0, 6.0, ((0, 32),), (0, 1, 32, 2.75)),
        "w_qkv": noise(seeds[3], (D, 3 * D), D ** -0.5, 0.21875, ((0, 4), (1, 8))),
        "w_out": noise(seeds[4], (D, D), (max(D * 4 // SLOTS, 1)) ** -0.5, 4.0, ((0, 4), (1, 8))),
        "w_up": noise(seeds[5], (D, FF), D ** -0.5, 0.21875, ((0, 4), (1, 8))),
        "w_down": noise(seeds[6], (FF, D), FF ** -0.5, 0.109375, ((0, 4), (1, 8))),
        "bias_q": noise(seeds[7], (D,), 0.5, 3.0, ((0, 32),)),
        "bias_v": noise(seeds[8], (D,), 0.5, 3.0, ((0, 32),)),
        "bias_o": noise(seeds[9], (D,), 0.3, 1.75, ((0, 32),)),
        "bias_up": noise(seeds[10], (FF,), 0.5, 3.0, ((0, 32),)),
        "bias_down": noise(seeds[11], (D,), 0.3, 1.75, ((0, 32),)),
        "gain_one": jnp.clip(1.0 + 0.1 * jax.random.normal(seeds[12], (D,), jnp.float32), 0.5, 1.5).astype(jnp.bfloat16),
        "shift_one": noise(seeds[13], (D,), 0.3, 1.75, ((0, 32),)),
        "gain_two": jnp.clip(1.0 + 0.1 * jax.random.normal(seeds[14], (D,), jnp.float32), 0.5, 1.5).astype(jnp.bfloat16),
        "shift_two": noise(seeds[15], (D,), 0.3, 1.75, ((0, 32),)),
    }


EPSILON = 1e-06
NEG_FILL = -1e+30

@jax.custom_vjp
def low(v):
    return lax.optimization_barrier(v.astype(jnp.bfloat16)).astype(jnp.float32)

@jax.custom_vjp
def low_back(v):
    return v

def low_keep(v):
    return (low(v), None)

def low_pass(kept, grad):
    return (grad,)

def back_keep(v):
    return (v, None)

def back_low(kept, grad):
    return (low(grad),)
low.defvjp(low_keep, low_pass)
low_back.defvjp(back_keep, back_low)

def matmul_hi(left_side, right_side):
    return jnp.dot(left_side, right_side, precision=lax.Precision.HIGHEST, preferred_element_type=jnp.float32)

def layer_norm(values, gain_vec, shift_vec):
    centre = values - lax.optimization_barrier(jnp.mean(values, axis=-1, keepdims=True))
    spread = lax.optimization_barrier(jnp.mean(centre * centre, axis=-1, keepdims=True))
    return centre * lax.rsqrt(spread + EPSILON) * gain_vec + shift_vec

def clip_forward(params, patch_rows, length):
    w_qkv, w_out, w_up, w_down, bias_q, bias_v, bias_o, bias_up, bias_down, gain_one, shift_one, gain_two, shift_two = params
    normed = low(layer_norm(patch_rows, gain_one, shift_one))
    bias_all = jnp.concatenate([bias_q, jnp.zeros_like(bias_q), bias_v])
    project = low_back(low(matmul_hi(normed, w_qkv) + bias_all))
    heads_all = jnp.transpose(project.reshape(SLOTS, 3, HEADS, HEAD_DIM), (1, 2, 0, 3))
    scores = jnp.einsum('hqd,hkd->hqk', heads_all[0], heads_all[1], precision=lax.Precision.HIGHEST) * HEAD_DIM ** (-0.5)
    scores = low_back(scores)
    live_keys = jnp.arange(SLOTS) < length
    scores = jnp.where(live_keys[None, None, :], scores, NEG_FILL)
    maximum = lax.optimization_barrier(jnp.max(scores, axis=-1, keepdims=True))
    exponent = jnp.exp(scores - maximum)
    weights = exponent / lax.optimization_barrier(jnp.sum(exponent, axis=-1, keepdims=True))
    mixed = jnp.einsum('hqk,hkd->qhd', low(weights), heads_all[2], precision=lax.Precision.HIGHEST)
    mixed = low_back(low(mixed.reshape(SLOTS, HEADS * HEAD_DIM)))
    residual = patch_rows + low_back(matmul_hi(mixed, w_out)) + bias_o
    normed_two = low(layer_norm(residual, gain_two, shift_two))
    inner_pre = low_back(matmul_hi(normed_two, w_up) + bias_up)
    active = low(jax.nn.gelu(inner_pre, approximate=False))
    return residual + matmul_hi(active, w_down) + bias_down

def forward(patch_rows, params, lengths):
    clip_rows = patch_rows.reshape(CLIPS, SLOTS, D)
    per_clip = jax.checkpoint(lambda clip_pair: clip_forward(params, clip_pair[0], clip_pair[1]))
    return lax.map(per_clip, (clip_rows, lengths)).reshape(CLIPS * SLOTS, D)

def reference(patches, lengths, cotangent, w_qkv, w_out, w_up, w_down, bias_q, bias_v, bias_o, bias_up, bias_down, gain_one, shift_one, gain_two, shift_two):
    params = tuple((weight_in.astype(jnp.float32) for weight_in in (w_qkv, w_out, w_up, w_down, bias_q, bias_v, bias_o, bias_up, bias_down, gain_one, shift_one, gain_two, shift_two)))

    def whole_layer(rows_in, params_in):
        return forward(rows_in, params_in, lengths)
    outputs, pullback = jax.vjp(whole_layer, patches.astype(jnp.float32), params)
    live_rows = (jnp.arange(SLOTS)[None, :] < lengths[:, None]).astype(jnp.float32).reshape(CLIPS * SLOTS, 1)
    grad_rows, grad_all = pullback(cotangent.astype(jnp.float32) * live_rows)
    return (outputs.astype(jnp.bfloat16), grad_rows, grad_all[0], grad_all[1], grad_all[2], grad_all[3], grad_all[4], grad_all[5], grad_all[6], grad_all[7], grad_all[8], grad_all[9], grad_all[10], grad_all[11], grad_all[12])
```

```python
import functools

import jax
import jax.numpy as jnp
from jax import lax
from jax.experimental import pallas as pl
from jax.experimental.pallas import tpu as pltpu
from jax.sharding import PartitionSpec as P

HEADS = 12
HEAD_DIM = 64
PAIR = 2 * HEAD_DIM
EPSILON = 1e-06
NEG_FILL = -1e30
BF = jnp.bfloat16
F32 = jnp.float32
AXES = ("gx", "gy")
BLOCKS = 8
AUX = 8
VMEM_BYTES = 60 << 20
MASKS_A = (0, 2, 4, 6, 1, 3, 5, 7)
MASKS_B = (0, 4, 2, 6, 1, 5, 3, 7)
ANY = pl.BlockSpec(memory_space=pl.ANY)


def nt(left, right):
    return lax.dot_general(left, right, (((1,), (1,)), ((), ())), preferred_element_type=F32)


def nn(left, right):
    return lax.dot_general(left, right, (((1,), (0,)), ((), ())), preferred_element_type=F32)


def tn(left, right):
    return lax.dot_general(left, right, (((0,), (0,)), ((), ())), preferred_element_type=F32)


def params(**extra):
    return pltpu.CompilerParams(vmem_limit_bytes=VMEM_BYTES, **extra)


def cost(flops, bytes_moved, transcendentals=0):
    return pl.CostEstimate(
        flops=int(flops), bytes_accessed=int(bytes_moved), transcendentals=int(transcendentals)
    )


def whole(shape):
    return pl.BlockSpec(shape, lambda *_: (0,) * len(shape))


def normalise(values):
    centre = values - jnp.mean(values, axis=-1, keepdims=True)
    spread = jnp.mean(centre * centre, axis=-1, keepdims=True)
    scale = lax.rsqrt(spread + EPSILON)
    return centre * scale, scale


def norm_back(grads, nhat, scale, gain):
    e = grads * gain
    return scale * (
        e
        - jnp.mean(e, axis=-1, keepdims=True)
        - nhat * jnp.mean(e * nhat, axis=-1, keepdims=True)
    )


def arrange_qkv_kernel(pos, *refs):
    pieces, (first_ref, second_ref), stacked = refs[:4], refs[4:6], refs[6]
    width, columns = first_ref.shape[1], pieces[0].shape[1]
    rows = width // 4
    vec_rows = []
    for k in range(4):
        place = pos[0] ^ k
        stacked[pl.ds(pl.multiple_of(place * rows, 8), rows), :] = pieces[k][0:rows, :].astype(F32)
        vec_rows.append(pieces[k][rows : rows + 1, :].astype(F32))
    turned = stacked[...].T.astype(BF)
    half = columns // 2
    first_ref[0:half, :] = turned[0:half]
    second_ref[0:half, :] = turned[half:columns]
    vec = jnp.concatenate(vec_rows, axis=0).astype(BF)
    lane = lax.broadcasted_iota(jnp.int32, (columns, width), 1)
    source = lax.broadcasted_iota(jnp.int32, (columns, width), 0)
    lane4 = lax.broadcasted_iota(jnp.int32, (4, width), 1)
    order = lax.broadcasted_iota(jnp.int32, (4, 1), 0)
    piece = width // (4 * BLOCKS)
    device = (pos[0] ^ order) * BLOCKS + pos[1]
    rows_out = []
    for j in range(8):
        pick = (source == piece * j + lane % piece).astype(BF)
        spread = nn(vec, pick)
        rows_out.append(
            jnp.sum(jnp.where(lane4 // piece == device, spread, 0.0), axis=0, keepdims=True)
        )
    first_ref[half : half + AUX, :] = jnp.concatenate(rows_out, axis=0).astype(BF)
    pick = (source == piece * 8 + lane % (4 * piece)).astype(BF)
    spread = jnp.where(lane4 // (4 * piece) == pos[1], nn(vec, pick), 0.0)
    rows_up = []
    for row in range(4):
        rows_up.append(
            jnp.sum(jnp.where((pos[0] ^ order) == row, spread, 0.0), axis=0, keepdims=True)
        )
    rows_up.append(jnp.zeros((AUX - 4, width), F32))
    second_ref[half : half + AUX, :] = jnp.concatenate(rows_up, axis=0).astype(BF)


def arrange_qkv(pos, pieces, width):
    rows, columns = pieces[0].shape
    out = jax.ShapeDtypeStruct((columns // 2 + AUX, width), BF)
    return pl.pallas_call(
        arrange_qkv_kernel,
        grid_spec=pltpu.PrefetchScalarGridSpec(
            num_scalar_prefetch=1,
            grid=(1,),
            in_specs=[whole((rows, columns))] * 4,
            out_specs=[whole(out.shape)] * 2,
            scratch_shapes=[pltpu.VMEM((width, columns), F32)],
        ),
        out_shape=[out, out],
        compiler_params=params(),
        cost_estimate=cost(4e6, 4 * rows * columns * 2 * 2),
        name="arrange_qkv",
    )(pos, *pieces)


def arrange_rest_kernel(pos, *refs):
    pieces, (first_ref, second_ref), up_all, out_all = refs[:4], refs[4:6], refs[6], refs[7]
    width = first_ref.shape[1]
    rows = width // 4
    wide, narrow = up_all.shape[1], out_all.shape[1]
    for k in range(4):
        place = pos[0] ^ k
        start = pl.multiple_of(place * rows, 8)
        up_all[pl.ds(start, rows), :] = pieces[k][:, 0:wide].astype(F32)
        out_all[pl.ds(start, rows), :] = pieces[k][:, 2 * wide : 2 * wide + narrow].astype(F32)
        down = pieces[k][:, wide : 2 * wide]
        at = pl.multiple_of(narrow // 2 + place * narrow, 16)
        second_ref[pl.ds(at, narrow), 0 : width // 2] = down[0:narrow]
        second_ref[pl.ds(at, narrow), width // 2 : width] = down[narrow : 2 * narrow]
    first_ref[0:wide, :] = up_all[...].T.astype(BF)
    turned = out_all[...].T.astype(BF)
    first_ref[wide : wide + narrow // 2, :] = turned[0 : narrow // 2]
    second_ref[0 : narrow // 2, :] = turned[narrow // 2 : narrow]


def arrange_rest(pos, pieces, width, wide, narrow):
    out = jax.ShapeDtypeStruct((wide + narrow // 2, width), BF)
    return pl.pallas_call(
        arrange_rest_kernel,
        grid_spec=pltpu.PrefetchScalarGridSpec(
            num_scalar_prefetch=1,
            grid=(1,),
            in_specs=[whole(pieces[0].shape)] * 4,
            out_specs=[whole(out.shape)] * 2,
            scratch_shapes=[pltpu.VMEM((width, wide), F32), pltpu.VMEM((width, narrow), F32)],
        ),
        out_shape=[out, out],
        compiler_params=params(),
        cost_estimate=cost(1e6, out.shape[0] * width * 2 * 4),
        name="arrange_rest",
    )(pos, *pieces)


def qkv_copies(table, halves, weights, sems):
    step = weights.shape[0] // (2 * BLOCKS)
    copies = []
    for j in range(2 * BLOCKS):
        source = halves[j // 2]
        size = source.shape[0] // 2
        copies.append(
            pltpu.make_async_copy(
                source.at[pl.ds((j % 2) * size, step)],
                weights.at[pl.ds(pl.multiple_of(table[j] * step, 16), step)],
                sems.at[j],
            )
        )
    return copies


def project_kernel(table, x_ref, *refs):
    halves, (proj_ref, normed_ref, vec_ref), (weights, aux, sems) = refs[:8], refs[8:11], refs[11:]
    j = pl.program_id(0)
    half = weights.shape[0] // (2 * BLOCKS)
    tile = proj_ref.shape[1]
    width = x_ref.shape[1]

    @pl.when(j == 0)
    def _():
        small = []
        for i in range(2 * BLOCKS):
            source = halves[i // 2]
            size = source.shape[0] // 2
            small.append(
                pltpu.make_async_copy(
                    source.at[pl.ds((i % 2) * size + half, AUX)],
                    aux.at[i],
                    sems.at[2 * BLOCKS + i],
                )
            )
        large = qkv_copies(table, halves, weights, sems)
        for copy in small + large:
            copy.start()
        nhat, _ = normalise(x_ref[...].astype(F32))
        for copy in small:
            copy.wait()
        vec_ref[0:AUX, :] = jnp.sum(aux[0:BLOCKS].astype(F32), axis=0)
        vec_ref[AUX : 2 * AUX, :] = jnp.sum(aux[BLOCKS : 2 * BLOCKS].astype(F32), axis=0)
        normed_ref[...] = (nhat * vec_ref[4:5, :] + vec_ref[5:6, :]).astype(BF)
        for copy in large:
            copy.wait()

    per = width // tile
    start = pl.multiple_of(j * tile, tile)
    lanes = pl.ds(pl.multiple_of(lax.rem(j, per) * tile, tile), tile)
    section = j // per
    bias = jnp.where(
        section == 0, vec_ref[0:1, lanes], jnp.where(section == 2, vec_ref[1:2, lanes], 0.0)
    )
    proj_ref[...] = (nt(normed_ref[...], weights[pl.ds(start, tile), :]) + bias).astype(BF)


def project(table, x, halves, tile=256):
    slots, width = x.shape
    columns = 3 * width
    return pl.pallas_call(
        project_kernel,
        grid_spec=pltpu.PrefetchScalarGridSpec(
            num_scalar_prefetch=1,
            grid=(columns // tile,),
            in_specs=[whole((slots, width))] + [ANY] * 8,
            out_specs=[
                pl.BlockSpec((slots, tile), lambda j, _: (0, j)),
                whole((slots, width)),
                whole((2 * AUX, width)),
            ],
            scratch_shapes=[
                pltpu.VMEM((columns, width), BF),
                pltpu.VMEM((2 * BLOCKS, AUX, width), BF),
                pltpu.SemaphoreType.DMA((4 * BLOCKS,)),
            ],
        ),
        out_shape=[
            jax.ShapeDtypeStruct((slots, columns), BF),
            jax.ShapeDtypeStruct((slots, width), BF),
            jax.ShapeDtypeStruct((2 * AUX, width), F32),
        ],
        compiler_params=params(),
        cost_estimate=cost(2 * slots * width * columns, slots * width * 10),
        name="project",
    )(table, x, *halves)


def attend_kernel(len_ref, q_ref, k_ref, v_ref, o_ref, lse_ref, qp, *, slots, padded):
    length = len_ref[0]
    lane = lax.broadcasted_iota(jnp.int32, (slots, PAIR), 1)
    row = lax.broadcasted_iota(jnp.int32, (slots, PAIR), 0)
    bias = jnp.where(row < length, 0.0, NEG_FILL)
    keys = k_ref[...].astype(F32)
    values = v_ref[...].astype(F32)
    queries = q_ref[...].astype(F32) * HEAD_DIM**-0.5
    outs = []
    for h in range(2):
        mine = (lane // HEAD_DIM) == h
        spare = (1 - h) * HEAD_DIM
        flag = lane == spare
        key_ext = jnp.where(mine, keys, jnp.where(flag, bias, 0.0)).astype(BF)
        value_ext = jnp.where(mine, values, jnp.where(flag, 1.0, 0.0)).astype(BF)
        qp[h, 0:slots, :] = jnp.where(mine, queries, jnp.where(flag, 1.0, 0.0)).astype(BF)
        if padded > slots:
            qp[h, slots:padded, :] = jnp.zeros((padded - slots, PAIR), BF)
        scores = nt(key_ext, qp[h])
        top = jnp.max(scores, axis=0, keepdims=True)
        weights = jnp.exp(scores - top).astype(BF)
        mixed = nn(value_ext.T, weights)
        total = mixed[spare : spare + 1, :]
        outs.append(mixed[h * HEAD_DIM : (h + 1) * HEAD_DIM, :] / total)
        lse_ref[0, h : h + 1, :] = top + jnp.log(total)
    o_ref[...] = jnp.concatenate(outs, axis=0).T[0:slots].astype(BF)


def attend(length, proj):
    slots = proj.shape[0]
    padded = -(-slots // 128) * 128
    width = proj.shape[1] // 3
    pairs = width // PAIR

    def spec(off):
        return pl.BlockSpec((slots, PAIR), lambda p, _: (0, off + p))

    return pl.pallas_call(
        functools.partial(attend_kernel, slots=slots, padded=padded),
        grid_spec=pltpu.PrefetchScalarGridSpec(
            num_scalar_prefetch=1,
            grid=(pairs,),
            in_specs=[spec(0), spec(pairs), spec(2 * pairs)],
            out_specs=[spec(0), pl.BlockSpec((1, 8, padded), lambda p, _: (p, 0, 0))],
            scratch_shapes=[pltpu.VMEM((2, padded, PAIR), BF)],
        ),
        out_shape=[
            jax.ShapeDtypeStruct((slots, width), BF),
            jax.ShapeDtypeStruct((pairs, 8, padded), F32),
        ],
        compiler_params=params(),
        cost_estimate=cost(
            2 * pairs * 8 * slots * slots * PAIR, slots * width * 8, 2 * pairs * slots * slots
        ),
        name="attend",
    )(length, proj, proj, proj)


def parts(values):
    high = values.astype(BF).astype(F32)
    rest = values - high
    mid = rest.astype(BF).astype(F32)
    return high, mid, (rest - mid).astype(BF).astype(F32)


def attend_back_kernel(
    len_ref,
    q_ref,
    k_ref,
    v_ref,
    g_ref,
    o_ref,
    lse_ref,
    dq_ref,
    dk_ref,
    dv_ref,
    qp,
    gp,
    *,
    slots,
    padded,
    tile,
):
    length = len_ref[0]
    lane = lax.broadcasted_iota(jnp.int32, (slots, PAIR), 1)
    row = lax.broadcasted_iota(jnp.int32, (slots, PAIR), 0)
    bias = jnp.where(row < length, 0.0, NEG_FILL)
    keys = k_ref[...].astype(F32)
    values = v_ref[...].astype(F32)
    queries = q_ref[...].astype(F32) * HEAD_DIM**-0.5
    grads = g_ref[...].astype(F32)
    products = grads * o_ref[...].astype(F32)
    d_queries, d_keys, d_values = [], [], []
    for h in range(2):
        mine = (lane // HEAD_DIM) == h
        spare = (1 - h) * HEAD_DIM
        flag = lane == spare
        dots = jnp.sum(jnp.where(mine, products, 0.0), axis=1, keepdims=True)
        high, mid, low = parts(-dots)
        ones = (lane >= spare) & (lane < spare + 3)
        value_ext = jnp.where(mine, values, jnp.where(ones, 1.0, 0.0)).astype(BF)
        tail = jnp.where(
            flag, high, jnp.where(lane == spare + 1, mid, jnp.where(lane == spare + 2, low, 0.0))
        )
        gp[h, 0:slots, :] = jnp.where(mine, grads, tail).astype(BF)
        key_ext = jnp.where(mine, keys, jnp.where(flag, bias, 0.0)).astype(BF)
        qp[h, 0:slots, :] = jnp.where(mine, queries, jnp.where(flag, 1.0, 0.0)).astype(BF)
        if padded > slots:
            gp[h, slots:padded, :] = jnp.zeros((padded - slots, PAIR), BF)
            qp[h, slots:padded, :] = jnp.zeros((padded - slots, PAIR), BF)
        keys_turned = key_ext.T[h * HEAD_DIM : (h + 1) * HEAD_DIM]
        d_key = d_value = None
        d_query = []
        for j in range(padded // tile):
            at = slice(j * tile, (j + 1) * tile)
            weights = jnp.exp(nt(key_ext, qp[h, at, :]) - lse_ref[0, h : h + 1, at])
            d_scores = (weights * nt(value_ext, gp[h, at, :])).astype(BF)
            more_value = nn(weights.astype(BF), gp[h, at, :])
            more_key = nn(d_scores, qp[h, at, :])
            d_value = more_value if d_value is None else d_value + more_value
            d_key = more_key if d_key is None else d_key + more_key
            d_query.append(nn(keys_turned, d_scores))
        d_queries.append(jnp.concatenate(d_query, axis=1))
        d_keys.append(d_key)
        d_values.append(d_value)
    turned = jnp.concatenate(d_queries, axis=0) * HEAD_DIM**-0.5
    dq_ref[...] = turned.T[0:slots].astype(BF)
    dk_ref[...] = jnp.where(lane < HEAD_DIM, d_keys[0], d_keys[1]).astype(BF)
    dv_ref[...] = jnp.where(lane < HEAD_DIM, d_values[0], d_values[1]).astype(BF)


def attend_back(length, proj, grads, mixed, totals, tile=256, first=0, count=None):
    slots = proj.shape[0]
    padded = -(-slots // 128) * 128
    width = proj.shape[1] // 3
    pairs = width // PAIR
    count = pairs if count is None else count

    def spec(off):
        return pl.BlockSpec((slots, PAIR), lambda p, _: (0, off + p))

    return pl.pallas_call(
        functools.partial(attend_back_kernel, slots=slots, padded=padded, tile=tile),
        grid_spec=pltpu.PrefetchScalarGridSpec(
            num_scalar_prefetch=1,
            grid=(count,),
            in_specs=[
                spec(first),
                spec(first + pairs),
                spec(first + 2 * pairs),
                spec(first),
                spec(first),
                pl.BlockSpec((1, 8, padded), lambda p, _: (first + p, 0, 0)),
            ],
            out_specs=[spec(0)] * 3,
            scratch_shapes=[pltpu.VMEM((2, padded, PAIR), BF)] * 2,
        ),
        out_shape=[jax.ShapeDtypeStruct((slots, count * PAIR), BF)] * 3,
        compiler_params=params(),
        cost_estimate=cost(
            2 * count * 20 * slots * slots * PAIR, slots * width * 16, 2 * count * slots * slots
        ),
        name="attend_back",
    )(length, proj, proj, proj, grads, mixed, totals)


def rest_copies(table, halves, w_out, w_up, w_down, sems):
    width = w_out.shape[0]
    narrow = width // BLOCKS
    wide = w_up.shape[0] // BLOCKS
    half = narrow // 2
    copies_out, copies_up, copies_down = [], [], []
    for j in range(2 * BLOCKS):
        source = halves[j // 2]
        size = source.shape[0] // 2
        base = (j % 2) * size
        block = table[j] // 2
        if j < BLOCKS:
            copies_up.append(
                pltpu.make_async_copy(
                    source.at[pl.ds(base, wide)],
                    w_up.at[pl.ds(pl.multiple_of(block * wide, 16), wide)],
                    sems.at[j],
                )
            )
            copies_out.append(
                pltpu.make_async_copy(
                    source.at[pl.ds(base + wide, half)],
                    w_out.at[pl.ds(pl.multiple_of(block * narrow, 16), half)],
                    sems.at[BLOCKS + j],
                )
            )
        else:
            copies_out.append(
                pltpu.make_async_copy(
                    source.at[pl.ds(base, half)],
                    w_out.at[pl.ds(pl.multiple_of(block * narrow + half, 16), half)],
                    sems.at[BLOCKS + j],
                )
            )
            for q in range(4):
                copies_down.append(
                    pltpu.make_async_copy(
                        source.at[pl.ds(base + half + q * narrow, narrow)],
                        w_down.at[
                            pl.ds(pl.multiple_of(block * narrow, 16), narrow),
                            pl.ds(q * width, width),
                        ],
                        sems.at[3 * BLOCKS + (j - BLOCKS) * 4 + q],
                    )
                )
    return copies_out, copies_up, copies_down


def middle_kernel(len_ref, table, x_ref, mixed_ref, cot_ref, vec_ref, *refs, chunk):
    halves = refs[:8]
    (
        out_ref,
        active_ref,
        d_inner_ref,
        normed_ref,
        d_resid_ref,
        d_branch_ref,
        d_mixed_ref,
        sums_ref,
    ) = refs[8:16]
    w_out, w_up, w_down, sems = refs[16:]
    i = pl.program_id(0)
    tile, width = x_ref.shape
    hidden = w_up.shape[0]

    copies_out, copies_up, copies_down = rest_copies(table, halves, w_out, w_up, w_down, sems)

    @pl.when(i == 0)
    def _():
        for copy in copies_out + copies_up + copies_down:
            copy.start()
        sums_ref[...] = jnp.zeros_like(sums_ref)
        for copy in copies_out:
            copy.wait()

    residual = x_ref[...].astype(F32) + nt(mixed_ref[...], w_out[...]) + vec_ref[2:3, :]
    nhat, scale = normalise(residual)
    normed = (nhat * vec_ref[6:7, :] + vec_ref[7:8, :]).astype(BF)
    normed_ref[...] = normed
    rows = lax.broadcasted_iota(jnp.int32, (tile, 1), 0) + i * tile
    seed_low = jnp.where(rows < len_ref[0], cot_ref[...], jnp.zeros_like(cot_ref))
    seed = seed_low.astype(F32)
    ones = jnp.ones((8, tile), BF)

    @pl.when(i == 0)
    def _():
        for copy in copies_up + copies_down:
            copy.wait()

    per = width // chunk

    def step(c, carry):
        out_sum, d_normed = carry
        at = pl.ds(pl.multiple_of(c * chunk, chunk), chunk)
        row = pl.ds(8 + c // per, 1)
        lanes = pl.ds(pl.multiple_of(lax.rem(c, per) * chunk, chunk), chunk)
        inner = nt(normed, w_up[at, :]) + vec_ref[row, lanes]
        cdf = 0.5 + 0.5 * lax.erf(inner * 0.5**0.5)
        active = (inner * cdf).astype(BF)
        active_ref[:, at] = active
        d_active = nn(seed_low, w_down[:, at])
        slope = cdf + inner * (jnp.exp(-0.5 * inner * inner) * 0.3989422804014327)
        d_inner = (d_active * slope).astype(BF)
        d_inner_ref[:, at] = d_inner
        sums_ref[row, lanes] += nn(ones, d_inner)[0:1]
        return (out_sum + nt(active, w_down[:, at]), d_normed + nn(d_inner, w_up[at, :]))

    zero = jnp.zeros((tile, width), F32)
    out_sum, d_normed = lax.fori_loop(0, hidden // chunk, step, (zero, zero))
    out_ref[...] = (residual + out_sum + vec_ref[3:4, :]).astype(BF)
    d_resid = seed + norm_back(d_normed, nhat, scale, vec_ref[6:7, :])
    d_resid_ref[...] = d_resid
    d_branch = d_resid.astype(BF)
    d_branch_ref[...] = d_branch
    d_mixed_ref[...] = nn(d_branch, w_out[...]).astype(BF)
    sums_ref[2:3, :] += jnp.sum(d_resid, axis=0, keepdims=True)
    sums_ref[3:4, :] += jnp.sum(seed, axis=0, keepdims=True)
    sums_ref[6:7, :] += jnp.sum(d_normed * nhat, axis=0, keepdims=True)
    sums_ref[7:8, :] += jnp.sum(d_normed, axis=0, keepdims=True)


def middle(length, table, x, mixed, cot, vec, halves, hidden, tile, chunk=768):
    slots, width = x.shape

    def rows(columns):
        return pl.BlockSpec((tile, columns), lambda i, *_: (i, 0))

    return pl.pallas_call(
        functools.partial(middle_kernel, chunk=chunk),
        grid_spec=pltpu.PrefetchScalarGridSpec(
            num_scalar_prefetch=2,
            grid=(slots // tile,),
            in_specs=[rows(width)] * 3 + [whole(vec.shape)] + [ANY] * 8,
            out_specs=[
                rows(width),
                rows(hidden),
                rows(hidden),
                rows(width),
                rows(width),
                rows(width),
                rows(width),
                whole(vec.shape),
            ],
            scratch_shapes=[
                pltpu.VMEM((width, width), BF),
                pltpu.VMEM((hidden, width), BF),
                pltpu.VMEM((width, hidden), BF),
                pltpu.SemaphoreType.DMA((7 * BLOCKS,)),
            ],
        ),
        out_shape=[
            jax.ShapeDtypeStruct((slots, width), BF),
            jax.ShapeDtypeStruct((slots, hidden), BF),
            jax.ShapeDtypeStruct((slots, hidden), BF),
            jax.ShapeDtypeStruct((slots, width), BF),
            jax.ShapeDtypeStruct((slots, width), F32),
            jax.ShapeDtypeStruct((slots, width), BF),
            jax.ShapeDtypeStruct((slots, width), BF),
            jax.ShapeDtypeStruct(vec.shape, F32),
        ],
        compiler_params=params(),
        cost_estimate=cost(
            2 * slots * width * (4 * hidden + 2 * width),
            slots * (hidden * 4 + width * 18) + hidden * width * 4,
            2 * slots * hidden,
        ),
        name="middle",
    )(length, table, x, mixed, cot, vec, *halves)


def rest_grads_kernel(
    len_ref,
    table,
    active_ref,
    d_inner_ref,
    normed_ref,
    cot_ref,
    d_branch_ref,
    mixed_ref,
    keep_ref,
    send_ref,
    sums,
    sems,
):
    z = pl.program_id(0)
    slots, width = normed_ref.shape
    narrow = width // BLOCKS
    wide = sums.shape[1] // 2 - narrow // 2
    rows = lax.broadcasted_iota(jnp.int32, (slots, 1), 0)
    seed = jnp.where(rows < len_ref[0], cot_ref[...], jnp.zeros_like(cot_ref))
    up = tn(d_inner_ref[...], normed_ref[...]).astype(BF)
    per = width // wide
    for j in range(per):
        sums[z * per + j, 0:wide, :] = up[j * wide : (j + 1) * wide]
    down = tn(seed, active_ref[...]).astype(BF)
    at = pl.ds(pl.multiple_of(wide + narrow + z * narrow, 16), narrow)
    for g in range(BLOCKS):
        sums[g, at, :] = down[g * narrow : (g + 1) * narrow]

    @pl.when(z == 0)
    def _():
        out = tn(d_branch_ref[...], mixed_ref[...]).astype(BF)
        for g in range(BLOCKS):
            sums[g, wide : wide + narrow, :] = out[g * narrow : (g + 1) * narrow]

    @pl.when(z == pl.num_programs(0) - 1)
    def _():
        copies = []
        for j in range(BLOCKS):
            target = keep_ref if j < BLOCKS // 2 else send_ref
            copies.append(
                pltpu.make_async_copy(
                    sums.at[table[j] // 2], target.at[j % (BLOCKS // 2)], sems.at[j]
                )
            )
        for copy in copies:
            copy.start()
        for copy in copies:
            copy.wait()


def rest_grads(length, table, active, d_inner, normed, cot, d_branch, mixed):
    slots, width = normed.shape
    hidden = active.shape[1]
    rows = 2 * (hidden // BLOCKS) + width // BLOCKS
    out = jax.ShapeDtypeStruct((BLOCKS // 2, rows, width), BF)
    return pl.pallas_call(
        rest_grads_kernel,
        grid_spec=pltpu.PrefetchScalarGridSpec(
            num_scalar_prefetch=2,
            grid=(hidden // width,),
            in_specs=[pl.BlockSpec((slots, width), lambda z, *_: (0, z))] * 2
            + [whole((slots, width))] * 4,
            out_specs=[ANY] * 2,
            scratch_shapes=[
                pltpu.VMEM((BLOCKS, rows, width), BF),
                pltpu.SemaphoreType.DMA((BLOCKS,)),
            ],
        ),
        out_shape=[out, out],
        compiler_params=params(),
        cost_estimate=cost(
            2 * slots * width * (2 * hidden + width), slots * hidden * 4 + out.size * 4
        ),
        name="rest_grads",
    )(length, table, active, d_inner, normed, cot, d_branch, mixed)


def qkv_grads_kernel(table, dq_ref, dk_ref, dv_ref, normed_ref, keep_ref, send_ref, sums, sems):
    width = normed_ref.shape[1]
    block = sums.shape[0] // BLOCKS
    for s, ref in enumerate((dq_ref, dk_ref, dv_ref)):
        sums[s * width : (s + 1) * width, :] = tn(ref[...], normed_ref[...]).astype(BF)
    copies = []
    for j in range(BLOCKS):
        target = keep_ref if j < BLOCKS // 2 else send_ref
        at = pl.ds(pl.multiple_of(table[j] // 2 * block, 16), block)
        copies.append(
            pltpu.make_async_copy(sums.at[at], target.at[j % (BLOCKS // 2)], sems.at[j])
        )
    for copy in copies:
        copy.start()
    for copy in copies:
        copy.wait()


def qkv_grads(table, d_parts, normed):
    slots, width = normed.shape
    out = jax.ShapeDtypeStruct((BLOCKS // 2, 3 * width // BLOCKS, width), BF)
    return pl.pallas_call(
        qkv_grads_kernel,
        grid_spec=pltpu.PrefetchScalarGridSpec(
            num_scalar_prefetch=1,
            grid=(1,),
            in_specs=[whole((slots, width))] * 4,
            out_specs=[ANY] * 2,
            scratch_shapes=[
                pltpu.VMEM((3 * width, width), BF),
                pltpu.SemaphoreType.DMA((BLOCKS,)),
            ],
        ),
        out_shape=[out, out],
        compiler_params=params(),
        cost_estimate=cost(6 * slots * width * width, slots * width * 8 + out.size * 4),
        name="qkv_grads",
    )(table, *d_parts, normed)


def last_kernel(
    table, dq_ref, dk_ref, dv_ref, x_ref, d_resid_ref, vec_ref, sums_in, *refs
):
    halves, (grad_ref, sums_ref), (weights, sems) = refs[:8], refs[8:10], refs[10:]
    i = pl.program_id(0)
    tile, width = x_ref.shape
    copies = qkv_copies(table, halves, weights, sems)

    @pl.when(i == 0)
    def _():
        for copy in copies:
            copy.start()
        sums_ref[...] = sums_in[...]
        for copy in copies:
            copy.wait()

    d_normed = nn(dq_ref[...], weights[0:width, :])
    d_normed += nn(dk_ref[...], weights[width : 2 * width, :])
    d_normed += nn(dv_ref[...], weights[2 * width : 3 * width, :])
    nhat, scale = normalise(x_ref[...].astype(F32))
    grad_ref[...] = d_resid_ref[...] + norm_back(d_normed, nhat, scale, vec_ref[4:5, :])
    ones = jnp.ones((8, tile), BF)
    sums_ref[0:1, :] += nn(ones, dq_ref[...])[0:1]
    sums_ref[1:2, :] += nn(ones, dv_ref[...])[0:1]
    sums_ref[4:5, :] += jnp.sum(d_normed * nhat, axis=0, keepdims=True)
    sums_ref[5:6, :] += jnp.sum(d_normed, axis=0, keepdims=True)


def last(table, d_parts, x, d_resid, vec, sums, halves, tile):
    slots, width = x.shape
    rows = pl.BlockSpec((tile, width), lambda i, _: (i, 0))
    return pl.pallas_call(
        last_kernel,
        grid_spec=pltpu.PrefetchScalarGridSpec(
            num_scalar_prefetch=1,
            grid=(slots // tile,),
            in_specs=[rows] * 5 + [whole(vec.shape)] * 2 + [ANY] * 8,
            out_specs=[rows, whole(vec.shape)],
            scratch_shapes=[
                pltpu.VMEM((3 * width, width), BF),
                pltpu.SemaphoreType.DMA((2 * BLOCKS,)),
            ],
        ),
        out_shape=[
            jax.ShapeDtypeStruct((slots, width), F32),
            jax.ShapeDtypeStruct(vec.shape, F32),
        ],
        compiler_params=params(),
        cost_estimate=cost(6 * slots * width * width, slots * width * 16),
        name="last",
    )(table, *d_parts, x, d_resid, vec, sums, *halves)


def swap(values, axis, mask, size):
    return lax.ppermute(values, axis, [(i, i ^ mask) for i in range(size)])


def gather_planes(message):
    return [message] + [swap(message, "gx", k, 4) for k in (1, 2, 3)]


def gather_blocks(first, second):
    from_x = swap(first, "gy", 2, BLOCKS)
    from_y = swap(second, "gy", 4, BLOCKS)
    a = jnp.concatenate([first, from_x], axis=0)
    b = jnp.concatenate([second, from_y], axis=0)
    a_y = swap(a, "gy", 4, BLOCKS)
    b_x = swap(b, "gy", 2, BLOCKS)
    a_c, b_c = swap(a, "gy", 1, BLOCKS), swap(b, "gy", 1, BLOCKS)
    a_yc, b_xc = swap(a_y, "gy", 1, BLOCKS), swap(b_x, "gy", 1, BLOCKS)
    return [a, a_y, a_c, a_yc, b, b_x, b_c, b_xc]


def add(left, right):
    return left.astype(F32) + right.astype(F32)


def scatter_blocks(keep, send):
    rows = keep.shape[1]
    half = rows // 2
    other = swap(send, "gy", 1, BLOCKS)

    def total(index, at):
        return add(keep[index, at], other[index, at]).astype(BF)

    top, bottom = slice(0, half), slice(half, rows)
    a_send = jnp.stack([total(2, top), total(3, top)])
    b_send = jnp.stack([total(1, bottom), total(3, bottom)])
    a_got = swap(a_send, "gy", 4, BLOCKS)
    b_got = swap(b_send, "gy", 2, BLOCKS)
    a_next = add(total(1, top), a_got[1]).astype(BF)
    b_next = add(total(2, bottom), b_got[1]).astype(BF)
    a_last = swap(a_next, "gy", 2, BLOCKS)
    b_last = swap(b_next, "gy", 4, BLOCKS)
    a = add(add(total(0, top), a_got[0]), a_last)
    b = add(add(total(0, bottom), b_got[0]), b_last)
    return jnp.concatenate([a, b], axis=0)


def scatter_planes(stacked):
    z = lax.axis_index("gx")
    mine = lax.dynamic_index_in_dim(stacked, z, 0, keepdims=False)
    low = stacked.astype(BF)
    total = mine.astype(F32)
    for k in (1, 2, 3):
        piece = lax.dynamic_index_in_dim(low, z ^ k, 0, keepdims=False)
        total = total + swap(piece, "gx", k, 4).astype(F32)
    return total


def per_device(
    patches,
    lengths,
    cotangent,
    w_qkv,
    w_out,
    w_up,
    w_down,
    bias_q,
    bias_v,
    bias_o,
    bias_up,
    bias_down,
    gain_one,
    shift_one,
    gain_two,
    shift_two,
    *,
    planes,
    columns,
):
    slots, width = patches.shape
    hidden = w_up.shape[1] * columns
    wide, narrow = hidden // BLOCKS, width // BLOCKS
    tile = slots // 3
    z, g = lax.axis_index("gx"), lax.axis_index("gy")
    fast = planes == 4 and columns == BLOCKS
    vectors = (bias_q, bias_v, bias_o, bias_down, gain_one, shift_one, gain_two, shift_two)
    if fast:
        pos = jnp.stack([z, g]).astype(jnp.int32)
        table = jnp.concatenate(
            [2 * (g ^ jnp.array(MASKS_A)), 2 * (g ^ jnp.array(MASKS_B)) + 1]
        ).astype(jnp.int32)
        grad_table = (2 * (g ^ jnp.array(MASKS_A))).astype(jnp.int32)
        vec_row = jnp.concatenate(vectors + (bias_up,))[None, :]
        message = jnp.concatenate(
            [w_qkv, vec_row, jnp.zeros((AUX - 1, w_qkv.shape[1]), BF)], axis=0
        )
        pieces = gather_planes(message)
        qkv_halves = gather_blocks(*arrange_qkv(pos, pieces, width))
        turned = w_down.T
        down = jnp.concatenate([turned[:, : width // 2], turned[:, width // 2 :]], axis=0)
        message = jnp.concatenate(
            [w_up, down, w_out, jnp.zeros((width // 4, 128 - narrow), BF)], axis=1
        )
        message, pieces[1] = lax.optimization_barrier((message, pieces[1]))
        pieces = gather_planes(message)
        rest_halves = gather_blocks(*arrange_rest(pos, pieces, width, wide, narrow))
    else:

        def everything(shard):
            return lax.all_gather(
                lax.all_gather(shard, "gx", axis=0, tiled=True), "gy", axis=1, tiled=True
            ).T

        table = jnp.concatenate([2 * jnp.arange(BLOCKS), 2 * jnp.arange(BLOCKS) + 1]).astype(
            jnp.int32
        )
        grad_table = (2 * jnp.arange(BLOCKS)).astype(jnp.int32)
        rows = jnp.stack([lax.all_gather(v, AXES, axis=0, tiled=True) for v in vectors])
        up_rows = lax.all_gather(bias_up, AXES, axis=0, tiled=True).reshape(4, width)
        up_rows = jnp.concatenate([up_rows, jnp.zeros((AUX - 4, width), BF)])
        qkv = everything(w_qkv).reshape(BLOCKS, 2, -1, width)

        def with_aux(blocks, aux):
            rest = jnp.zeros((BLOCKS - 1, AUX, width), BF)
            both = jnp.concatenate([blocks, jnp.concatenate([aux[None], rest])], axis=1)
            return list(both.reshape(4, -1, width))

        qkv_halves = with_aux(qkv[:, 0], rows) + with_aux(qkv[:, 1], up_rows)
        down = everything(w_down).reshape(BLOCKS, narrow, 4, width)
        down = jnp.transpose(down, (0, 2, 1, 3)).reshape(BLOCKS, wide, width)
        rest = jnp.concatenate(
            [
                everything(w_up).reshape(BLOCKS, wide, width),
                everything(w_out).reshape(BLOCKS, narrow, width),
                down,
            ],
            axis=1,
        ).reshape(BLOCKS, 2, -1, width)
        rest_halves = list(rest[:, 0].reshape(4, -1, width)) + list(
            rest[:, 1].reshape(4, -1, width)
        )

    proj, normed, vec = project(table, patches, qkv_halves)
    mixed, totals = attend(lengths, proj)
    out_rows, active, d_inner, normed_two, d_resid, d_branch, d_mixed, sums = middle(
        lengths, table, patches, mixed, cotangent, vec, rest_halves, hidden, tile
    )
    rest_keep, rest_send = rest_grads(
        lengths, grad_table, active, d_inner, normed_two, cotangent, d_branch, mixed
    )
    d_parts = attend_back(lengths, proj, d_mixed, mixed, totals)
    qkv_keep, qkv_send = qkv_grads(grad_table, d_parts, normed)
    grad_rows, sums = last(table, d_parts, patches, d_resid, vec, sums, qkv_halves, tile)

    if fast:
        rest = scatter_blocks(rest_keep, rest_send)
        up = rest[:wide].T.reshape(4, width // 4, wide)
        out = rest[wide : wide + narrow].T.reshape(4, width // 4, narrow)
        down = jnp.transpose(rest[wide + narrow :].reshape(4, narrow, width), (0, 2, 1))
        grad_up, grad_out, grad_down = scatter_planes(up), scatter_planes(out), scatter_planes(down)
        qkv = scatter_blocks(qkv_keep, qkv_send)
        grad_qkv = scatter_planes(qkv.T.reshape(4, width // 4, -1))
        for axis, mask, size in (
            ("gy", 1, 8),
            ("gy", 2, 8),
            ("gy", 4, 8),
            ("gx", 1, 4),
            ("gx", 2, 4),
        ):
            sums = sums + swap(sums, axis, mask, size)
        device = z * columns + g
        own = lax.dynamic_slice(sums, (0, device * (narrow // 4)), (8, narrow // 4))
        own_up = lax.dynamic_slice(sums, (8 + z, g * narrow), (1, narrow))[0]
        own = [own[j] for j in range(8)]
    else:

        def spread(grads, axis_size):
            low = grads.astype(BF)
            part = lax.psum_scatter(low, "gy", scatter_dimension=0, tiled=True)
            return lax.psum_scatter(part.T, "gx", scatter_dimension=0, tiled=True).astype(F32)

        rest = jnp.concatenate([rest_keep, rest_send], axis=0)
        grad_up = spread(rest[:, :wide].reshape(hidden, width), columns)
        grad_out = spread(rest[:, wide : wide + narrow].reshape(width, width), columns)
        down = rest[:, wide + narrow :].reshape(BLOCKS, 4, narrow, width)
        grad_down = spread(jnp.transpose(down, (0, 2, 1, 3)).reshape(width, hidden), columns)
        qkv = jnp.concatenate([qkv_keep, qkv_send], axis=0).reshape(3 * width, width)
        grad_qkv = spread(qkv, columns)

        def share(vector):
            return lax.psum_scatter(vector, AXES, scatter_dimension=0, tiled=True)

        own = [share(sums[j]) for j in range(8)]
        own_up = share(sums[8:12].reshape(hidden))

    return (
        out_rows,
        grad_rows,
        grad_qkv,
        grad_out,
        grad_up,
        grad_down,
        own[0],
        own[1],
        own[2],
        own_up,
        own[3],
        own[4],
        own[5],
        own[6],
        own[7],
    )


def solution(mesh):
    by_rows = P(AXES, None)
    by_parts = P(AXES)
    matrix = P("gx", "gy")
    in_specs = (by_rows, by_parts, by_rows) + (matrix,) * 4 + (by_parts,) * 9
    out_specs = (by_rows, by_rows) + (matrix,) * 4 + (by_parts,) * 9
    body = functools.partial(per_device, planes=mesh.shape["gx"], columns=mesh.shape["gy"])
    return jax.shard_map(body, mesh=mesh, in_specs=in_specs, out_specs=out_specs, check_vma=False)
```

```python
import functools

import jax
import jax.numpy as jnp
from jax import lax
from jax.experimental import pallas as pl
from jax.experimental.pallas import tpu as pltpu
from jax.sharding import PartitionSpec as P

HEADS = 12
HEAD_DIM = 64
PAIR = 2 * HEAD_DIM
EPSILON = 1e-06
NEG_FILL = -1e30
BF = jnp.bfloat16
F32 = jnp.float32
AXES = ("gx", "gy")
BLOCKS = 8
AUX = 16
VMEM_BYTES = 60 << 20
MASKS_A = (0, 2, 4, 6, 1, 3, 5, 7)
MASKS_B = (0, 4, 2, 6, 1, 5, 3, 7)
PLANES = (0, 2, 1, 3)
ANY = pl.BlockSpec(memory_space=pl.ANY)


def nt(left, right):
    return lax.dot_general(left, right, (((1,), (1,)), ((), ())), preferred_element_type=F32)


def nn(left, right):
    return lax.dot_general(left, right, (((1,), (0,)), ((), ())), preferred_element_type=F32)


def tn(left, right):
    return lax.dot_general(left, right, (((0,), (0,)), ((), ())), preferred_element_type=F32)


def params(**extra):
    return pltpu.CompilerParams(vmem_limit_bytes=VMEM_BYTES, **extra)


def cost(flops, bytes_moved, transcendentals=0):
    return pl.CostEstimate(
        flops=int(flops), bytes_accessed=int(bytes_moved), transcendentals=int(transcendentals)
    )


def whole(shape):
    return pl.BlockSpec(shape, lambda *_: (0,) * len(shape))


def normalise(values):
    centre = values - jnp.mean(values, axis=-1, keepdims=True)
    spread = jnp.mean(centre * centre, axis=-1, keepdims=True)
    scale = lax.rsqrt(spread + EPSILON)
    return centre * scale, scale


def norm_back(grads, nhat, scale, gain):
    e = grads * gain
    return scale * (
        e
        - jnp.mean(e, axis=-1, keepdims=True)
        - nhat * jnp.mean(e * nhat, axis=-1, keepdims=True)
    )


def pack_kernel(w_ref, *refs):
    vectors, out_ref = refs[:-1], refs[-1]
    rows = w_ref.shape[0]
    out_ref[0:rows, :] = w_ref[...]
    out_ref[rows:, :] = jnp.zeros((out_ref.shape[0] - rows, out_ref.shape[1]), BF)
    pieces = [ref[...].astype(F32) for ref in vectors]
    out_ref[rows : rows + 8, :] = jnp.broadcast_to(
        jnp.concatenate(pieces, axis=1), (8, out_ref.shape[1])
    ).astype(BF)


def pack(w_qkv, vectors):
    rows, columns = w_qkv.shape
    shape = (rows + 8, columns)
    return pl.pallas_call(
        pack_kernel,
        out_shape=jax.ShapeDtypeStruct(shape, BF),
        compiler_params=params(),
        cost_estimate=cost(1e4, rows * columns * 4),
        name="pack",
    )(w_qkv, *[v[None, :] for v in vectors])


def pack_rest_kernel(up_ref, out_ref, down_ref, both_ref, turned_ref):
    wide, narrow = up_ref.shape[1], out_ref.shape[1]
    both_ref[:, 0:wide] = up_ref[...]
    both_ref[:, wide : wide + narrow] = out_ref[...]
    both_ref[:, wide + narrow :] = jnp.zeros(
        (both_ref.shape[0], both_ref.shape[1] - wide - narrow), BF
    )
    turned_ref[...] = down_ref[...].astype(F32).T.astype(BF)


def pack_rest(w_up, w_out, w_down):
    rows = w_up.shape[0]
    columns = -(-(w_up.shape[1] + w_out.shape[1]) // 128) * 128
    return pl.pallas_call(
        pack_rest_kernel,
        out_shape=[
            jax.ShapeDtypeStruct((rows, columns), BF),
            jax.ShapeDtypeStruct(w_down.shape[::-1], BF),
        ],
        compiler_params=params(),
        cost_estimate=cost(1e4, rows * columns * 4 + w_down.size * 4),
        name="pack_rest",
    )(w_up, w_out, w_down)


def arrange_qkv_kernel(pos, *refs):
    pieces, (first_ref, second_ref), stacked = refs[:4], refs[4:6], refs[6]
    width, columns = first_ref.shape[1], pieces[0].shape[1]
    half = columns // 2
    rows = width // 4
    vec_rows = []
    for k in range(4):
        place = pos[0] ^ k
        stacked[pl.ds(pl.multiple_of(place * rows, 8), rows), :] = pieces[k][0:rows, :].astype(F32)
        vec_rows.append(pieces[k][rows : rows + 1, :].astype(F32))
    turned = stacked[...].T.astype(BF)
    first_ref[0:half, :] = turned[0:half]
    second_ref[...] = turned[half:columns]
    vec = jnp.concatenate(vec_rows, axis=0).astype(BF)
    lane = lax.broadcasted_iota(jnp.int32, (columns, width), 1)
    source = lax.broadcasted_iota(jnp.int32, (columns, width), 0)
    lane4 = lax.broadcasted_iota(jnp.int32, (4, width), 1)
    order = lax.broadcasted_iota(jnp.int32, (4, 1), 0)
    piece = width // (4 * BLOCKS)
    device = (pos[0] ^ order) * BLOCKS + pos[1]
    here = lane4 // piece == device
    base = lane % piece
    rows_out = []
    for j in range(8):
        spread = nn(vec, (source == piece * j + base).astype(BF))
        rows_out.append(jnp.sum(jnp.where(here, spread, 0.0), axis=0, keepdims=True))
    pick = (source == piece * 8 + lane % (4 * piece)).astype(BF)
    spread = jnp.where(lane4 // (4 * piece) == pos[1], nn(vec, pick), 0.0)
    for row in range(4):
        rows_out.append(
            jnp.sum(jnp.where((pos[0] ^ order) == row, spread, 0.0), axis=0, keepdims=True)
        )
    rows_out.append(jnp.zeros((AUX - 12, width), F32))
    first_ref[half : half + AUX, :] = jnp.concatenate(rows_out, axis=0).astype(BF)


def arrange_qkv(pos, pieces, width):
    rows, columns = pieces[0].shape
    out = [
        jax.ShapeDtypeStruct((columns // 2 + AUX, width), BF),
        jax.ShapeDtypeStruct((columns // 2, width), BF),
    ]
    return pl.pallas_call(
        arrange_qkv_kernel,
        grid_spec=pltpu.PrefetchScalarGridSpec(
            num_scalar_prefetch=1,
            grid=(1,),
            in_specs=[whole((rows, columns))] * 4,
            out_specs=[whole(o.shape) for o in out],
            scratch_shapes=[pltpu.VMEM((width, columns), F32)],
        ),
        out_shape=out,
        compiler_params=params(),
        cost_estimate=cost(4e6, 4 * rows * columns * 2 * 2),
        name="arrange_qkv",
    )(pos, *pieces)


def arrange_rest_kernel(pos, *refs):
    pieces, (first_ref, second_ref), stacked = refs[:4], refs[4:6], refs[6]
    rows = first_ref.shape[1] // 4
    half = first_ref.shape[0]
    for k in range(4):
        start = pl.multiple_of((pos[0] ^ k) * rows, 8)
        stacked[pl.ds(start, rows), :] = pieces[k][...].astype(F32)
    turned = stacked[...].T.astype(BF)
    first_ref[...] = turned[0:half]
    second_ref[...] = turned[half : 2 * half]


def arrange_rest(pos, pieces, width, height):
    out = jax.ShapeDtypeStruct((height // 2, width), BF)
    return pl.pallas_call(
        arrange_rest_kernel,
        grid_spec=pltpu.PrefetchScalarGridSpec(
            num_scalar_prefetch=1,
            grid=(1,),
            in_specs=[whole(pieces[0].shape)] * 4,
            out_specs=[whole(out.shape)] * 2,
            scratch_shapes=[pltpu.VMEM((width, pieces[0].shape[1]), F32)],
        ),
        out_shape=[out, out],
        compiler_params=params(),
        cost_estimate=cost(1e6, out.shape[0] * width * 2 * 4),
        name="arrange_rest",
    )(pos, *pieces)


def qkv_copies(table, halves, weights, sems):
    step = weights.shape[0] // (2 * BLOCKS)
    copies = []
    for j in range(2 * BLOCKS):
        source = halves[j // 2]
        start = table[j] * (2 * step) + j // BLOCKS * step
        copies.append(
            pltpu.make_async_copy(
                source.at[pl.ds(j % 2 * (source.shape[0] // 2), step)],
                weights.at[pl.ds(pl.multiple_of(start, 16), step)],
                sems.at[j],
            )
        )
    return copies


def project_kernel(table, x_ref, *refs):
    blocks, (proj_ref, normed_ref, vec_ref), (weights, aux, sems) = refs[:8], refs[8:11], refs[11:]
    j = pl.program_id(0)
    step = weights.shape[0] // (2 * BLOCKS)
    tile = proj_ref.shape[1]
    width = x_ref.shape[1]

    @pl.when(j == 0)
    def _():
        small = [
            pltpu.make_async_copy(
                blocks[i // 2].at[pl.ds(i % 2 * (step + AUX) + step, AUX)],
                aux.at[i],
                sems.at[2 * BLOCKS + i],
            )
            for i in range(BLOCKS)
        ]
        large = qkv_copies(table, blocks, weights, sems)
        for copy in small + large:
            copy.start()
        nhat, _ = normalise(x_ref[...].astype(F32))
        for copy in small:
            copy.wait()
        vec_ref[...] = jnp.sum(aux[...].astype(F32), axis=0)
        normed_ref[...] = (nhat * vec_ref[4:5, :] + vec_ref[5:6, :]).astype(BF)
        for copy in large:
            copy.wait()

    per = width // tile
    start = pl.multiple_of(j * tile, tile)
    lanes = pl.ds(pl.multiple_of(lax.rem(j, per) * tile, tile), tile)
    section = j // per
    bias = jnp.where(
        section == 0, vec_ref[0:1, lanes], jnp.where(section == 2, vec_ref[1:2, lanes], 0.0)
    )
    proj_ref[...] = (nt(normed_ref[...], weights[pl.ds(start, tile), :]) + bias).astype(BF)


def project(table, x, blocks, tile=256):
    slots, width = x.shape
    columns = 3 * width
    return pl.pallas_call(
        project_kernel,
        grid_spec=pltpu.PrefetchScalarGridSpec(
            num_scalar_prefetch=1,
            grid=(columns // tile,),
            in_specs=[whole((slots, width))] + [ANY] * 8,
            out_specs=[
                pl.BlockSpec((slots, tile), lambda j, _: (0, j)),
                whole((slots, width)),
                whole((AUX, width)),
            ],
            scratch_shapes=[
                pltpu.VMEM((columns, width), BF),
                pltpu.VMEM((BLOCKS, AUX, width), BF),
                pltpu.SemaphoreType.DMA((3 * BLOCKS,)),
            ],
        ),
        out_shape=[
            jax.ShapeDtypeStruct((slots, columns), BF),
            jax.ShapeDtypeStruct((slots, width), BF),
            jax.ShapeDtypeStruct((AUX, width), F32),
        ],
        compiler_params=params(),
        cost_estimate=cost(2 * slots * width * columns, slots * width * 10),
        name="project",
    )(table, x, *blocks)


def attend_kernel(len_ref, q_ref, k_ref, v_ref, *refs, slots, padded):
    o_ref, lse_ref, qp = refs[-3:]
    length = len_ref[0]
    lane = lax.broadcasted_iota(jnp.int32, (slots, PAIR), 1)
    row = lax.broadcasted_iota(jnp.int32, (slots, PAIR), 0)
    bias = jnp.where(row < length, 0.0, NEG_FILL)
    keys = k_ref[...].astype(F32)
    values = v_ref[...].astype(F32)
    queries = q_ref[...].astype(F32) * HEAD_DIM**-0.5
    outs = []
    for h in range(2):
        mine = (lane // HEAD_DIM) == h
        spare = (1 - h) * HEAD_DIM
        flag = lane == spare
        key_ext = jnp.where(mine, keys, jnp.where(flag, bias, 0.0)).astype(BF)
        value_ext = jnp.where(mine, values, jnp.where(flag, 1.0, 0.0)).astype(BF)
        qp[h, 0:slots, :] = jnp.where(mine, queries, jnp.where(flag, 1.0, 0.0)).astype(BF)
        if padded > slots:
            qp[h, slots:padded, :] = jnp.zeros((padded - slots, PAIR), BF)
        scores = nt(key_ext, qp[h])
        top = jnp.max(scores, axis=0, keepdims=True)
        weights = jnp.exp(scores - top).astype(BF)
        mixed = nn(value_ext.T, weights)
        total = mixed[spare : spare + 1, :]
        outs.append(mixed[h * HEAD_DIM : (h + 1) * HEAD_DIM, :] / total)
        lse_ref[0, h : h + 1, :] = top + jnp.log(total)
    o_ref[...] = jnp.concatenate(outs, axis=0).T[0:slots].astype(BF)


def attend(length, proj, first=0, count=None, into=()):
    slots = proj.shape[0]
    padded = -(-slots // 128) * 128
    width = proj.shape[1] // 3
    pairs = width // PAIR
    count = pairs if count is None else count

    def spec(off):
        return pl.BlockSpec((slots, PAIR), lambda p, _: (0, off + first + p))

    return pl.pallas_call(
        functools.partial(attend_kernel, slots=slots, padded=padded),
        grid_spec=pltpu.PrefetchScalarGridSpec(
            num_scalar_prefetch=1,
            grid=(count,),
            in_specs=[spec(0), spec(pairs), spec(2 * pairs)] + [ANY] * len(into),
            out_specs=[spec(0), pl.BlockSpec((1, 8, padded), lambda p, _: (first + p, 0, 0))],
            scratch_shapes=[pltpu.VMEM((2, padded, PAIR), BF)],
        ),
        out_shape=[
            jax.ShapeDtypeStruct((slots, width), BF),
            jax.ShapeDtypeStruct((pairs, 8, padded), F32),
        ],
        input_output_aliases={4 + i: i for i in range(len(into))},
        compiler_params=params(),
        cost_estimate=cost(
            2 * count * 8 * slots * slots * PAIR, slots * width * 8, 2 * count * slots * slots
        ),
        name="attend",
    )(length, proj, proj, proj, *into)


def parts(values):
    high = values.astype(BF).astype(F32)
    rest = values - high
    mid = rest.astype(BF).astype(F32)
    return high, mid, (rest - mid).astype(BF).astype(F32)


def attend_back_kernel(
    len_ref,
    q_ref,
    k_ref,
    v_ref,
    g_ref,
    o_ref,
    lse_ref,
    dq_ref,
    dk_ref,
    dv_ref,
    qp,
    gp,
    *,
    slots,
    padded,
    tile,
):
    length = len_ref[0]
    lane = lax.broadcasted_iota(jnp.int32, (slots, PAIR), 1)
    row = lax.broadcasted_iota(jnp.int32, (slots, PAIR), 0)
    bias = jnp.where(row < length, 0.0, NEG_FILL)
    keys = k_ref[...].astype(F32)
    values = v_ref[...].astype(F32)
    queries = q_ref[...].astype(F32) * HEAD_DIM**-0.5
    grads = g_ref[...].astype(F32)
    products = grads * o_ref[...].astype(F32)
    d_queries, d_keys, d_values = [], [], []
    for h in range(2):
        mine = (lane // HEAD_DIM) == h
        spare = (1 - h) * HEAD_DIM
        flag = lane == spare
        dots = jnp.sum(jnp.where(mine, products, 0.0), axis=1, keepdims=True)
        high, mid, low = parts(-dots)
        ones = (lane >= spare) & (lane < spare + 3)
        value_ext = jnp.where(mine, values, jnp.where(ones, 1.0, 0.0)).astype(BF)
        tail = jnp.where(
            flag, high, jnp.where(lane == spare + 1, mid, jnp.where(lane == spare + 2, low, 0.0))
        )
        gp[h, 0:slots, :] = jnp.where(mine, grads, tail).astype(BF)
        key_ext = jnp.where(mine, keys, jnp.where(flag, bias, 0.0)).astype(BF)
        qp[h, 0:slots, :] = jnp.where(mine, queries, jnp.where(flag, 1.0, 0.0)).astype(BF)
        if padded > slots:
            gp[h, slots:padded, :] = jnp.zeros((padded - slots, PAIR), BF)
            qp[h, slots:padded, :] = jnp.zeros((padded - slots, PAIR), BF)
        keys_turned = key_ext.T[h * HEAD_DIM : (h + 1) * HEAD_DIM]
        d_key = d_value = None
        d_query = []
        for j in range(padded // tile):
            at = slice(j * tile, (j + 1) * tile)
            weights = jnp.exp(nt(key_ext, qp[h, at, :]) - lse_ref[0, h : h + 1, at])
            d_scores = (weights * nt(value_ext, gp[h, at, :])).astype(BF)
            more_value = nn(weights.astype(BF), gp[h, at, :])
            more_key = nn(d_scores, qp[h, at, :])
            d_value = more_value if d_value is None else d_value + more_value
            d_key = more_key if d_key is None else d_key + more_key
            d_query.append(nn(keys_turned, d_scores))
        d_queries.append(jnp.concatenate(d_query, axis=1))
        d_keys.append(d_key)
        d_values.append(d_value)
    turned = jnp.concatenate(d_queries, axis=0) * HEAD_DIM**-0.5
    dq_ref[...] = turned.T[0:slots].astype(BF)
    dk_ref[...] = jnp.where(lane < HEAD_DIM, d_keys[0], d_keys[1]).astype(BF)
    dv_ref[...] = jnp.where(lane < HEAD_DIM, d_values[0], d_values[1]).astype(BF)


def attend_back(length, proj, grads, mixed, totals, tile=256, first=0, count=None):
    slots = proj.shape[0]
    padded = -(-slots // 128) * 128
    width = proj.shape[1] // 3
    pairs = width // PAIR
    count = pairs if count is None else count

    def spec(off):
        return pl.BlockSpec((slots, PAIR), lambda p, _: (0, off + p))

    return pl.pallas_call(
        functools.partial(attend_back_kernel, slots=slots, padded=padded, tile=tile),
        grid_spec=pltpu.PrefetchScalarGridSpec(
            num_scalar_prefetch=1,
            grid=(count,),
            in_specs=[
                spec(first),
                spec(first + pairs),
                spec(first + 2 * pairs),
                spec(first),
                spec(first),
                pl.BlockSpec((1, 8, padded), lambda p, _: (first + p, 0, 0)),
            ],
            out_specs=[spec(0)] * 3,
            scratch_shapes=[pltpu.VMEM((2, padded, PAIR), BF)] * 2,
        ),
        out_shape=[jax.ShapeDtypeStruct((slots, count * PAIR), BF)] * 3,
        compiler_params=params(),
        cost_estimate=cost(
            2 * count * 20 * slots * slots * PAIR, slots * width * 16, 2 * count * slots * slots
        ),
        name="attend_back",
    )(length, proj, proj, proj, grads, mixed, totals)


def rest_copies(table, halves, downs, w_out, w_up, w_down, sems):
    width = w_out.shape[0]
    narrow = width // BLOCKS
    wide = w_up.shape[0] // BLOCKS
    half = (wide + narrow) // 2
    copies_out, copies_up, copies_down = [], [], []
    for j in range(2 * BLOCKS):
        block = table[j]
        base = j % 2 * half
        size = half if j < BLOCKS else wide - half
        start = block * wide + j // BLOCKS * half
        copies_up.append(
            pltpu.make_async_copy(
                halves[j // 2].at[pl.ds(base, size)],
                w_up.at[pl.ds(pl.multiple_of(start, 16), size)],
                sems.at[j],
            )
        )
        if j >= BLOCKS:
            copies_out.append(
                pltpu.make_async_copy(
                    halves[j // 2].at[pl.ds(base + size, narrow)],
                    w_out.at[pl.ds(pl.multiple_of(block * narrow, 16), narrow)],
                    sems.at[BLOCKS + j],
                )
            )
        for k in range(2):
            plane = table[2 * BLOCKS + j // BLOCKS * 2 + k]
            copies_down.append(
                pltpu.make_async_copy(
                    downs[j // 2].at[pl.ds((j % 2 * 2 + k) * narrow, narrow)],
                    w_down.at[
                        pl.ds(pl.multiple_of(block * narrow, 16), narrow),
                        pl.ds(pl.multiple_of(plane * width, 128), width),
                    ],
                    sems.at[3 * BLOCKS + j * 2 + k],
                )
            )
    return copies_out, copies_up, copies_down


def middle_kernel(len_ref, table, x_ref, mixed_ref, cot_ref, vec_ref, *refs, chunk):
    blocks, downs = refs[:8], refs[8:16]
    (
        out_ref,
        active_ref,
        d_inner_ref,
        normed_ref,
        d_resid_ref,
        d_branch_ref,
        d_mixed_ref,
        sums_ref,
    ) = refs[16:24]
    w_out, w_up, w_down, sems = refs[24:]
    i = pl.program_id(0)
    tile, width = x_ref.shape
    hidden = w_up.shape[0]

    copies_out, copies_up, copies_down = rest_copies(
        table, blocks, downs, w_out, w_up, w_down, sems
    )

    @pl.when(i == 0)
    def _():
        for copy in copies_out + copies_up + copies_down:
            copy.start()
        sums_ref[...] = jnp.zeros_like(sums_ref)
        for copy in copies_out:
            copy.wait()

    residual = x_ref[...].astype(F32) + nt(mixed_ref[...], w_out[...]) + vec_ref[2:3, :]
    nhat, scale = normalise(residual)
    normed = (nhat * vec_ref[6:7, :] + vec_ref[7:8, :]).astype(BF)
    normed_ref[...] = normed
    rows = lax.broadcasted_iota(jnp.int32, (tile, 1), 0) + i * tile
    seed_low = jnp.where(rows < len_ref[0], cot_ref[...], jnp.zeros_like(cot_ref))
    seed = seed_low.astype(F32)
    ones = jnp.ones((8, tile), BF)

    @pl.when(i == 0)
    def _():
        for copy in copies_up + copies_down:
            copy.wait()

    per = width // chunk

    def step(c, carry):
        out_sum, d_normed = carry
        at = pl.ds(pl.multiple_of(c * chunk, chunk), chunk)
        row = pl.ds(8 + c // per, 1)
        lanes = pl.ds(pl.multiple_of(lax.rem(c, per) * chunk, chunk), chunk)
        inner = nt(normed, w_up[at, :]) + vec_ref[row, lanes]
        cdf = 0.5 + 0.5 * lax.erf(inner * 0.5**0.5)
        active = (inner * cdf).astype(BF)
        active_ref[:, at] = active
        d_active = nn(seed_low, w_down[:, at])
        slope = cdf + inner * (jnp.exp(-0.5 * inner * inner) * 0.3989422804014327)
        d_inner = (d_active * slope).astype(BF)
        d_inner_ref[:, at] = d_inner
        sums_ref[row, lanes] += nn(ones, d_inner)[0:1]
        return (out_sum + nt(active, w_down[:, at]), d_normed + nn(d_inner, w_up[at, :]))

    zero = jnp.zeros((tile, width), F32)
    out_sum, d_normed = lax.fori_loop(0, hidden // chunk, step, (zero, zero))
    out_ref[...] = (residual + out_sum + vec_ref[3:4, :]).astype(BF)
    d_resid = seed + norm_back(d_normed, nhat, scale, vec_ref[6:7, :])
    d_resid_ref[...] = d_resid
    d_branch = d_resid.astype(BF)
    d_branch_ref[...] = d_branch
    d_mixed_ref[...] = nn(d_branch, w_out[...]).astype(BF)
    sums_ref[2:3, :] += jnp.sum(d_resid, axis=0, keepdims=True)
    sums_ref[3:4, :] += jnp.sum(seed, axis=0, keepdims=True)
    sums_ref[6:7, :] += jnp.sum(d_normed * nhat, axis=0, keepdims=True)
    sums_ref[7:8, :] += jnp.sum(d_normed, axis=0, keepdims=True)


def middle(length, table, x, mixed, cot, vec, blocks, downs, hidden, tile, chunk=768):
    slots, width = x.shape

    def rows(columns):
        return pl.BlockSpec((tile, columns), lambda i, *_: (i, 0))

    return pl.pallas_call(
        functools.partial(middle_kernel, chunk=chunk),
        grid_spec=pltpu.PrefetchScalarGridSpec(
            num_scalar_prefetch=2,
            grid=(slots // tile,),
            in_specs=[rows(width)] * 3 + [whole(vec.shape)] + [ANY] * 16,
            out_specs=[
                rows(width),
                rows(hidden),
                rows(hidden),
                rows(width),
                rows(width),
                rows(width),
                rows(width),
                whole(vec.shape),
            ],
            scratch_shapes=[
                pltpu.VMEM((width, width), BF),
                pltpu.VMEM((hidden, width), BF),
                pltpu.VMEM((width, hidden), BF),
                pltpu.SemaphoreType.DMA((7 * BLOCKS,)),
            ],
        ),
        out_shape=[
            jax.ShapeDtypeStruct((slots, width), BF),
            jax.ShapeDtypeStruct((slots, hidden), BF),
            jax.ShapeDtypeStruct((slots, hidden), BF),
            jax.ShapeDtypeStruct((slots, width), BF),
            jax.ShapeDtypeStruct((slots, width), F32),
            jax.ShapeDtypeStruct((slots, width), BF),
            jax.ShapeDtypeStruct((slots, width), BF),
            jax.ShapeDtypeStruct(vec.shape, F32),
        ],
        compiler_params=params(),
        cost_estimate=cost(
            2 * slots * width * (4 * hidden + 2 * width),
            slots * (hidden * 4 + width * 18) + hidden * width * 4,
            2 * slots * hidden,
        ),
        name="middle",
    )(length, table, x, mixed, cot, vec, *blocks, *downs)


def deliver(copies):
    for copy in copies:
        copy.start()
    for copy in copies:
        copy.wait()


def down_grads_kernel(len_ref, table, active_ref, cot_ref, keep_ref, send_ref, sums, sems):
    z = pl.program_id(0)
    slots, width = cot_ref.shape
    narrow = width // BLOCKS
    rows = lax.broadcasted_iota(jnp.int32, (slots, 1), 0)
    seed = jnp.where(rows < len_ref[0], cot_ref[...], jnp.zeros_like(cot_ref))
    sums[z] = tn(seed, active_ref[...]).astype(BF)

    @pl.when(z == pl.num_programs(0) - 1)
    def _():
        copies = []
        for j in range(BLOCKS):
            target = keep_ref if j < 4 else send_ref
            at = pl.ds(pl.multiple_of(table[j] * narrow, 16), narrow)
            for k in range(4):
                copies.append(
                    pltpu.make_async_copy(
                        sums.at[table[2 * BLOCKS + PLANES[k]], at],
                        target.at[k, j % 4],
                        sems.at[j * 4 + k],
                    )
                )
        deliver(copies)


def down_grads(length, table, active, cot):
    slots, width = cot.shape
    hidden = active.shape[1]
    out = jax.ShapeDtypeStruct((4, 4, width // BLOCKS, width), BF)
    return pl.pallas_call(
        down_grads_kernel,
        grid_spec=pltpu.PrefetchScalarGridSpec(
            num_scalar_prefetch=2,
            grid=(hidden // width,),
            in_specs=[pl.BlockSpec((slots, width), lambda z, *_: (0, z)), whole((slots, width))],
            out_specs=[ANY] * 2,
            scratch_shapes=[
                pltpu.VMEM((4, width, width), BF),
                pltpu.SemaphoreType.DMA((4 * BLOCKS,)),
            ],
        ),
        out_shape=[out, out],
        compiler_params=params(),
        cost_estimate=cost(2 * slots * width * hidden, slots * hidden * 2 + out.size * 4),
        name="down_grads",
    )(length, table, active, cot)


def up_grads_kernel(
    table, d_inner_ref, normed_ref, d_branch_ref, mixed_ref, keep_ref, send_ref, sums, sems
):
    z = pl.program_id(0)
    slots, width = normed_ref.shape
    narrow = width // BLOCKS
    wide = sums.shape[1] - narrow
    up = tn(d_inner_ref[...], normed_ref[...]).astype(BF)
    per = width // wide
    for j in range(per):
        sums[z * per + j, 0:wide, :] = up[j * wide : (j + 1) * wide]

    @pl.when(z == 0)
    def _():
        out = tn(d_branch_ref[...], mixed_ref[...]).astype(BF)
        for g in range(BLOCKS):
            sums[g, wide : wide + narrow, :] = out[g * narrow : (g + 1) * narrow]

    @pl.when(z == pl.num_programs(0) - 1)
    def _():
        deliver(
            [
                pltpu.make_async_copy(
                    sums.at[table[j]], (keep_ref if j < 4 else send_ref).at[j % 4], sems.at[j]
                )
                for j in range(BLOCKS)
            ]
        )


def up_grads(table, d_inner, normed, d_branch, mixed):
    slots, width = normed.shape
    hidden = d_inner.shape[1]
    rows = hidden // BLOCKS + width // BLOCKS
    out = jax.ShapeDtypeStruct((4, rows, width), BF)
    return pl.pallas_call(
        up_grads_kernel,
        grid_spec=pltpu.PrefetchScalarGridSpec(
            num_scalar_prefetch=1,
            grid=(hidden // width,),
            in_specs=[pl.BlockSpec((slots, width), lambda z, *_: (0, z))]
            + [whole((slots, width))] * 3,
            out_specs=[ANY] * 2,
            scratch_shapes=[
                pltpu.VMEM((BLOCKS, rows, width), BF),
                pltpu.SemaphoreType.DMA((BLOCKS,)),
            ],
        ),
        out_shape=[out, out],
        compiler_params=params(),
        cost_estimate=cost(
            2 * slots * width * (hidden + width), slots * hidden * 2 + out.size * 4
        ),
        name="up_grads",
    )(table, d_inner, normed, d_branch, mixed)


def qkv_grads_kernel(table, *refs):
    parts_in, normed_ref, (keep_ref, send_ref, sums, sems) = refs[:-5], refs[-5], refs[-4:]
    width = normed_ref.shape[1]
    block = sums.shape[0] // BLOCKS
    groups = len(parts_in) // 3
    for s in range(3):
        start = s * width
        for i in range(groups):
            ref = parts_in[i * 3 + s]
            sums[start : start + ref.shape[1], :] = tn(ref[...], normed_ref[...]).astype(BF)
            start += ref.shape[1]
    deliver(
        [
            pltpu.make_async_copy(
                sums.at[pl.ds(pl.multiple_of(table[j] * block, 16), block)],
                (keep_ref if j < 4 else send_ref).at[j % 4],
                sems.at[j],
            )
            for j in range(BLOCKS)
        ]
    )


def qkv_grads(table, d_parts, normed):
    slots, width = normed.shape
    out = jax.ShapeDtypeStruct((4, 3 * width // BLOCKS, width), BF)
    return pl.pallas_call(
        qkv_grads_kernel,
        grid_spec=pltpu.PrefetchScalarGridSpec(
            num_scalar_prefetch=1,
            grid=(1,),
            in_specs=[whole(part.shape) for part in d_parts] + [whole((slots, width))],
            out_specs=[ANY] * 2,
            scratch_shapes=[
                pltpu.VMEM((3 * width, width), BF),
                pltpu.SemaphoreType.DMA((BLOCKS,)),
            ],
        ),
        out_shape=[out, out],
        compiler_params=params(),
        cost_estimate=cost(6 * slots * width * width, slots * width * 8 + out.size * 4),
        name="qkv_grads",
    )(table, *d_parts, normed)


def last_kernel(table, x_ref, d_resid_ref, vec_ref, sums_in, *refs, groups):
    parts_in, blocks = refs[: 3 * groups], refs[3 * groups : 3 * groups + 8]
    grad_ref, sums_ref, weights, sems = refs[3 * groups + 8 :]
    i = pl.program_id(0)
    tile, width = x_ref.shape
    copies = qkv_copies(table, blocks, weights, sems)

    @pl.when(i == 0)
    def _():
        for copy in copies:
            copy.start()
        sums_ref[...] = sums_in[...]
        for copy in copies:
            copy.wait()

    ones = jnp.ones((8, tile), BF)
    d_normed = jnp.zeros((tile, width), F32)
    for s in range(3):
        start = 0
        for j in range(groups):
            ref = parts_in[j * 3 + s]
            end = start + ref.shape[1]
            d_normed += nn(ref[...], weights[s * width + start : s * width + end, :])
            if s != 1:
                row = s // 2
                sums_ref[row : row + 1, start:end] += nn(ones, ref[...])[0:1]
            start = end
    nhat, scale = normalise(x_ref[...].astype(F32))
    grad_ref[...] = d_resid_ref[...] + norm_back(d_normed, nhat, scale, vec_ref[4:5, :])
    sums_ref[4:5, :] += jnp.sum(d_normed * nhat, axis=0, keepdims=True)
    sums_ref[5:6, :] += jnp.sum(d_normed, axis=0, keepdims=True)


def last(table, d_parts, x, d_resid, vec, sums, blocks, tile):
    slots, width = x.shape

    def rows(columns):
        return pl.BlockSpec((tile, columns), lambda i, _: (i, 0))

    return pl.pallas_call(
        functools.partial(last_kernel, groups=len(d_parts) // 3),
        grid_spec=pltpu.PrefetchScalarGridSpec(
            num_scalar_prefetch=1,
            grid=(slots // tile,),
            in_specs=[rows(width)] * 2
            + [whole(vec.shape)] * 2
            + [rows(part.shape[1]) for part in d_parts]
            + [ANY] * 8,
            out_specs=[rows(width), whole(vec.shape)],
            scratch_shapes=[
                pltpu.VMEM((3 * width, width), BF),
                pltpu.SemaphoreType.DMA((2 * BLOCKS,)),
            ],
        ),
        out_shape=[
            jax.ShapeDtypeStruct((slots, width), F32),
            jax.ShapeDtypeStruct(vec.shape, F32),
        ],
        compiler_params=params(),
        cost_estimate=cost(6 * slots * width * width, slots * width * 16),
        name="last",
    )(table, x, d_resid, vec, sums, *d_parts, *blocks)


def fold_kernel(table, *refs):
    terms, outs, turned = refs[:4], refs[4:-1], refs[-1]
    rows = turned.shape[0] // 4
    total = terms[0][...].astype(F32)
    for term in terms[1:]:
        total += term[...].astype(F32)
    turned[...] = total.T

    def plane(k):
        return turned[pl.ds(pl.multiple_of(table[2 * BLOCKS + k] * rows, 8), rows), :]

    if len(outs) == 4:
        for k in range(4):
            outs[k][...] = plane(k).astype(outs[k].dtype)
    else:
        for k in range(4):
            outs[k // 2][k % 2] = plane(PLANES[k]).astype(outs[k // 2].dtype)


def fold(table, terms, paired):
    columns, width = terms[0].shape
    shape = (width // 4, columns)
    if paired:
        out = [jax.ShapeDtypeStruct((2, *shape), dtype) for dtype in (F32, BF)]
    else:
        out = [jax.ShapeDtypeStruct(shape, dtype) for dtype in (F32, BF, BF, BF)]
    return pl.pallas_call(
        fold_kernel,
        grid_spec=pltpu.PrefetchScalarGridSpec(
            num_scalar_prefetch=1,
            grid=(1,),
            in_specs=[whole(terms[0].shape)] * 4,
            out_specs=[whole(o.shape) for o in out],
            scratch_shapes=[pltpu.VMEM((width, columns), F32)],
        ),
        out_shape=out,
        compiler_params=params(),
        cost_estimate=cost(1e6, columns * width * 12),
        name="fold",
    )(table, *terms)


def swap(values, axis, mask, size):
    return lax.ppermute(values, axis, [(i, i ^ mask) for i in range(size)])


def in_turn(*values):
    return lax.optimization_barrier(values)


def gather_planes(message):
    return [message] + [swap(message, "gx", k, 4) for k in (1, 2, 3)]


def near(first, second):
    return swap(first, "gy", 2, BLOCKS), swap(second, "gy", 4, BLOCKS)


def far(first, second):
    return swap(first, "gy", 4, BLOCKS), swap(second, "gy", 2, BLOCKS)


def join(first, second):
    return jnp.concatenate([first, second], axis=0)


def with_cores(a, b, a_far, b_far):
    a_core, b_core, a_other, b_other = [swap(v, "gy", 1, BLOCKS) for v in (a, b, a_far, b_far)]
    return [a, a_far, a_core, a_other, b, b_far, b_core, b_other]


def add(*terms):
    total = terms[0].astype(F32)
    for term in terms[1:]:
        total = total + term.astype(F32)
    return total


def per_device(
    patches,
    lengths,
    cotangent,
    w_qkv,
    w_out,
    w_up,
    w_down,
    bias_q,
    bias_v,
    bias_o,
    bias_up,
    bias_down,
    gain_one,
    shift_one,
    gain_two,
    shift_two,
    *,
    planes,
    columns,
):
    slots, width = patches.shape
    hidden = w_up.shape[1] * columns
    wide, narrow = hidden // BLOCKS, width // BLOCKS
    tile = slots // 3
    z, g = lax.axis_index("gx"), lax.axis_index("gy")
    fast = planes == 4 and columns == BLOCKS
    vectors = (bias_q, bias_v, bias_o, bias_down, gain_one, shift_one, gain_two, shift_two)
    if fast:
        pos = jnp.stack([z, g]).astype(jnp.int32)
        table = jnp.concatenate(
            [g ^ jnp.array(MASKS_A), g ^ jnp.array(MASKS_B), z ^ jnp.arange(4)]
        ).astype(jnp.int32)
        message = pack(w_qkv, vectors + (bias_up,))
        message, *rest = in_turn(message, w_up, w_out, w_down)
        pieces = gather_planes(message)
        both, down = pack_rest(*rest)
        qa, qb = arrange_qkv(pos, pieces, width)
        qa, qb, both = in_turn(qa, qb, both)
        qa_near, qb_near = near(qa, qb)
        pieces = gather_planes(both)
        qa, qb = join(qa, qa_near), join(qb, qb_near)
        qa_far, qb_far = far(qa, qb)
        ra, rb = arrange_rest(pos, pieces, width, wide + narrow)
        ra, rb, down = in_turn(ra, rb, down)
        qa, qb, qa_far, qb_far, ra = in_turn(qa, qb, qa_far, qb_far, ra)
        qkv_blocks = with_cores(qa, qb, qa_far, qb_far)
        ra_near, rb_near = near(ra, rb)
        down_planes = gather_planes(down)
    else:

        def everything(shard):
            return lax.all_gather(
                lax.all_gather(shard, "gx", axis=0, tiled=True), "gy", axis=1, tiled=True
            ).T

        order = jnp.arange(BLOCKS)
        table = jnp.concatenate([order, order, jnp.arange(4)]).astype(jnp.int32)
        aux = [lax.all_gather(v, AXES, axis=0, tiled=True)[None] for v in vectors]
        aux.append(lax.all_gather(bias_up, AXES, axis=0, tiled=True).reshape(4, width))
        aux.append(jnp.zeros((AUX - 12, width), BF))
        none = jnp.zeros((BLOCKS - 1, AUX, width), BF)
        aux = jnp.concatenate([jnp.concatenate(aux)[None], none])

        def halved(blocks, extra=None):
            half = blocks.shape[1] // 2
            first = blocks[:, :half]
            if extra is not None:
                first = jnp.concatenate([first, extra], axis=1)
            second = blocks[:, half:]
            return list(first.reshape(4, -1, width)) + list(second.reshape(4, -1, width))

        qkv_blocks = halved(everything(w_qkv).reshape(BLOCKS, -1, width), aux)
        up = everything(w_up).reshape(BLOCKS, wide, width)
        out = everything(w_out).reshape(BLOCKS, narrow, width)
        rest_blocks = halved(jnp.concatenate([up, out], axis=1))
        down = everything(w_down).reshape(BLOCKS, narrow, 4, width)
        downs = halved(jnp.transpose(down, (0, 2, 1, 3)).reshape(BLOCKS, wide, width))

    proj, normed, vec = project(table, patches, qkv_blocks)
    if fast:
        ra_near, rb_near, length, proj = in_turn(ra_near, rb_near, lengths, proj)
        ra, rb = join(ra, ra_near), join(rb, rb_near)
        da, db = join(*down_planes[:2]), join(*down_planes[2:])
        length, ra, rb, da, db = in_turn(length, ra, rb, da, db)
        ra_far, rb_far = far(ra, rb)
        da_near, db_near = near(da, db)
        half = HEADS // 4
        mixed, totals = attend(length, proj, 0, half)
        mixed, totals, da_near, db_near = in_turn(mixed, totals, da_near, db_near)
        da, db = join(da, da_near), join(db, db_near)
        length, da, db, mixed, totals = in_turn(length, da, db, mixed, totals)
        da_far, db_far = far(da, db)
        mixed, totals = attend(length, proj, half, half, (mixed, totals))
        mixed, ra, rb, ra_far, rb_far, da, db, da_far, db_far = in_turn(
            mixed, ra, rb, ra_far, rb_far, da, db, da_far, db_far
        )
        rest_blocks = with_cores(ra, rb, ra_far, rb_far)
        downs = with_cores(da, db, da_far, db_far)
    else:
        mixed, totals = attend(lengths, proj)
    out_rows, active, d_inner, normed_two, d_resid, d_branch, d_mixed, sums = middle(
        lengths, table, patches, mixed, cotangent, vec, rest_blocks, downs, hidden, tile
    )
    down_keep, down_send = down_grads(lengths, table, active, cotangent)
    down_keep, down_send, d_inner = in_turn(down_keep, down_send, d_inner)
    up_keep, up_send = up_grads(table, d_inner, normed_two, d_branch, mixed)

    def back(length, first, count):
        return list(
            attend_back(length, proj, d_mixed, mixed, totals, first=first, count=count)
        )

    if fast:
        down_got = swap(down_send, "gy", 1, BLOCKS)
        up_got = swap(up_send, "gy", 1, BLOCKS)
        down_keep, down_got, up_keep = in_turn(down_keep, down_got, up_keep)
        down_next = add(down_keep[2:], down_got[2:]).astype(BF)
        length, down_next = in_turn(lengths, down_next)
        down_near = swap(down_next, "gx", 1, 4)
        d_parts = back(length, 0, 2)
        d_parts[0], up_keep, up_got = in_turn(d_parts[0], up_keep, up_got)
        up_sums = [add(up_keep[r], up_got[r]).astype(BF) for r in range(4)]
        length, *up_sums = in_turn(length, *up_sums)
        up_blocks = [swap(up_sums[r], "gy", MASKS_A[r], BLOCKS) for r in (1, 2, 3)]
        more = back(length, 2, 1)
        more[0], down_near, down_keep = in_turn(more[0], down_near, down_keep)
        d_parts += more
        down_sum = add(down_keep[0], down_got[0], down_near[0])
        down_next = add(down_keep[1], down_got[1], down_near[1]).astype(BF)
        length, down_next, down_sum = in_turn(length, down_next, down_sum)
        down_far = swap(down_next, "gx", 2, 4)
        more = back(length, 3, 3)
        more[0], down_far, *up_blocks = in_turn(more[0], down_far, *up_blocks)
        d_parts += more
        down_sums = [add(down_sum[r], down_far[r]).astype(BF) for r in range(4)]
        up_keep, up_send = fold(table, up_sums[:1] + up_blocks, True)
        table, up_keep, up_send, *down_sums = in_turn(table, up_keep, up_send, *down_sums)
        down_blocks = [swap(down_sums[r], "gy", MASKS_A[r], BLOCKS) for r in (1, 2, 3)]
        up_near = swap(up_send, "gx", 1, 4)
        qkv_keep, qkv_send = qkv_grads(table, d_parts, normed)
        qkv_keep, qkv_send, up_near, *down_blocks = in_turn(
            qkv_keep, qkv_send, up_near, *down_blocks
        )
        qkv_got = swap(qkv_send, "gy", 1, BLOCKS)
        grad_down = add(down_sums[0], *down_blocks).T
        up_sum = add(up_keep[0], up_near[0])
        up_next = add(up_keep[1], up_near[1]).astype(BF)
        qkv_keep, qkv_got, up_next = in_turn(qkv_keep, qkv_got, up_next)
        up_far = swap(up_next, "gx", 2, 4)
        qkv_sums = [add(qkv_keep[r], qkv_got[r]).astype(BF) for r in range(4)]
        table, grad_down, *qkv_sums = in_turn(table, grad_down, *qkv_sums)
        qkv_got = [swap(qkv_sums[r], "gy", MASKS_A[r], BLOCKS) for r in (1, 2, 3)]
        grad_rows, sums = last(table, d_parts, patches, d_resid, vec, sums, qkv_blocks, tile)
        up_far, sums = in_turn(up_far, sums)
        up_sum = add(up_sum, up_far)
        grad_up, grad_out = up_sum[:, :wide], up_sum[:, wide:]
        steps = (("gy", 1, 8), ("gy", 2, 8), ("gy", 4, 8), ("gx", 1, 4), ("gx", 2, 4))
        for axis, mask, size in steps[:2]:
            sums = sums + swap(sums, axis, mask, size)
        table, sums = in_turn(table, sums)
        qkv_pieces = fold(table, qkv_sums[:1] + qkv_got, False)
        sums, *qkv_pieces = in_turn(sums, *qkv_pieces)
        qkv_planes = [swap(qkv_pieces[k], "gx", k, 4) for k in (1, 2, 3)]
        for axis, mask, size in steps[2:]:
            sums = sums + swap(sums, axis, mask, size)
        sums, *qkv_planes = in_turn(sums, *qkv_planes)
        grad_qkv = add(qkv_pieces[0], *qkv_planes)
        device = z * columns + g
        own = lax.dynamic_slice(sums, (0, device * (narrow // 4)), (8, narrow // 4))
        own_up = lax.dynamic_slice(sums, (8 + z, g * narrow), (1, narrow))[0]
        own = [own[j] for j in range(8)]
    else:
        d_parts = back(lengths, 0, 2) + back(lengths, 2, 1) + back(lengths, 3, 3)
        qkv_keep, qkv_send = qkv_grads(table, d_parts, normed)
        grad_rows, sums = last(table, d_parts, patches, d_resid, vec, sums, qkv_blocks, tile)

        def spread(grads):
            part = lax.psum_scatter(grads, "gy", scatter_dimension=0, tiled=True)
            return lax.psum_scatter(part.T, "gx", scatter_dimension=0, tiled=True).astype(F32)

        rest = jnp.concatenate([up_keep, up_send], axis=0)
        grad_up = spread(rest[:, :wide].reshape(hidden, width))
        grad_out = spread(rest[:, wide:].reshape(width, width))
        down = jnp.stack([down_keep, down_send])[:, jnp.array(PLANES)]
        grad_down = spread(jnp.transpose(down, (0, 2, 3, 1, 4)).reshape(width, hidden))
        grad_qkv = spread(jnp.concatenate([qkv_keep, qkv_send]).reshape(3 * width, width))

        def share(vector):
            return lax.psum_scatter(vector, AXES, scatter_dimension=0, tiled=True)

        own = [share(sums[j]) for j in range(8)]
        own_up = share(sums[8:12].reshape(hidden))

    return (
        out_rows,
        grad_rows,
        grad_qkv,
        grad_out,
        grad_up,
        grad_down,
        own[0],
        own[1],
        own[2],
        own_up,
        own[3],
        own[4],
        own[5],
        own[6],
        own[7],
    )


def solution(mesh):
    by_rows = P(AXES, None)
    by_parts = P(AXES)
    matrix = P("gx", "gy")
    in_specs = (by_rows, by_parts, by_rows) + (matrix,) * 4 + (by_parts,) * 9
    out_specs = (by_rows, by_rows) + (matrix,) * 4 + (by_parts,) * 9
    body = functools.partial(per_device, planes=mesh.shape["gx"], columns=mesh.shape["gy"])
    return jax.shard_map(body, mesh=mesh, in_specs=in_specs, out_specs=out_specs, check_vma=False)
```

```python
import functools

import jax
import jax.numpy as jnp
from jax import lax
from jax.experimental import pallas as pl
from jax.experimental.pallas import tpu as pltpu
from jax.sharding import PartitionSpec as P

HEADS = 12
HEAD_DIM = 64
PAIR = 2 * HEAD_DIM
EPSILON = 1e-06
NEG_FILL = -1e30
BF = jnp.bfloat16
F32 = jnp.float32
AXES = ("gx", "gy")
BLOCKS = 8
AUX = 16
MIB = 1 << 20
MASKS_A = (0, 2, 4, 6, 1, 3, 5, 7)
MASKS_B = (0, 4, 2, 6, 1, 5, 3, 7)
PLANES = (0, 2, 1, 3)
PLACE_AT = 2 * BLOCKS + 4
RELATIVE_AT = PLACE_AT + 4
ANY = pl.BlockSpec(memory_space=pl.ANY)


def nt(left, right):
    return lax.dot_general(left, right, (((1,), (1,)), ((), ())), preferred_element_type=F32)


def nn(left, right):
    return lax.dot_general(left, right, (((1,), (0,)), ((), ())), preferred_element_type=F32)


def tn(left, right):
    return lax.dot_general(left, right, (((0,), (0,)), ((), ())), preferred_element_type=F32)


def params(mebibytes):
    return pltpu.CompilerParams(vmem_limit_bytes=mebibytes * MIB)


def cost(flops, bytes_moved, transcendentals=0):
    return pl.CostEstimate(
        flops=int(flops), bytes_accessed=int(bytes_moved), transcendentals=int(transcendentals)
    )


def whole(shape):
    return pl.BlockSpec(shape, lambda *_: (0,) * len(shape))


def normalise(values):
    centre = values - jnp.mean(values, axis=-1, keepdims=True)
    spread = jnp.mean(centre * centre, axis=-1, keepdims=True)
    scale = lax.rsqrt(spread + EPSILON)
    return centre * scale, scale


def norm_back(grads, nhat, scale, gain):
    e = grads * gain
    return scale * (
        e
        - jnp.mean(e, axis=-1, keepdims=True)
        - nhat * jnp.mean(e * nhat, axis=-1, keepdims=True)
    )


def pack_kernel(w_ref, up_ref, out_ref, down_ref, *refs):
    vectors, message_ref, both_ref = refs[:-2], refs[-2], refs[-1]
    rows = w_ref.shape[0]
    message_ref[0:rows, :] = w_ref[...]
    pieces = [ref[...].astype(F32) for ref in vectors]
    message_ref[rows : rows + 8, :] = jnp.broadcast_to(
        jnp.concatenate(pieces, axis=1), (8, message_ref.shape[1])
    ).astype(BF)
    wide, narrow = up_ref.shape[1], out_ref.shape[1]
    edge = both_ref.shape[1] - wide
    both_ref[:, 0:wide] = up_ref[...]
    both_ref[:, wide : wide + narrow] = out_ref[...]
    both_ref[:, wide + narrow : edge] = jnp.zeros(
        (both_ref.shape[0], edge - wide - narrow), BF
    )
    both_ref[0:narrow, edge:] = down_ref[:, 0:wide]
    both_ref[narrow : 2 * narrow, edge:] = down_ref[:, wide : 2 * wide]


def pack(w_qkv, w_up, w_out, w_down, vectors):
    rows, columns = w_qkv.shape
    wide = w_up.shape[1]
    edge = -(-(wide + w_out.shape[1]) // 128) * 128
    return pl.pallas_call(
        pack_kernel,
        out_shape=[
            jax.ShapeDtypeStruct((rows + 8, columns), BF),
            jax.ShapeDtypeStruct((rows, edge + wide), BF),
        ],
        compiler_params=params(63),
        cost_estimate=cost(1e4, rows * (columns + edge + wide) * 4),
        name="pack",
    )(w_qkv, w_up, w_out, w_down.T, *[v[None, :] for v in vectors])


def arrange_qkv_kernel(pos, *refs):
    pieces, out_ref, stacked = refs[:4], refs[4], refs[5]
    width, columns = out_ref.shape[1], pieces[0].shape[1]
    rows = width // 4
    vec_rows = []
    for k in range(4):
        place = pos[0] ^ k
        stacked[pl.ds(pl.multiple_of(place * rows, 8), rows), :] = pieces[k][0:rows, :].astype(F32)
        vec_rows.append(pieces[k][rows : rows + 1, :].astype(F32))
    out_ref[0:columns, :] = stacked[...].T.astype(BF)
    vec = jnp.concatenate(vec_rows, axis=0).astype(BF)
    lane = lax.broadcasted_iota(jnp.int32, (columns, width), 1)
    source = lax.broadcasted_iota(jnp.int32, (columns, width), 0)
    lane4 = lax.broadcasted_iota(jnp.int32, (4, width), 1)
    order = lax.broadcasted_iota(jnp.int32, (4, 1), 0)
    piece = width // (4 * BLOCKS)
    device = (pos[0] ^ order) * BLOCKS + pos[1]
    here = lane4 // piece == device
    base = lane % piece
    rows_out = []
    for j in range(8):
        spread = nn(vec, (source == piece * j + base).astype(BF))
        rows_out.append(jnp.sum(jnp.where(here, spread, 0.0), axis=0, keepdims=True))
    pick = (source == piece * 8 + lane % (4 * piece)).astype(BF)
    spread = jnp.where(lane4 // (4 * piece) == pos[1], nn(vec, pick), 0.0)
    for row in range(4):
        rows_out.append(
            jnp.sum(jnp.where((pos[0] ^ order) == row, spread, 0.0), axis=0, keepdims=True)
        )
    rows_out.append(jnp.zeros((AUX - 12, width), F32))
    out_ref[columns : columns + AUX, :] = jnp.concatenate(rows_out, axis=0).astype(BF)


def arrange_qkv(pos, pieces, width):
    rows, columns = pieces[0].shape
    out = jax.ShapeDtypeStruct((columns + AUX, width), BF)
    return pl.pallas_call(
        arrange_qkv_kernel,
        grid_spec=pltpu.PrefetchScalarGridSpec(
            num_scalar_prefetch=1,
            grid=(1,),
            in_specs=[whole((rows, columns))] * 4,
            out_specs=whole(out.shape),
            scratch_shapes=[pltpu.VMEM((width, columns), F32)],
        ),
        out_shape=out,
        compiler_params=params(16),
        cost_estimate=cost(4e6, 4 * rows * columns * 2 * 2),
        name="arrange_qkv",
    )(pos, *pieces)


def arrange_rest_kernel(pos, own_ref, near_ref, far_ref, first_ref, second_ref, stacked):
    rows = first_ref.shape[1] // 4
    half = first_ref.shape[0]
    edge = far_ref.shape[1]
    pieces = [own_ref[:, 0:edge], near_ref[:, 0:edge], far_ref[0:rows], far_ref[rows : 2 * rows]]
    for k in range(4):
        start = pl.multiple_of((pos[0] ^ k) * rows, 8)
        stacked[pl.ds(start, rows), :] = pieces[k].astype(F32)
    turned = stacked[...].T.astype(BF)
    first_ref[...] = turned[0:half]
    second_ref[...] = turned[half : 2 * half]


def arrange_rest(pos, own, near_piece, far_pieces, width, height):
    out = jax.ShapeDtypeStruct((height // 2, width), BF)
    return pl.pallas_call(
        arrange_rest_kernel,
        grid_spec=pltpu.PrefetchScalarGridSpec(
            num_scalar_prefetch=1,
            grid=(1,),
            in_specs=[whole(own.shape)] * 2 + [whole(far_pieces.shape)],
            out_specs=[whole(out.shape)] * 2,
            scratch_shapes=[pltpu.VMEM((width, far_pieces.shape[1]), F32)],
        ),
        out_shape=[out, out],
        compiler_params=params(16),
        cost_estimate=cost(1e6, out.shape[0] * width * 2 * 4),
        name="arrange_rest",
    )(pos, own, near_piece, far_pieces)


def arrange_down_kernel(own_ref, near_ref, far_ref, first_ref, second_ref):
    wide = far_ref.shape[1]
    rows = own_ref.shape[0]
    narrow = rows // 2
    edge = own_ref.shape[1] - wide
    pieces = [own_ref[:, edge:], near_ref[:, edge:], far_ref[0:rows], far_ref[rows : 2 * rows]]
    for k in range(4):
        target = (first_ref, second_ref)[k // 2]
        at = k % 2 * narrow
        target[at : at + narrow, 0:wide] = pieces[k][0:narrow]
        target[at : at + narrow, wide : 2 * wide] = pieces[k][narrow:rows]


def arrange_down(own, near_piece, far_pieces):
    rows, wide = own.shape[0], far_pieces.shape[1]
    out = jax.ShapeDtypeStruct((rows, 2 * wide), BF)
    return pl.pallas_call(
        arrange_down_kernel,
        out_shape=[out, out],
        compiler_params=params(16),
        cost_estimate=cost(1e4, rows * wide * 2 * 8),
        name="arrange_down",
    )(own, near_piece, far_pieces)


def qkv_copies(table, blocks, weights, sems):
    step = weights.shape[0] // BLOCKS
    return [
        pltpu.make_async_copy(
            blocks[j].at[pl.ds(0, step)],
            weights.at[pl.ds(pl.multiple_of(table[j] * step, 16), step)],
            sems.at[j],
        )
        for j in range(BLOCKS)
    ]


def project_kernel(table, x_ref, *refs):
    blocks, (proj_ref, normed_ref, vec_ref), (weights, aux, sems) = refs[:8], refs[8:11], refs[11:]
    j = pl.program_id(0)
    step = weights.shape[0] // BLOCKS
    tile = proj_ref.shape[1]
    width = x_ref.shape[1]

    @pl.when(j == 0)
    def _():
        small = [
            pltpu.make_async_copy(
                blocks[i].at[pl.ds(step, AUX)], aux.at[i], sems.at[BLOCKS + i]
            )
            for i in range(BLOCKS)
        ]
        large = qkv_copies(table, blocks, weights, sems)
        for copy in small + large:
            copy.start()
        nhat, _ = normalise(x_ref[...].astype(F32))
        for copy in small:
            copy.wait()
        vec_ref[...] = jnp.sum(aux[...].astype(F32), axis=0)
        normed_ref[...] = (nhat * vec_ref[4:5, :] + vec_ref[5:6, :]).astype(BF)
        for copy in large:
            copy.wait()

    per = width // tile
    start = pl.multiple_of(j * tile, tile)
    lanes = pl.ds(pl.multiple_of(lax.rem(j, per) * tile, tile), tile)
    section = j // per
    bias = jnp.where(
        section == 0, vec_ref[0:1, lanes], jnp.where(section == 2, vec_ref[1:2, lanes], 0.0)
    )
    proj_ref[...] = (nt(normed_ref[...], weights[pl.ds(start, tile), :]) + bias).astype(BF)


def project(table, x, blocks, tile=256):
    slots, width = x.shape
    columns = 3 * width
    return pl.pallas_call(
        project_kernel,
        grid_spec=pltpu.PrefetchScalarGridSpec(
            num_scalar_prefetch=1,
            grid=(columns // tile,),
            in_specs=[whole((slots, width))] + [ANY] * 8,
            out_specs=[
                pl.BlockSpec((slots, tile), lambda j, _: (0, j)),
                whole((slots, width)),
                whole((AUX, width)),
            ],
            scratch_shapes=[
                pltpu.VMEM((columns, width), BF),
                pltpu.VMEM((BLOCKS, AUX, width), BF),
                pltpu.SemaphoreType.DMA((3 * BLOCKS,)),
            ],
        ),
        out_shape=[
            jax.ShapeDtypeStruct((slots, columns), BF),
            jax.ShapeDtypeStruct((slots, width), BF),
            jax.ShapeDtypeStruct((AUX, width), F32),
        ],
        compiler_params=params(32),
        cost_estimate=cost(2 * slots * width * columns, slots * width * 10),
        name="project",
    )(table, x, *blocks)


def attend_kernel(len_ref, q_ref, k_ref, v_ref, *refs, slots, padded):
    o_ref, lse_ref, qp = refs[-3:]
    length = len_ref[0]
    lane = lax.broadcasted_iota(jnp.int32, (slots, PAIR), 1)
    row = lax.broadcasted_iota(jnp.int32, (slots, PAIR), 0)
    bias = jnp.where(row < length, 0.0, NEG_FILL)
    keys = k_ref[...].astype(F32)
    values = v_ref[...].astype(F32)
    queries = q_ref[...].astype(F32) * HEAD_DIM**-0.5
    outs = []
    for h in range(2):
        mine = (lane // HEAD_DIM) == h
        spare = (1 - h) * HEAD_DIM
        flag = lane == spare
        key_ext = jnp.where(mine, keys, jnp.where(flag, bias, 0.0)).astype(BF)
        value_ext = jnp.where(mine, values, jnp.where(flag, 1.0, 0.0)).astype(BF)
        qp[h, 0:slots, :] = jnp.where(mine, queries, jnp.where(flag, 1.0, 0.0)).astype(BF)
        if padded > slots:
            qp[h, slots:padded, :] = jnp.zeros((padded - slots, PAIR), BF)
        scores = nt(key_ext, qp[h])
        top = jnp.max(scores, axis=0, keepdims=True)
        weights = jnp.exp(scores - top).astype(BF)
        mixed = nn(value_ext.T, weights)
        total = mixed[spare : spare + 1, :]
        outs.append(mixed[h * HEAD_DIM : (h + 1) * HEAD_DIM, :] / total)
        lse_ref[0, h : h + 1, :] = top + jnp.log(total)
    o_ref[...] = jnp.concatenate(outs, axis=0).T[0:slots].astype(BF)


def attend(length, proj, first=0, count=None, into=()):
    slots = proj.shape[0]
    padded = -(-slots // 128) * 128
    width = proj.shape[1] // 3
    pairs = width // PAIR
    count = pairs if count is None else count

    def spec(off):
        return pl.BlockSpec((slots, PAIR), lambda p, _: (0, off + first + p))

    return pl.pallas_call(
        functools.partial(attend_kernel, slots=slots, padded=padded),
        grid_spec=pltpu.PrefetchScalarGridSpec(
            num_scalar_prefetch=1,
            grid=(count,),
            in_specs=[spec(0), spec(pairs), spec(2 * pairs)] + [ANY] * len(into),
            out_specs=[spec(0), pl.BlockSpec((1, 8, padded), lambda p, _: (first + p, 0, 0))],
            scratch_shapes=[pltpu.VMEM((2, padded, PAIR), BF)],
        ),
        out_shape=[
            jax.ShapeDtypeStruct((slots, width), BF),
            jax.ShapeDtypeStruct((pairs, 8, padded), F32),
        ],
        input_output_aliases={4 + i: i for i in range(len(into))},
        compiler_params=params(63),
        cost_estimate=cost(
            2 * count * 8 * slots * slots * PAIR, slots * width * 8, 2 * count * slots * slots
        ),
        name="attend",
    )(length, proj, proj, proj, *into)


def parts(values):
    high = values.astype(BF).astype(F32)
    rest = values - high
    mid = rest.astype(BF).astype(F32)
    return high, mid, (rest - mid).astype(BF).astype(F32)


def attend_back_kernel(
    len_ref,
    q_ref,
    k_ref,
    v_ref,
    g_ref,
    o_ref,
    lse_ref,
    dq_ref,
    dk_ref,
    dv_ref,
    qp,
    gp,
    *,
    slots,
    padded,
    tile,
):
    length = len_ref[0]
    lane = lax.broadcasted_iota(jnp.int32, (slots, PAIR), 1)
    row = lax.broadcasted_iota(jnp.int32, (slots, PAIR), 0)
    bias = jnp.where(row < length, 0.0, NEG_FILL)
    keys = k_ref[...].astype(F32)
    values = v_ref[...].astype(F32)
    queries = q_ref[...].astype(F32) * HEAD_DIM**-0.5
    grads = g_ref[...].astype(F32)
    products = grads * o_ref[...].astype(F32)
    d_queries, d_keys, d_values = [], [], []
    for h in range(2):
        mine = (lane // HEAD_DIM) == h
        spare = (1 - h) * HEAD_DIM
        flag = lane == spare
        dots = jnp.sum(jnp.where(mine, products, 0.0), axis=1, keepdims=True)
        high, mid, low = parts(-dots)
        ones = (lane >= spare) & (lane < spare + 3)
        value_ext = jnp.where(mine, values, jnp.where(ones, 1.0, 0.0)).astype(BF)
        tail = jnp.where(
            flag, high, jnp.where(lane == spare + 1, mid, jnp.where(lane == spare + 2, low, 0.0))
        )
        gp[h, 0:slots, :] = jnp.where(mine, grads, tail).astype(BF)
        key_ext = jnp.where(mine, keys, jnp.where(flag, bias, 0.0)).astype(BF)
        qp[h, 0:slots, :] = jnp.where(mine, queries, jnp.where(flag, 1.0, 0.0)).astype(BF)
        if padded > slots:
            gp[h, slots:padded, :] = jnp.zeros((padded - slots, PAIR), BF)
            qp[h, slots:padded, :] = jnp.zeros((padded - slots, PAIR), BF)
        keys_turned = key_ext.T[h * HEAD_DIM : (h + 1) * HEAD_DIM]
        d_key = d_value = None
        d_query = []
        for j in range(padded // tile):
            at = slice(j * tile, (j + 1) * tile)
            weights = jnp.exp(nt(key_ext, qp[h, at, :]) - lse_ref[0, h : h + 1, at])
            d_scores = (weights * nt(value_ext, gp[h, at, :])).astype(BF)
            more_value = nn(weights.astype(BF), gp[h, at, :])
            more_key = nn(d_scores, qp[h, at, :])
            d_value = more_value if d_value is None else d_value + more_value
            d_key = more_key if d_key is None else d_key + more_key
            d_query.append(nn(keys_turned, d_scores))
        d_queries.append(jnp.concatenate(d_query, axis=1))
        d_keys.append(d_key)
        d_values.append(d_value)
    turned = jnp.concatenate(d_queries, axis=0) * HEAD_DIM**-0.5
    dq_ref[...] = turned.T[0:slots].astype(BF)
    dk_ref[...] = jnp.where(lane < HEAD_DIM, d_keys[0], d_keys[1]).astype(BF)
    dv_ref[...] = jnp.where(lane < HEAD_DIM, d_values[0], d_values[1]).astype(BF)


def attend_back(length, proj, grads, mixed, totals, tile=256, first=0, count=None):
    slots = proj.shape[0]
    padded = -(-slots // 128) * 128
    width = proj.shape[1] // 3
    pairs = width // PAIR
    count = pairs if count is None else count

    def spec(off):
        return pl.BlockSpec((slots, PAIR), lambda p, _: (0, off + p))

    return pl.pallas_call(
        functools.partial(attend_back_kernel, slots=slots, padded=padded, tile=tile),
        grid_spec=pltpu.PrefetchScalarGridSpec(
            num_scalar_prefetch=1,
            grid=(count,),
            in_specs=[
                spec(first),
                spec(first + pairs),
                spec(first + 2 * pairs),
                spec(first),
                spec(first),
                pl.BlockSpec((1, 8, padded), lambda p, _: (first + p, 0, 0)),
            ],
            out_specs=[spec(0)] * 3,
            scratch_shapes=[pltpu.VMEM((2, padded, PAIR), BF)] * 2,
        ),
        out_shape=[jax.ShapeDtypeStruct((slots, count * PAIR), BF)] * 3,
        compiler_params=params(40),
        cost_estimate=cost(
            2 * count * 20 * slots * slots * PAIR, slots * width * 16, 2 * count * slots * slots
        ),
        name="attend_back",
    )(length, proj, proj, proj, grads, mixed, totals)


def rest_copies(table, halves, downs, w_out, w_up, w_down, sems):
    width = w_out.shape[0]
    narrow = width // BLOCKS
    wide = w_up.shape[0] // BLOCKS
    half = (wide + narrow) // 2
    copies_out, copies_up, copies_down = [], [], []
    for j in range(2 * BLOCKS):
        block = table[j]
        base = j % 2 * half
        size = half if j < BLOCKS else wide - half
        start = block * wide + j // BLOCKS * half
        copies_up.append(
            pltpu.make_async_copy(
                halves[j // 2].at[pl.ds(base, size)],
                w_up.at[pl.ds(pl.multiple_of(start, 16), size)],
                sems.at[j],
            )
        )
        if j >= BLOCKS:
            copies_out.append(
                pltpu.make_async_copy(
                    halves[j // 2].at[pl.ds(base + size, narrow)],
                    w_out.at[pl.ds(pl.multiple_of(block * narrow, 16), narrow)],
                    sems.at[BLOCKS + j],
                )
            )
        for k in range(2):
            plane = table[2 * BLOCKS + j // BLOCKS * 2 + k]
            copies_down.append(
                pltpu.make_async_copy(
                    downs[j // 2].at[pl.ds((j % 2 * 2 + k) * narrow, narrow)],
                    w_down.at[
                        pl.ds(pl.multiple_of(block * narrow, 16), narrow),
                        pl.ds(pl.multiple_of(plane * width, 128), width),
                    ],
                    sems.at[3 * BLOCKS + j * 2 + k],
                )
            )
    return copies_out, copies_up, copies_down


def middle_kernel(len_ref, table, x_ref, mixed_ref, cot_ref, vec_ref, *refs, chunk):
    blocks, downs = refs[:8], refs[8:16]
    (
        out_ref,
        active_ref,
        d_inner_ref,
        normed_ref,
        d_resid_ref,
        d_branch_ref,
        d_mixed_ref,
        sums_ref,
    ) = refs[16:24]
    w_out, w_up, w_down, sems = refs[24:]
    i = pl.program_id(0)
    tile, width = x_ref.shape
    hidden = w_up.shape[0]

    copies_out, copies_up, copies_down = rest_copies(
        table, blocks, downs, w_out, w_up, w_down, sems
    )

    @pl.when(i == 0)
    def _():
        for copy in copies_out + copies_up + copies_down:
            copy.start()
        sums_ref[...] = jnp.zeros_like(sums_ref)
        for copy in copies_out:
            copy.wait()

    residual = x_ref[...].astype(F32) + nt(mixed_ref[...], w_out[...]) + vec_ref[2:3, :]
    nhat, scale = normalise(residual)
    normed = (nhat * vec_ref[6:7, :] + vec_ref[7:8, :]).astype(BF)
    normed_ref[...] = normed
    rows = lax.broadcasted_iota(jnp.int32, (tile, 1), 0) + i * tile
    seed_low = jnp.where(rows < len_ref[0], cot_ref[...], jnp.zeros_like(cot_ref))
    seed = seed_low.astype(F32)
    ones = jnp.ones((8, tile), BF)

    @pl.when(i == 0)
    def _():
        for copy in copies_up + copies_down:
            copy.wait()

    per = width // chunk

    def step(c, carry):
        out_sum, d_normed = carry
        at = pl.ds(pl.multiple_of(c * chunk, chunk), chunk)
        row = pl.ds(8 + c // per, 1)
        lanes = pl.ds(pl.multiple_of(lax.rem(c, per) * chunk, chunk), chunk)
        inner = nt(normed, w_up[at, :]) + vec_ref[row, lanes]
        cdf = 0.5 + 0.5 * lax.erf(inner * 0.5**0.5)
        active = (inner * cdf).astype(BF)
        active_ref[:, at] = active
        d_active = nn(seed_low, w_down[:, at])
        slope = cdf + inner * (jnp.exp(-0.5 * inner * inner) * 0.3989422804014327)
        d_inner = (d_active * slope).astype(BF)
        d_inner_ref[:, at] = d_inner
        sums_ref[row, lanes] += nn(ones, d_inner)[0:1]
        return (out_sum + nt(active, w_down[:, at]), d_normed + nn(d_inner, w_up[at, :]))

    zero = jnp.zeros((tile, width), F32)
    out_sum, d_normed = lax.fori_loop(0, hidden // chunk, step, (zero, zero), unroll=True)
    out_ref[...] = (residual + out_sum + vec_ref[3:4, :]).astype(BF)
    d_resid = seed + norm_back(d_normed, nhat, scale, vec_ref[6:7, :])
    d_resid_ref[...] = d_resid
    d_branch = d_resid.astype(BF)
    d_branch_ref[...] = d_branch
    d_mixed_ref[...] = nn(d_branch, w_out[...]).astype(BF)
    sums_ref[2:3, :] += jnp.sum(d_resid, axis=0, keepdims=True)
    sums_ref[3:4, :] += jnp.sum(seed, axis=0, keepdims=True)
    sums_ref[6:7, :] += jnp.sum(d_normed * nhat, axis=0, keepdims=True)
    sums_ref[7:8, :] += jnp.sum(d_normed, axis=0, keepdims=True)


def middle(length, table, x, mixed, cot, vec, blocks, downs, hidden, tile, chunk=768):
    slots, width = x.shape

    def rows(columns):
        return pl.BlockSpec((tile, columns), lambda i, *_: (i, 0))

    return pl.pallas_call(
        functools.partial(middle_kernel, chunk=chunk),
        grid_spec=pltpu.PrefetchScalarGridSpec(
            num_scalar_prefetch=2,
            grid=(slots // tile,),
            in_specs=[rows(width)] * 3 + [whole(vec.shape)] + [ANY] * 16,
            out_specs=[
                rows(width),
                rows(hidden),
                rows(hidden),
                rows(width),
                rows(width),
                rows(width),
                rows(width),
                whole(vec.shape),
            ],
            scratch_shapes=[
                pltpu.VMEM((width, width), BF),
                pltpu.VMEM((hidden, width), BF),
                pltpu.VMEM((width, hidden), BF),
                pltpu.SemaphoreType.DMA((7 * BLOCKS,)),
            ],
        ),
        out_shape=[
            jax.ShapeDtypeStruct((slots, width), BF),
            jax.ShapeDtypeStruct((slots, hidden), BF),
            jax.ShapeDtypeStruct((slots, hidden), BF),
            jax.ShapeDtypeStruct((slots, width), BF),
            jax.ShapeDtypeStruct((slots, width), F32),
            jax.ShapeDtypeStruct((slots, width), BF),
            jax.ShapeDtypeStruct((slots, width), BF),
            jax.ShapeDtypeStruct(vec.shape, F32),
        ],
        compiler_params=params(63),
        cost_estimate=cost(
            2 * slots * width * (4 * hidden + 2 * width),
            slots * (hidden * 4 + width * 18) + hidden * width * 4,
            2 * slots * hidden,
        ),
        name="middle",
    )(length, table, x, mixed, cot, vec, *blocks, *downs)


def deliver(copies):
    for copy in copies:
        copy.start()


def collect(copies):
    for copy in copies:
        copy.wait()


def down_grads_kernel(
    len_ref, table, active_ref, cot_ref, keep_ref, send_ref, sums, sems
):
    z = pl.program_id(0)
    slots, width = cot_ref.shape
    narrow = width // BLOCKS
    rows = lax.broadcasted_iota(jnp.int32, (slots, 1), 0)
    seed = jnp.where(rows < len_ref[0], cot_ref[...], jnp.zeros_like(cot_ref))
    sums[z] = tn(seed, active_ref[...]).astype(BF)

    def plane(index):
        copies = []
        for j in range(BLOCKS):
            target = keep_ref if j < 4 else send_ref
            at = pl.ds(pl.multiple_of(table[j] * narrow, 16), narrow)
            copies.append(
                pltpu.make_async_copy(
                    sums.at[index, at],
                    target.at[table[PLACE_AT + index], j % 4],
                    sems.at[index * BLOCKS + j],
                )
            )
        return copies

    deliver(plane(z))

    @pl.when(z == pl.num_programs(0) - 1)
    def _():
        for index in range(4):
            collect(plane(index))


def down_grads(length, table, active, cot):
    slots, width = cot.shape
    hidden = active.shape[1]
    out = jax.ShapeDtypeStruct((4, 4, width // BLOCKS, width), BF)
    return pl.pallas_call(
        down_grads_kernel,
        grid_spec=pltpu.PrefetchScalarGridSpec(
            num_scalar_prefetch=2,
            grid=(hidden // width,),
            in_specs=[pl.BlockSpec((slots, width), lambda z, *_: (0, z)), whole((slots, width))],
            out_specs=[ANY] * 2,
            scratch_shapes=[
                pltpu.VMEM((4, width, width), BF),
                pltpu.SemaphoreType.DMA((4 * BLOCKS,)),
            ],
        ),
        out_shape=[out, out],
        compiler_params=params(63),
        cost_estimate=cost(2 * slots * width * hidden, slots * hidden * 2 + out.size * 4),
        name="down_grads",
    )(length, table, active, cot)


def up_grads_kernel(
    table, d_inner_ref, normed_ref, d_branch_ref, mixed_ref, keep_ref, send_ref, sums, sems
):
    z = pl.program_id(0)
    slots, width = normed_ref.shape
    narrow = width // BLOCKS
    wide = sums.shape[1] - narrow
    up = tn(d_inner_ref[...], normed_ref[...]).astype(BF)
    per = width // wide
    for j in range(per):
        sums[z * per + j, 0:wide, :] = up[j * wide : (j + 1) * wide]

    @pl.when(z == 0)
    def _():
        out = tn(d_branch_ref[...], mixed_ref[...]).astype(BF)
        for g in range(BLOCKS):
            sums[g, wide : wide + narrow, :] = out[g * narrow : (g + 1) * narrow]

    def block(g):
        index = table[RELATIVE_AT + g]
        source = sums.at[g]
        return (
            pltpu.make_async_copy(source, keep_ref.at[lax.rem(index, 4)], sems.at[g]),
            pltpu.make_async_copy(source, send_ref.at[lax.rem(index, 4)], sems.at[g]),
            index < 4,
        )

    for j in range(per):
        keep, send, kept = block(z * per + j)

        @pl.when(kept)
        def _():
            keep.start()

        @pl.when(jnp.logical_not(kept))
        def _():
            send.start()

    @pl.when(z == pl.num_programs(0) - 1)
    def _():
        for g in range(BLOCKS):
            block(g)[0].wait()


def up_grads(table, d_inner, normed, d_branch, mixed):
    slots, width = normed.shape
    hidden = d_inner.shape[1]
    rows = hidden // BLOCKS + width // BLOCKS
    out = jax.ShapeDtypeStruct((4, rows, width), BF)
    return pl.pallas_call(
        up_grads_kernel,
        grid_spec=pltpu.PrefetchScalarGridSpec(
            num_scalar_prefetch=1,
            grid=(hidden // width,),
            in_specs=[pl.BlockSpec((slots, width), lambda z, *_: (0, z))]
            + [whole((slots, width))] * 3,
            out_specs=[ANY] * 2,
            scratch_shapes=[
                pltpu.VMEM((BLOCKS, rows, width), BF),
                pltpu.SemaphoreType.DMA((BLOCKS,)),
            ],
        ),
        out_shape=[out, out],
        compiler_params=params(40),
        cost_estimate=cost(
            2 * slots * width * (hidden + width), slots * hidden * 2 + out.size * 4
        ),
        name="up_grads",
    )(table, d_inner, normed, d_branch, mixed)


def qkv_grads_kernel(table, *refs, count):
    parts_in, normed_ref, (keep_ref, send_ref) = (
        refs[:count],
        refs[count],
        refs[count + 1 : count + 3],
    )
    sums, sems, loads = refs[-3:]
    local, sources = refs[-3 - count : -3], parts_in
    width = normed_ref.shape[1]
    block = sums.shape[0] // BLOCKS
    groups = count // 3
    copies = [
        pltpu.make_async_copy(sources[i], local[i], loads.at[i]) for i in range(count)
    ]
    for s in range(3):
        for i in range(groups):
            copies[i * 3 + s].start()
    for s in range(3):
        start = s * width
        for i in range(groups):
            copies[i * 3 + s].wait()
            part = local[i * 3 + s]
            sums[start : start + part.shape[1], :] = tn(part[...], normed_ref[...]).astype(BF)
            start += part.shape[1]
    copies = [
        pltpu.make_async_copy(
            sums.at[pl.ds(pl.multiple_of(table[j] * block, 16), block)],
            (keep_ref if j < 4 else send_ref).at[j % 4],
            sems.at[j],
        )
        for j in range(BLOCKS)
    ]
    deliver(copies)
    collect(copies)


def qkv_grads(table, d_parts, normed):
    slots, width = normed.shape
    out = jax.ShapeDtypeStruct((4, 3 * width // BLOCKS, width), BF)
    return pl.pallas_call(
        functools.partial(qkv_grads_kernel, count=len(d_parts)),
        grid_spec=pltpu.PrefetchScalarGridSpec(
            num_scalar_prefetch=1,
            grid=(1,),
            in_specs=[ANY] * len(d_parts) + [whole((slots, width))],
            out_specs=[ANY] * 2,
            scratch_shapes=[pltpu.VMEM(part.shape, BF) for part in d_parts]
            + [
                pltpu.VMEM((3 * width, width), BF),
                pltpu.SemaphoreType.DMA((BLOCKS,)),
                pltpu.SemaphoreType.DMA((len(d_parts),)),
            ],
        ),
        out_shape=[out, out],
        compiler_params=params(32),
        cost_estimate=cost(6 * slots * width * width, slots * width * 8 + out.size * 4),
        name="qkv_grads",
    )(table, *d_parts, normed)


def last_kernel(table, x_ref, d_resid_ref, vec_ref, sums_in, *refs, groups):
    parts_in, blocks = refs[: 3 * groups], refs[3 * groups : 3 * groups + 8]
    grad_ref, sums_ref, weights, sems = refs[3 * groups + 8 :]
    i = pl.program_id(0)
    tile, width = x_ref.shape
    copies = qkv_copies(table, blocks, weights, sems)

    @pl.when(i == 0)
    def _():
        for copy in copies:
            copy.start()
        sums_ref[...] = sums_in[...]
        for copy in copies:
            copy.wait()

    ones = jnp.ones((8, tile), BF)
    d_normed = jnp.zeros((tile, width), F32)
    for s in range(3):
        start = 0
        for j in range(groups):
            ref = parts_in[j * 3 + s]
            end = start + ref.shape[1]
            d_normed += nn(ref[...], weights[s * width + start : s * width + end, :])
            if s != 1:
                row = s // 2
                sums_ref[row : row + 1, start:end] += nn(ones, ref[...])[0:1]
            start = end
    nhat, scale = normalise(x_ref[...].astype(F32))
    grad_ref[...] = d_resid_ref[...] + norm_back(d_normed, nhat, scale, vec_ref[4:5, :])
    sums_ref[4:5, :] += jnp.sum(d_normed * nhat, axis=0, keepdims=True)
    sums_ref[5:6, :] += jnp.sum(d_normed, axis=0, keepdims=True)


def last(table, d_parts, x, d_resid, vec, sums, blocks, tile):
    slots, width = x.shape

    def rows(columns):
        return pl.BlockSpec((tile, columns), lambda i, _: (i, 0))

    return pl.pallas_call(
        functools.partial(last_kernel, groups=len(d_parts) // 3),
        grid_spec=pltpu.PrefetchScalarGridSpec(
            num_scalar_prefetch=1,
            grid=(slots // tile,),
            in_specs=[rows(width)] * 2
            + [whole(vec.shape)] * 2
            + [rows(part.shape[1]) for part in d_parts]
            + [ANY] * 8,
            out_specs=[rows(width), whole(vec.shape)],
            scratch_shapes=[
                pltpu.VMEM((3 * width, width), BF),
                pltpu.SemaphoreType.DMA((2 * BLOCKS,)),
            ],
        ),
        out_shape=[
            jax.ShapeDtypeStruct((slots, width), F32),
            jax.ShapeDtypeStruct(vec.shape, F32),
        ],
        compiler_params=params(40),
        cost_estimate=cost(6 * slots * width * width, slots * width * 16),
        name="last",
    )(table, x, d_resid, vec, sums, *d_parts, *blocks)


def fold_kernel(table, *refs):
    terms, outs, turned = refs[:4], refs[4:-1], refs[-1]
    rows = turned.shape[0] // 4
    total = terms[0][...].astype(F32)
    for term in terms[1:]:
        total += term[...].astype(F32)
    turned[...] = total.T

    def plane(k):
        return turned[pl.ds(pl.multiple_of(table[2 * BLOCKS + k] * rows, 8), rows), :]

    if len(outs) == 4:
        for k in range(4):
            outs[k][...] = plane(k).astype(outs[k].dtype)
    else:
        for k in range(4):
            outs[k // 2][k % 2] = plane(PLANES[k]).astype(outs[k // 2].dtype)


def fold(table, terms, paired):
    columns, width = terms[0].shape
    shape = (width // 4, columns)
    if paired:
        out = [jax.ShapeDtypeStruct((2, *shape), dtype) for dtype in (F32, BF)]
    else:
        out = [jax.ShapeDtypeStruct(shape, dtype) for dtype in (F32, BF, BF, BF)]
    return pl.pallas_call(
        fold_kernel,
        grid_spec=pltpu.PrefetchScalarGridSpec(
            num_scalar_prefetch=1,
            grid=(1,),
            in_specs=[whole(terms[0].shape)] * 4,
            out_specs=[whole(o.shape) for o in out],
            scratch_shapes=[pltpu.VMEM((width, columns), F32)],
        ),
        out_shape=out,
        compiler_params=params(16),
        cost_estimate=cost(1e6, columns * width * 12),
        name="fold",
    )(table, *terms)


def swap(values, axis, mask, size):
    return lax.ppermute(values, axis, [(i, i ^ mask) for i in range(size)])


def in_turn(*values):
    return lax.optimization_barrier(values)


def gather_planes(message):
    return [message] + [swap(message, "gx", k, 4) for k in (1, 2, 3)]


def orders(z, g):
    planes, blocks = z ^ jnp.arange(4), g ^ jnp.arange(BLOCKS)
    return jnp.concatenate(
        [
            g ^ jnp.array(MASKS_A),
            g ^ jnp.array(MASKS_B),
            planes,
            planes % 2 * 2 + planes // 2,
            blocks % 2 * 4 + blocks // 2,
        ]
    ).astype(jnp.int32)


def near(first, second):
    return swap(first, "gy", 2, BLOCKS), swap(second, "gy", 4, BLOCKS)


def far(first, second):
    return swap(first, "gy", 4, BLOCKS), swap(second, "gy", 2, BLOCKS)


def join(first, second):
    return jnp.concatenate([first, second], axis=0)


def with_cores(a, b, a_far, b_far):
    a_core, b_core, a_other, b_other = [swap(v, "gy", 1, BLOCKS) for v in (a, b, a_far, b_far)]
    return [a, a_far, a_core, a_other, b, b_far, b_core, b_other]


def add(*terms):
    total = terms[0].astype(F32)
    for term in terms[1:]:
        total = total + term.astype(F32)
    return total


def per_device(
    patches,
    lengths,
    cotangent,
    w_qkv,
    w_out,
    w_up,
    w_down,
    bias_q,
    bias_v,
    bias_o,
    bias_up,
    bias_down,
    gain_one,
    shift_one,
    gain_two,
    shift_two,
    *,
    planes,
    columns,
):
    slots, width = patches.shape
    hidden = w_up.shape[1] * columns
    wide, narrow = hidden // BLOCKS, width // BLOCKS
    tile = slots // 3
    z, g = lax.axis_index("gx"), lax.axis_index("gy")
    fast = planes == 4 and columns == BLOCKS
    vectors = (bias_q, bias_v, bias_o, bias_down, gain_one, shift_one, gain_two, shift_two)
    if fast:
        pos = jnp.stack([z, g]).astype(jnp.int32)
        table = orders(z, g)
        message, own = pack(w_qkv, w_up, w_out, w_down, vectors + (bias_up,))
        pieces = gather_planes(message)
        near_piece = swap(own, "gx", 1, 4)
        block, near_piece = in_turn(arrange_qkv(pos, pieces, width), near_piece)
        edge = own.shape[1] - wide
        up_message = join(own[:, :edge], near_piece[:, :edge])
        down_message = join(own[:, edge:], near_piece[:, edge:])
        qkv_blocks = [block] + [swap(block, "gy", mask, BLOCKS) for mask in MASKS_A[1:4]]
        far_pieces = swap(up_message, "gx", 2, 4)
        far_pieces, *qkv_blocks = in_turn(far_pieces, *qkv_blocks)
        qkv_blocks += [swap(block, "gy", 1, BLOCKS) for block in qkv_blocks]
        ra, rb = arrange_rest(pos, own, near_piece, far_pieces, width, wide + narrow)
        ra, rb, down_message, table = in_turn(ra, rb, down_message, table)
        ra_near, rb_near = near(ra, rb)
        down_far = swap(down_message, "gx", 2, 4)
    else:

        def everything(shard):
            return lax.all_gather(
                lax.all_gather(shard, "gx", axis=0, tiled=True), "gy", axis=1, tiled=True
            ).T

        order = jnp.arange(BLOCKS)
        place = jnp.array(PLANES)
        table = jnp.concatenate([order, order, jnp.arange(4), place, order]).astype(jnp.int32)
        aux = [lax.all_gather(v, AXES, axis=0, tiled=True)[None] for v in vectors]
        aux.append(lax.all_gather(bias_up, AXES, axis=0, tiled=True).reshape(4, width))
        aux.append(jnp.zeros((AUX - 12, width), BF))
        none = jnp.zeros((BLOCKS - 1, AUX, width), BF)
        aux = jnp.concatenate([jnp.concatenate(aux)[None], none])

        def halved(blocks):
            half = blocks.shape[1] // 2
            first, second = blocks[:, :half], blocks[:, half:]
            return list(first.reshape(4, -1, width)) + list(second.reshape(4, -1, width))

        qkv_blocks = list(
            jnp.concatenate([everything(w_qkv).reshape(BLOCKS, -1, width), aux], axis=1)
        )
        up = everything(w_up).reshape(BLOCKS, wide, width)
        out = everything(w_out).reshape(BLOCKS, narrow, width)
        rest_blocks = halved(jnp.concatenate([up, out], axis=1))
        down = everything(w_down).reshape(BLOCKS, narrow, 4, width)
        downs = halved(jnp.transpose(down, (0, 2, 1, 3)).reshape(BLOCKS, wide, width))

    proj, normed, vec = project(table, patches, qkv_blocks)
    if fast:
        ra_near, rb_near, length, proj, down_far = in_turn(
            ra_near, rb_near, lengths, proj, down_far
        )
        ra, rb = join(ra, ra_near), join(rb, rb_near)
        da, db = arrange_down(own, near_piece, down_far)
        length, ra, rb, da, db = in_turn(length, ra, rb, da, db)
        ra_far, rb_far = far(ra, rb)
        da_near, db_near = near(da, db)
        half = HEADS // 4
        mixed, totals = attend(length, proj, 0, half)
        mixed, totals, da_near, db_near = in_turn(mixed, totals, da_near, db_near)
        da, db = join(da, da_near), join(db, db_near)
        length, da, db, mixed, totals = in_turn(length, da, db, mixed, totals)
        da_far, db_far = far(da, db)
        mixed, totals = attend(length, proj, half, half, (mixed, totals))
        mixed, ra, rb, ra_far, rb_far, da, db, da_far, db_far = in_turn(
            mixed, ra, rb, ra_far, rb_far, da, db, da_far, db_far
        )
        rest_blocks = with_cores(ra, rb, ra_far, rb_far)
        downs = with_cores(da, db, da_far, db_far)
    else:
        mixed, totals = attend(lengths, proj)
    out_rows, active, d_inner, normed_two, d_resid, d_branch, d_mixed, sums = middle(
        lengths, table, patches, mixed, cotangent, vec, rest_blocks, downs, hidden, tile
    )
    down_keep, down_send = down_grads(lengths, table, active, cotangent)
    down_keep, down_send, d_inner = in_turn(down_keep, down_send, d_inner)
    up_keep, up_send = up_grads(table, d_inner, normed_two, d_branch, mixed)

    def back(length, first, count):
        return list(
            attend_back(length, proj, d_mixed, mixed, totals, first=first, count=count)
        )

    if fast:
        down_got = swap(down_send, "gy", 1, BLOCKS)
        up_got = swap(up_send, "gy", 1, BLOCKS)
        down_keep, down_got, up_keep = in_turn(down_keep, down_got, up_keep)
        down_next = add(down_keep[2:], down_got[2:]).astype(BF)
        length, down_next = in_turn(lengths, down_next)
        down_near = swap(down_next, "gx", 1, 4)
        d_parts = back(length, 0, 2)
        d_parts[0], up_keep, up_got = in_turn(d_parts[0], up_keep, up_got)
        up_sums = [add(up_keep[r], up_got[r]).astype(BF) for r in range(4)]
        length, *up_sums = in_turn(length, *up_sums)
        up_blocks = [swap(up_sums[r], "gy", MASKS_A[r], BLOCKS) for r in (1, 2, 3)]
        more = back(length, 2, 1)
        more[0], down_near, down_keep = in_turn(more[0], down_near, down_keep)
        d_parts += more
        down_sum = add(down_keep[0], down_got[0], down_near[0])
        down_next = add(down_keep[1], down_got[1], down_near[1]).astype(BF)
        length, down_next, down_sum = in_turn(length, down_next, down_sum)
        down_far = swap(down_next, "gx", 2, 4)
        more = back(length, 3, 3)
        more[0], down_far, *up_blocks = in_turn(more[0], down_far, *up_blocks)
        d_parts += more
        down_sums = [add(down_sum[r], down_far[r]).astype(BF) for r in range(4)]
        up_keep, up_send = fold(table, up_sums[:1] + up_blocks, True)
        table, up_keep, up_send, *down_sums = in_turn(table, up_keep, up_send, *down_sums)
        down_blocks = [swap(down_sums[r], "gy", MASKS_A[r], BLOCKS) for r in (1, 2, 3)]
        up_near = swap(up_send, "gx", 1, 4)
        qkv_keep, qkv_send = qkv_grads(table, d_parts, normed)
        qkv_keep, qkv_send, up_near, *down_blocks = in_turn(
            qkv_keep, qkv_send, up_near, *down_blocks
        )
        qkv_got = swap(qkv_send, "gy", 1, BLOCKS)
        grad_down = add(down_sums[0], *down_blocks).T
        up_sum = add(up_keep[0], up_near[0])
        up_next = add(up_keep[1], up_near[1]).astype(BF)
        qkv_keep, qkv_got, up_next = in_turn(qkv_keep, qkv_got, up_next)
        up_far = swap(up_next, "gx", 2, 4)
        qkv_sums = [add(qkv_keep[r], qkv_got[r]).astype(BF) for r in range(4)]
        table, grad_down, *qkv_sums = in_turn(table, grad_down, *qkv_sums)
        qkv_got = [swap(qkv_sums[r], "gy", MASKS_A[r], BLOCKS) for r in (1, 2, 3)]
        grad_rows, sums = last(table, d_parts, patches, d_resid, vec, sums, qkv_blocks, tile)
        up_far, sums = in_turn(up_far, sums)
        up_sum = add(up_sum, up_far)
        grad_up, grad_out = up_sum[:, :wide], up_sum[:, wide:]
        steps = (("gy", 1, 8), ("gy", 2, 8), ("gy", 4, 8), ("gx", 1, 4), ("gx", 2, 4))
        for axis, mask, size in steps[:3]:
            sums = sums + swap(sums, axis, mask, size)
        table, sums = in_turn(table, sums)
        qkv_pieces = fold(table, qkv_sums[:1] + qkv_got, False)
        sums, *qkv_pieces = in_turn(sums, *qkv_pieces)
        qkv_planes = [swap(qkv_pieces[k], "gx", k, 4) for k in (1, 2, 3)]
        for axis, mask, size in steps[3:]:
            sums = sums + swap(sums, axis, mask, size)
        sums, *qkv_planes = in_turn(sums, *qkv_planes)
        grad_qkv = add(qkv_pieces[0], *qkv_planes)
        device = z * columns + g
        own = lax.dynamic_slice(sums, (0, device * (narrow // 4)), (8, narrow // 4))
        own_up = lax.dynamic_slice(sums, (8 + z, g * narrow), (1, narrow))[0]
        own = [own[j] for j in range(8)]
    else:
        d_parts = back(lengths, 0, 2) + back(lengths, 2, 1) + back(lengths, 3, 3)
        qkv_keep, qkv_send = qkv_grads(table, d_parts, normed)
        grad_rows, sums = last(table, d_parts, patches, d_resid, vec, sums, qkv_blocks, tile)

        def spread(grads):
            part = lax.psum_scatter(grads, "gy", scatter_dimension=0, tiled=True)
            return lax.psum_scatter(part.T, "gx", scatter_dimension=0, tiled=True).astype(F32)

        rest = jnp.concatenate([up_keep, up_send], axis=0)
        grad_up = spread(rest[:, :wide].reshape(hidden, width))
        grad_out = spread(rest[:, wide:].reshape(width, width))
        down = jnp.stack([down_keep, down_send])[:, jnp.array(PLANES)]
        grad_down = spread(jnp.transpose(down, (0, 2, 3, 1, 4)).reshape(width, hidden))
        grad_qkv = spread(jnp.concatenate([qkv_keep, qkv_send]).reshape(3 * width, width))

        def share(vector):
            return lax.psum_scatter(vector, AXES, scatter_dimension=0, tiled=True)

        own = [share(sums[j]) for j in range(8)]
        own_up = share(sums[8:12].reshape(hidden))

    return (
        out_rows,
        grad_rows,
        grad_qkv,
        grad_out,
        grad_up,
        grad_down,
        own[0],
        own[1],
        own[2],
        own_up,
        own[3],
        own[4],
        own[5],
        own[6],
        own[7],
    )


def solution(mesh):
    by_rows = P(AXES, None)
    by_parts = P(AXES)
    matrix = P("gx", "gy")
    in_specs = (by_rows, by_parts, by_rows) + (matrix,) * 4 + (by_parts,) * 9
    out_specs = (by_rows, by_rows) + (matrix,) * 4 + (by_parts,) * 9
    body = functools.partial(per_device, planes=mesh.shape["gx"], columns=mesh.shape["gy"])
    return jax.shard_map(body, mesh=mesh, in_specs=in_specs, out_specs=out_specs, check_vma=False)
```

```python
import functools

import jax
import jax.numpy as jnp
from jax import lax
from jax.experimental import pallas as pl
from jax.experimental.pallas import tpu as pltpu
from jax.sharding import PartitionSpec as P

HEADS = 12
HEAD_DIM = 64
PAIR = 2 * HEAD_DIM
EPSILON = 1e-06
NEG_FILL = -1e30
BF = jnp.bfloat16
F32 = jnp.float32
AXES = ("gx", "gy")
BLOCKS = 8
AUX = 16
MIB = 1 << 20
MASKS_A = (0, 2, 4, 6, 1, 3, 5, 7)
MASKS_B = (0, 4, 2, 6, 1, 5, 3, 7)
PLANES = (0, 2, 1, 3)
PLACE_AT = 2 * BLOCKS + 4
RELATIVE_AT = PLACE_AT + 4
ANY = pl.BlockSpec(memory_space=pl.ANY)


def nt(left, right):
    return lax.dot_general(left, right, (((1,), (1,)), ((), ())), preferred_element_type=F32)


def nn(left, right):
    return lax.dot_general(left, right, (((1,), (0,)), ((), ())), preferred_element_type=F32)


def tn(left, right):
    return lax.dot_general(left, right, (((0,), (0,)), ((), ())), preferred_element_type=F32)


def params(mebibytes):
    return pltpu.CompilerParams(vmem_limit_bytes=mebibytes * MIB)


def cost(flops, bytes_moved, transcendentals=0):
    return pl.CostEstimate(
        flops=int(flops), bytes_accessed=int(bytes_moved), transcendentals=int(transcendentals)
    )


def whole(shape):
    return pl.BlockSpec(shape, lambda *_: (0,) * len(shape))


def normalise(values):
    centre = values - jnp.mean(values, axis=-1, keepdims=True)
    spread = jnp.mean(centre * centre, axis=-1, keepdims=True)
    scale = lax.rsqrt(spread + EPSILON)
    return centre * scale, scale


def norm_back(grads, nhat, scale, gain):
    e = grads * gain
    return scale * (
        e
        - jnp.mean(e, axis=-1, keepdims=True)
        - nhat * jnp.mean(e * nhat, axis=-1, keepdims=True)
    )


def pack_kernel(w_ref, up_ref, out_ref, down_ref, *refs):
    vectors, message_ref, both_ref = refs[:-2], refs[-2], refs[-1]
    rows = w_ref.shape[0]
    message_ref[0:rows, :] = w_ref[...]
    pieces = [ref[...].astype(F32) for ref in vectors]
    message_ref[rows : rows + 8, :] = jnp.broadcast_to(
        jnp.concatenate(pieces, axis=1), (8, message_ref.shape[1])
    ).astype(BF)
    wide, narrow = up_ref.shape[1], out_ref.shape[1]
    edge = both_ref.shape[1] - wide
    both_ref[:, 0:wide] = up_ref[...]
    both_ref[:, wide : wide + narrow] = out_ref[...]
    both_ref[:, wide + narrow : edge] = jnp.zeros(
        (both_ref.shape[0], edge - wide - narrow), BF
    )
    both_ref[0:narrow, edge:] = down_ref[:, 0:wide]
    both_ref[narrow : 2 * narrow, edge:] = down_ref[:, wide : 2 * wide]


def pack(w_qkv, w_up, w_out, w_down, vectors):
    rows, columns = w_qkv.shape
    wide = w_up.shape[1]
    edge = -(-(wide + w_out.shape[1]) // 128) * 128
    return pl.pallas_call(
        pack_kernel,
        out_shape=[
            jax.ShapeDtypeStruct((rows + 8, columns), BF),
            jax.ShapeDtypeStruct((rows, edge + wide), BF),
        ],
        compiler_params=params(63),
        cost_estimate=cost(1e4, rows * (columns + edge + wide) * 4),
        name="pack",
    )(w_qkv, w_up, w_out, w_down.T, *[v[None, :] for v in vectors])


def arrange_qkv_kernel(pos, *refs):
    pieces, out_ref, stacked = refs[:4], refs[4], refs[5]
    width, columns = out_ref.shape[1], pieces[0].shape[1]
    rows = width // 4
    vec_rows = []
    for k in range(4):
        place = pos[0] ^ k
        stacked[pl.ds(pl.multiple_of(place * rows, 8), rows), :] = pieces[k][0:rows, :].astype(F32)
        vec_rows.append(pieces[k][rows : rows + 1, :].astype(F32))
    out_ref[0:columns, :] = stacked[...].T.astype(BF)
    vec = jnp.concatenate(vec_rows, axis=0).astype(BF)
    lane = lax.broadcasted_iota(jnp.int32, (columns, width), 1)
    source = lax.broadcasted_iota(jnp.int32, (columns, width), 0)
    lane4 = lax.broadcasted_iota(jnp.int32, (4, width), 1)
    order = lax.broadcasted_iota(jnp.int32, (4, 1), 0)
    piece = width // (4 * BLOCKS)
    device = (pos[0] ^ order) * BLOCKS + pos[1]
    here = lane4 // piece == device
    base = lane % piece
    rows_out = []
    for j in range(8):
        spread = nn(vec, (source == piece * j + base).astype(BF))
        rows_out.append(jnp.sum(jnp.where(here, spread, 0.0), axis=0, keepdims=True))
    pick = (source == piece * 8 + lane % (4 * piece)).astype(BF)
    spread = jnp.where(lane4 // (4 * piece) == pos[1], nn(vec, pick), 0.0)
    for row in range(4):
        rows_out.append(
            jnp.sum(jnp.where((pos[0] ^ order) == row, spread, 0.0), axis=0, keepdims=True)
        )
    rows_out.append(jnp.zeros((AUX - 12, width), F32))
    out_ref[columns : columns + AUX, :] = jnp.concatenate(rows_out, axis=0).astype(BF)


def arrange_qkv(pos, pieces, width):
    rows, columns = pieces[0].shape
    out = jax.ShapeDtypeStruct((columns + AUX, width), BF)
    return pl.pallas_call(
        arrange_qkv_kernel,
        grid_spec=pltpu.PrefetchScalarGridSpec(
            num_scalar_prefetch=1,
            grid=(1,),
            in_specs=[whole((rows, columns))] * 4,
            out_specs=whole(out.shape),
            scratch_shapes=[pltpu.VMEM((width, columns), F32)],
        ),
        out_shape=out,
        compiler_params=params(16),
        cost_estimate=cost(4e6, 4 * rows * columns * 2 * 2),
        name="arrange_qkv",
    )(pos, *pieces)


def arrange_rest_kernel(pos, own_ref, near_ref, far_ref, first_ref, second_ref, stacked):
    rows = first_ref.shape[1] // 4
    half = first_ref.shape[0]
    edge = far_ref.shape[1]
    pieces = [own_ref[:, 0:edge], near_ref[:, 0:edge], far_ref[0:rows], far_ref[rows : 2 * rows]]
    for k in range(4):
        start = pl.multiple_of((pos[0] ^ k) * rows, 8)
        stacked[pl.ds(start, rows), :] = pieces[k].astype(F32)
    turned = stacked[...].T.astype(BF)
    first_ref[...] = turned[0:half]
    second_ref[...] = turned[half : 2 * half]


def arrange_rest(pos, own, near_piece, far_pieces, width, height):
    out = jax.ShapeDtypeStruct((height // 2, width), BF)
    return pl.pallas_call(
        arrange_rest_kernel,
        grid_spec=pltpu.PrefetchScalarGridSpec(
            num_scalar_prefetch=1,
            grid=(1,),
            in_specs=[whole(own.shape)] * 2 + [whole(far_pieces.shape)],
            out_specs=[whole(out.shape)] * 2,
            scratch_shapes=[pltpu.VMEM((width, far_pieces.shape[1]), F32)],
        ),
        out_shape=[out, out],
        compiler_params=params(16),
        cost_estimate=cost(1e6, out.shape[0] * width * 2 * 4),
        name="arrange_rest",
    )(pos, own, near_piece, far_pieces)


def arrange_down_kernel(own_ref, near_ref, far_ref, first_ref, second_ref):
    wide = far_ref.shape[1]
    rows = own_ref.shape[0]
    narrow = rows // 2
    edge = own_ref.shape[1] - wide
    pieces = [own_ref[:, edge:], near_ref[:, edge:], far_ref[0:rows], far_ref[rows : 2 * rows]]
    for k in range(4):
        target = (first_ref, second_ref)[k // 2]
        at = k % 2 * narrow
        target[at : at + narrow, 0:wide] = pieces[k][0:narrow]
        target[at : at + narrow, wide : 2 * wide] = pieces[k][narrow:rows]


def arrange_down(own, near_piece, far_pieces):
    rows, wide = own.shape[0], far_pieces.shape[1]
    out = jax.ShapeDtypeStruct((rows, 2 * wide), BF)
    return pl.pallas_call(
        arrange_down_kernel,
        out_shape=[out, out],
        compiler_params=params(16),
        cost_estimate=cost(1e4, rows * wide * 2 * 8),
        name="arrange_down",
    )(own, near_piece, far_pieces)


def qkv_copies(table, blocks, weights, sems):
    step = weights.shape[0] // BLOCKS
    return [
        pltpu.make_async_copy(
            blocks[j].at[pl.ds(0, step)],
            weights.at[pl.ds(pl.multiple_of(table[j] * step, 16), step)],
            sems.at[j],
        )
        for j in range(BLOCKS)
    ]


def project_kernel(table, x_ref, *refs):
    blocks, (proj_ref, normed_ref, vec_ref), (weights, aux, sems) = refs[:8], refs[8:11], refs[11:]
    j = pl.program_id(0)
    step = weights.shape[0] // BLOCKS
    tile = proj_ref.shape[1]
    width = x_ref.shape[1]

    @pl.when(j == 0)
    def _():
        small = [
            pltpu.make_async_copy(
                blocks[i].at[pl.ds(step, AUX)], aux.at[i], sems.at[BLOCKS + i]
            )
            for i in range(BLOCKS)
        ]
        large = qkv_copies(table, blocks, weights, sems)
        for copy in small + large:
            copy.start()
        nhat, _ = normalise(x_ref[...].astype(F32))
        for copy in small:
            copy.wait()
        vec_ref[...] = jnp.sum(aux[...].astype(F32), axis=0)
        normed_ref[...] = (nhat * vec_ref[4:5, :] + vec_ref[5:6, :]).astype(BF)
        for copy in large:
            copy.wait()

    per = width // tile
    start = pl.multiple_of(j * tile, tile)
    lanes = pl.ds(pl.multiple_of(lax.rem(j, per) * tile, tile), tile)
    section = j // per
    bias = jnp.where(
        section == 0, vec_ref[0:1, lanes], jnp.where(section == 2, vec_ref[1:2, lanes], 0.0)
    )
    proj_ref[...] = (nt(normed_ref[...], weights[pl.ds(start, tile), :]) + bias).astype(BF)


def project(table, x, blocks, tile=256):
    slots, width = x.shape
    columns = 3 * width
    return pl.pallas_call(
        project_kernel,
        grid_spec=pltpu.PrefetchScalarGridSpec(
            num_scalar_prefetch=1,
            grid=(columns // tile,),
            in_specs=[whole((slots, width))] + [ANY] * 8,
            out_specs=[
                pl.BlockSpec((slots, tile), lambda j, _: (0, j)),
                whole((slots, width)),
                whole((AUX, width)),
            ],
            scratch_shapes=[
                pltpu.VMEM((columns, width), BF),
                pltpu.VMEM((BLOCKS, AUX, width), BF),
                pltpu.SemaphoreType.DMA((3 * BLOCKS,)),
            ],
        ),
        out_shape=[
            jax.ShapeDtypeStruct((slots, columns), BF),
            jax.ShapeDtypeStruct((slots, width), BF),
            jax.ShapeDtypeStruct((AUX, width), F32),
        ],
        compiler_params=params(32),
        cost_estimate=cost(2 * slots * width * columns, slots * width * 10),
        name="project",
    )(table, x, *blocks)


def attend_kernel(len_ref, q_ref, k_ref, v_ref, *refs, slots, padded):
    o_ref, lse_ref, qp = refs[-3:]
    length = len_ref[0]
    lane = lax.broadcasted_iota(jnp.int32, (slots, PAIR), 1)
    row = lax.broadcasted_iota(jnp.int32, (slots, PAIR), 0)
    bias = jnp.where(row < length, 0.0, NEG_FILL)
    keys = k_ref[...].astype(F32)
    values = v_ref[...].astype(F32)
    queries = q_ref[...].astype(F32) * HEAD_DIM**-0.5
    outs = []
    for h in range(2):
        mine = (lane // HEAD_DIM) == h
        spare = (1 - h) * HEAD_DIM
        flag = lane == spare
        key_ext = jnp.where(mine, keys, jnp.where(flag, bias, 0.0)).astype(BF)
        value_ext = jnp.where(mine, values, jnp.where(flag, 1.0, 0.0)).astype(BF)
        qp[h, 0:slots, :] = jnp.where(mine, queries, jnp.where(flag, 1.0, 0.0)).astype(BF)
        if padded > slots:
            qp[h, slots:padded, :] = jnp.zeros((padded - slots, PAIR), BF)
        scores = nt(key_ext, qp[h])
        top = jnp.max(scores, axis=0, keepdims=True)
        weights = jnp.exp(scores - top).astype(BF)
        mixed = nn(value_ext.T, weights)
        total = mixed[spare : spare + 1, :]
        outs.append(mixed[h * HEAD_DIM : (h + 1) * HEAD_DIM, :] / total)
        lse_ref[0, h : h + 1, :] = top + jnp.log(total)
    o_ref[...] = jnp.concatenate(outs, axis=0).T[0:slots].astype(BF)


def attend(length, proj, first=0, count=None, into=()):
    slots = proj.shape[0]
    padded = -(-slots // 128) * 128
    width = proj.shape[1] // 3
    pairs = width // PAIR
    count = pairs if count is None else count

    def spec(off):
        return pl.BlockSpec((slots, PAIR), lambda p, _: (0, off + first + p))

    return pl.pallas_call(
        functools.partial(attend_kernel, slots=slots, padded=padded),
        grid_spec=pltpu.PrefetchScalarGridSpec(
            num_scalar_prefetch=1,
            grid=(count,),
            in_specs=[spec(0), spec(pairs), spec(2 * pairs)] + [ANY] * len(into),
            out_specs=[spec(0), pl.BlockSpec((1, 8, padded), lambda p, _: (first + p, 0, 0))],
            scratch_shapes=[pltpu.VMEM((2, padded, PAIR), BF)],
        ),
        out_shape=[
            jax.ShapeDtypeStruct((slots, width), BF),
            jax.ShapeDtypeStruct((pairs, 8, padded), F32),
        ],
        input_output_aliases={4 + i: i for i in range(len(into))},
        compiler_params=params(63),
        cost_estimate=cost(
            2 * count * 8 * slots * slots * PAIR, slots * width * 8, 2 * count * slots * slots
        ),
        name="attend",
    )(length, proj, proj, proj, *into)


def parts(values):
    high = values.astype(BF).astype(F32)
    rest = values - high
    mid = rest.astype(BF).astype(F32)
    return high, mid, (rest - mid).astype(BF).astype(F32)


def attend_back_kernel(
    len_ref,
    q_ref,
    k_ref,
    v_ref,
    g_ref,
    o_ref,
    lse_ref,
    dq_ref,
    dk_ref,
    dv_ref,
    qp,
    gp,
    *,
    slots,
    padded,
    tile,
):
    length = len_ref[0]
    lane = lax.broadcasted_iota(jnp.int32, (slots, PAIR), 1)
    row = lax.broadcasted_iota(jnp.int32, (slots, PAIR), 0)
    bias = jnp.where(row < length, 0.0, NEG_FILL)
    keys = k_ref[...].astype(F32)
    values = v_ref[...].astype(F32)
    queries = q_ref[...].astype(F32) * HEAD_DIM**-0.5
    grads = g_ref[...].astype(F32)
    products = grads * o_ref[...].astype(F32)
    d_queries, d_keys, d_values = [], [], []
    for h in range(2):
        mine = (lane // HEAD_DIM) == h
        spare = (1 - h) * HEAD_DIM
        flag = lane == spare
        dots = jnp.sum(jnp.where(mine, products, 0.0), axis=1, keepdims=True)
        high, mid, low = parts(-dots)
        ones = (lane >= spare) & (lane < spare + 3)
        value_ext = jnp.where(mine, values, jnp.where(ones, 1.0, 0.0)).astype(BF)
        tail = jnp.where(
            flag, high, jnp.where(lane == spare + 1, mid, jnp.where(lane == spare + 2, low, 0.0))
        )
        gp[h, 0:slots, :] = jnp.where(mine, grads, tail).astype(BF)
        key_ext = jnp.where(mine, keys, jnp.where(flag, bias, 0.0)).astype(BF)
        qp[h, 0:slots, :] = jnp.where(mine, queries, jnp.where(flag, 1.0, 0.0)).astype(BF)
        if padded > slots:
            gp[h, slots:padded, :] = jnp.zeros((padded - slots, PAIR), BF)
            qp[h, slots:padded, :] = jnp.zeros((padded - slots, PAIR), BF)
        keys_turned = key_ext.T[h * HEAD_DIM : (h + 1) * HEAD_DIM]
        d_key = d_value = None
        d_query = []
        for j in range(padded // tile):
            at = slice(j * tile, (j + 1) * tile)
            weights = jnp.exp(nt(key_ext, qp[h, at, :]) - lse_ref[0, h : h + 1, at])
            d_scores = (weights * nt(value_ext, gp[h, at, :])).astype(BF)
            more_value = nn(weights.astype(BF), gp[h, at, :])
            more_key = nn(d_scores, qp[h, at, :])
            d_value = more_value if d_value is None else d_value + more_value
            d_key = more_key if d_key is None else d_key + more_key
            d_query.append(nn(keys_turned, d_scores))
        d_queries.append(jnp.concatenate(d_query, axis=1))
        d_keys.append(d_key)
        d_values.append(d_value)
    turned = jnp.concatenate(d_queries, axis=0) * HEAD_DIM**-0.5
    dq_ref[...] = turned.T[0:slots].astype(BF)
    dk_ref[...] = jnp.where(lane < HEAD_DIM, d_keys[0], d_keys[1]).astype(BF)
    dv_ref[...] = jnp.where(lane < HEAD_DIM, d_values[0], d_values[1]).astype(BF)


def attend_back(length, proj, grads, mixed, totals, tile=256, first=0, count=None):
    slots = proj.shape[0]
    padded = -(-slots // 128) * 128
    width = proj.shape[1] // 3
    pairs = width // PAIR
    count = pairs if count is None else count

    def spec(off):
        return pl.BlockSpec((slots, PAIR), lambda p, _: (0, off + p))

    return pl.pallas_call(
        functools.partial(attend_back_kernel, slots=slots, padded=padded, tile=tile),
        grid_spec=pltpu.PrefetchScalarGridSpec(
            num_scalar_prefetch=1,
            grid=(count,),
            in_specs=[
                spec(first),
                spec(first + pairs),
                spec(first + 2 * pairs),
                spec(first),
                spec(first),
                pl.BlockSpec((1, 8, padded), lambda p, _: (first + p, 0, 0)),
            ],
            out_specs=[spec(0)] * 3,
            scratch_shapes=[pltpu.VMEM((2, padded, PAIR), BF)] * 2,
        ),
        out_shape=[jax.ShapeDtypeStruct((slots, count * PAIR), BF)] * 3,
        compiler_params=params(40),
        cost_estimate=cost(
            2 * count * 20 * slots * slots * PAIR, slots * width * 16, 2 * count * slots * slots
        ),
        name="attend_back",
    )(length, proj, proj, proj, grads, mixed, totals)


def rest_copies(table, halves, downs, w_out, w_up, w_down, sems):
    width = w_out.shape[0]
    narrow = width // BLOCKS
    wide = w_up.shape[0] // BLOCKS
    half = (wide + narrow) // 2
    copies_out, copies_up, copies_down = [], [], []
    for j in range(2 * BLOCKS):
        block = table[j]
        base = j % 2 * half
        size = half if j < BLOCKS else wide - half
        start = block * wide + j // BLOCKS * half
        copies_up.append(
            pltpu.make_async_copy(
                halves[j // 2].at[pl.ds(base, size)],
                w_up.at[pl.ds(pl.multiple_of(start, 16), size)],
                sems.at[j],
            )
        )
        if j >= BLOCKS:
            copies_out.append(
                pltpu.make_async_copy(
                    halves[j // 2].at[pl.ds(base + size, narrow)],
                    w_out.at[pl.ds(pl.multiple_of(block * narrow, 16), narrow)],
                    sems.at[BLOCKS + j],
                )
            )
        for k in range(2):
            plane = table[2 * BLOCKS + j // BLOCKS * 2 + k]
            copies_down.append(
                pltpu.make_async_copy(
                    downs[j // 2].at[pl.ds((j % 2 * 2 + k) * narrow, narrow)],
                    w_down.at[
                        pl.ds(pl.multiple_of(block * narrow, 16), narrow),
                        pl.ds(pl.multiple_of(plane * width, 128), width),
                    ],
                    sems.at[3 * BLOCKS + j * 2 + k],
                )
            )
    return copies_out, copies_up, copies_down


def middle_kernel(len_ref, table, x_ref, mixed_ref, cot_ref, vec_ref, *refs, chunk):
    blocks, downs = refs[:8], refs[8:16]
    (
        out_ref,
        active_ref,
        d_inner_ref,
        normed_ref,
        d_resid_ref,
        d_branch_ref,
        d_mixed_ref,
        sums_ref,
    ) = refs[16:24]
    w_out, w_up, w_down, sems = refs[24:]
    i = pl.program_id(0)
    tile, width = x_ref.shape
    hidden = w_up.shape[0]

    copies_out, copies_up, copies_down = rest_copies(
        table, blocks, downs, w_out, w_up, w_down, sems
    )

    @pl.when(i == 0)
    def _():
        for copy in copies_out + copies_up + copies_down:
            copy.start()
        sums_ref[...] = jnp.zeros_like(sums_ref)
        for copy in copies_out:
            copy.wait()

    residual = x_ref[...].astype(F32) + nt(mixed_ref[...], w_out[...]) + vec_ref[2:3, :]
    nhat, scale = normalise(residual)
    normed = (nhat * vec_ref[6:7, :] + vec_ref[7:8, :]).astype(BF)
    normed_ref[...] = normed
    rows = lax.broadcasted_iota(jnp.int32, (tile, 1), 0) + i * tile
    seed_low = jnp.where(rows < len_ref[0], cot_ref[...], jnp.zeros_like(cot_ref))
    seed = seed_low.astype(F32)
    ones = jnp.ones((8, tile), BF)

    @pl.when(i == 0)
    def _():
        for copy in copies_up + copies_down:
            copy.wait()

    per = width // chunk

    def step(c, carry):
        out_sum, d_normed = carry
        at = pl.ds(pl.multiple_of(c * chunk, chunk), chunk)
        row = pl.ds(8 + c // per, 1)
        lanes = pl.ds(pl.multiple_of(lax.rem(c, per) * chunk, chunk), chunk)
        inner = nt(normed, w_up[at, :]) + vec_ref[row, lanes]
        cdf = 0.5 + 0.5 * lax.erf(inner * 0.5**0.5)
        active = (inner * cdf).astype(BF)
        active_ref[:, at] = active
        d_active = nn(seed_low, w_down[:, at])
        slope = cdf + inner * (jnp.exp(-0.5 * inner * inner) * 0.3989422804014327)
        d_inner = (d_active * slope).astype(BF)
        d_inner_ref[:, at] = d_inner
        sums_ref[row, lanes] += nn(ones, d_inner)[0:1]
        return (out_sum + nt(active, w_down[:, at]), d_normed + nn(d_inner, w_up[at, :]))

    zero = jnp.zeros((tile, width), F32)
    out_sum, d_normed = lax.fori_loop(0, hidden // chunk, step, (zero, zero), unroll=True)
    out_ref[...] = (residual + out_sum + vec_ref[3:4, :]).astype(BF)
    d_resid = seed + norm_back(d_normed, nhat, scale, vec_ref[6:7, :])
    d_resid_ref[...] = d_resid
    d_branch = d_resid.astype(BF)
    d_branch_ref[...] = d_branch
    d_mixed_ref[...] = nn(d_branch, w_out[...]).astype(BF)
    sums_ref[2:3, :] += jnp.sum(d_resid, axis=0, keepdims=True)
    sums_ref[3:4, :] += jnp.sum(seed, axis=0, keepdims=True)
    sums_ref[6:7, :] += jnp.sum(d_normed * nhat, axis=0, keepdims=True)
    sums_ref[7:8, :] += jnp.sum(d_normed, axis=0, keepdims=True)


def middle(length, table, x, mixed, cot, vec, blocks, downs, hidden, tile, chunk=768):
    slots, width = x.shape

    def rows(columns):
        return pl.BlockSpec((tile, columns), lambda i, *_: (i, 0))

    return pl.pallas_call(
        functools.partial(middle_kernel, chunk=chunk),
        grid_spec=pltpu.PrefetchScalarGridSpec(
            num_scalar_prefetch=2,
            grid=(slots // tile,),
            in_specs=[rows(width)] * 3 + [whole(vec.shape)] + [ANY] * 16,
            out_specs=[
                rows(width),
                rows(hidden),
                rows(hidden),
                rows(width),
                rows(width),
                rows(width),
                rows(width),
                whole(vec.shape),
            ],
            scratch_shapes=[
                pltpu.VMEM((width, width), BF),
                pltpu.VMEM((hidden, width), BF),
                pltpu.VMEM((width, hidden), BF),
                pltpu.SemaphoreType.DMA((7 * BLOCKS,)),
            ],
        ),
        out_shape=[
            jax.ShapeDtypeStruct((slots, width), BF),
            jax.ShapeDtypeStruct((slots, hidden), BF),
            jax.ShapeDtypeStruct((slots, hidden), BF),
            jax.ShapeDtypeStruct((slots, width), BF),
            jax.ShapeDtypeStruct((slots, width), F32),
            jax.ShapeDtypeStruct((slots, width), BF),
            jax.ShapeDtypeStruct((slots, width), BF),
            jax.ShapeDtypeStruct(vec.shape, F32),
        ],
        compiler_params=params(63),
        cost_estimate=cost(
            2 * slots * width * (4 * hidden + 2 * width),
            slots * (hidden * 4 + width * 18) + hidden * width * 4,
            2 * slots * hidden,
        ),
        name="middle",
    )(length, table, x, mixed, cot, vec, *blocks, *downs)


def deliver(copies):
    for copy in copies:
        copy.start()


def collect(copies):
    for copy in copies:
        copy.wait()


def down_grads_kernel(
    len_ref, table, active_ref, cot_ref, keep_ref, send_ref, sums, sems
):
    z = pl.program_id(0)
    slots, width = cot_ref.shape
    narrow = width // BLOCKS
    rows = lax.broadcasted_iota(jnp.int32, (slots, 1), 0)
    seed = jnp.where(rows < len_ref[0], cot_ref[...], jnp.zeros_like(cot_ref))
    sums[z] = tn(seed, active_ref[...]).astype(BF)

    def plane(index):
        copies = []
        for j in range(BLOCKS):
            target = keep_ref if j < 4 else send_ref
            at = pl.ds(pl.multiple_of(table[j] * narrow, 16), narrow)
            copies.append(
                pltpu.make_async_copy(
                    sums.at[index, at],
                    target.at[table[PLACE_AT + index], j % 4],
                    sems.at[index * BLOCKS + j],
                )
            )
        return copies

    deliver(plane(z))

    @pl.when(z == pl.num_programs(0) - 1)
    def _():
        for index in range(4):
            collect(plane(index))


def down_grads(length, table, active, cot):
    slots, width = cot.shape
    hidden = active.shape[1]
    out = jax.ShapeDtypeStruct((4, 4, width // BLOCKS, width), BF)
    return pl.pallas_call(
        down_grads_kernel,
        grid_spec=pltpu.PrefetchScalarGridSpec(
            num_scalar_prefetch=2,
            grid=(hidden // width,),
            in_specs=[pl.BlockSpec((slots, width), lambda z, *_: (0, z)), whole((slots, width))],
            out_specs=[ANY] * 2,
            scratch_shapes=[
                pltpu.VMEM((4, width, width), BF),
                pltpu.SemaphoreType.DMA((4 * BLOCKS,)),
            ],
        ),
        out_shape=[out, out],
        compiler_params=params(63),
        cost_estimate=cost(2 * slots * width * hidden, slots * hidden * 2 + out.size * 4),
        name="down_grads",
    )(length, table, active, cot)


def up_grads_kernel(
    table, d_inner_ref, normed_ref, d_branch_ref, mixed_ref, keep_ref, send_ref, sums, sems
):
    z = pl.program_id(0)
    slots, width = normed_ref.shape
    narrow = width // BLOCKS
    wide = sums.shape[1] - narrow
    up = tn(d_inner_ref[...], normed_ref[...]).astype(BF)
    per = width // wide
    for j in range(per):
        sums[z * per + j, 0:wide, :] = up[j * wide : (j + 1) * wide]

    @pl.when(z == 0)
    def _():
        out = tn(d_branch_ref[...], mixed_ref[...]).astype(BF)
        for g in range(BLOCKS):
            sums[g, wide : wide + narrow, :] = out[g * narrow : (g + 1) * narrow]

    def block(g):
        index = table[RELATIVE_AT + g]
        source = sums.at[g]
        return (
            pltpu.make_async_copy(source, keep_ref.at[lax.rem(index, 4)], sems.at[g]),
            pltpu.make_async_copy(source, send_ref.at[lax.rem(index, 4)], sems.at[g]),
            index < 4,
        )

    for j in range(per):
        keep, send, kept = block(z * per + j)

        @pl.when(kept)
        def _():
            keep.start()

        @pl.when(jnp.logical_not(kept))
        def _():
            send.start()

    @pl.when(z == pl.num_programs(0) - 1)
    def _():
        for g in range(BLOCKS):
            block(g)[0].wait()


def up_grads(table, d_inner, normed, d_branch, mixed):
    slots, width = normed.shape
    hidden = d_inner.shape[1]
    rows = hidden // BLOCKS + width // BLOCKS
    out = jax.ShapeDtypeStruct((4, rows, width), BF)
    return pl.pallas_call(
        up_grads_kernel,
        grid_spec=pltpu.PrefetchScalarGridSpec(
            num_scalar_prefetch=1,
            grid=(hidden // width,),
            in_specs=[pl.BlockSpec((slots, width), lambda z, *_: (0, z))]
            + [whole((slots, width))] * 3,
            out_specs=[ANY] * 2,
            scratch_shapes=[
                pltpu.VMEM((BLOCKS, rows, width), BF),
                pltpu.SemaphoreType.DMA((BLOCKS,)),
            ],
        ),
        out_shape=[out, out],
        compiler_params=params(63),
        cost_estimate=cost(
            2 * slots * width * (hidden + width), slots * hidden * 2 + out.size * 4
        ),
        name="up_grads",
    )(table, d_inner, normed, d_branch, mixed)


def qkv_grads_kernel(table, *refs):
    parts_in, normed_ref, (keep_ref, send_ref, sums, sems) = refs[:-5], refs[-5], refs[-4:]
    width = normed_ref.shape[1]
    block = sums.shape[0] // BLOCKS
    groups = len(parts_in) // 3
    for s in range(3):
        start = s * width
        for i in range(groups):
            part = parts_in[i * 3 + s]
            sums[start : start + part.shape[1], :] = tn(part[...], normed_ref[...]).astype(BF)
            start += part.shape[1]
    copies = [
        pltpu.make_async_copy(
            sums.at[pl.ds(pl.multiple_of(table[j] * block, 16), block)],
            (keep_ref if j < 4 else send_ref).at[j % 4],
            sems.at[j],
        )
        for j in range(BLOCKS)
    ]
    deliver(copies)
    collect(copies)


def qkv_grads(table, d_parts, normed):
    slots, width = normed.shape
    out = jax.ShapeDtypeStruct((4, 3 * width // BLOCKS, width), BF)
    return pl.pallas_call(
        qkv_grads_kernel,
        grid_spec=pltpu.PrefetchScalarGridSpec(
            num_scalar_prefetch=1,
            grid=(1,),
            in_specs=[whole(part.shape) for part in d_parts] + [whole((slots, width))],
            out_specs=[ANY] * 2,
            scratch_shapes=[
                pltpu.VMEM((3 * width, width), BF),
                pltpu.SemaphoreType.DMA((BLOCKS,)),
            ],
        ),
        out_shape=[out, out],
        compiler_params=params(40),
        cost_estimate=cost(6 * slots * width * width, slots * width * 8 + out.size * 4),
        name="qkv_grads",
    )(table, *d_parts, normed)


def last_kernel(table, x_ref, d_resid_ref, vec_ref, sums_in, *refs, groups):
    parts_in, blocks = refs[: 3 * groups], refs[3 * groups : 3 * groups + 8]
    grad_ref, sums_ref, weights, sems = refs[3 * groups + 8 :]
    i = pl.program_id(0)
    tile, width = x_ref.shape
    copies = qkv_copies(table, blocks, weights, sems)

    @pl.when(i == 0)
    def _():
        for copy in copies:
            copy.start()
        sums_ref[...] = sums_in[...]
        for copy in copies:
            copy.wait()

    ones = jnp.ones((8, tile), BF)
    d_normed = jnp.zeros((tile, width), F32)
    for s in range(3):
        start = 0
        for j in range(groups):
            ref = parts_in[j * 3 + s]
            end = start + ref.shape[1]
            d_normed += nn(ref[...], weights[s * width + start : s * width + end, :])
            if s != 1:
                row = s // 2
                sums_ref[row : row + 1, start:end] += nn(ones, ref[...])[0:1]
            start = end
    nhat, scale = normalise(x_ref[...].astype(F32))
    grad_ref[...] = d_resid_ref[...] + norm_back(d_normed, nhat, scale, vec_ref[4:5, :])
    sums_ref[4:5, :] += jnp.sum(d_normed * nhat, axis=0, keepdims=True)
    sums_ref[5:6, :] += jnp.sum(d_normed, axis=0, keepdims=True)


def last(table, d_parts, x, d_resid, vec, sums, blocks, tile):
    slots, width = x.shape

    def rows(columns):
        return pl.BlockSpec((tile, columns), lambda i, _: (i, 0))

    return pl.pallas_call(
        functools.partial(last_kernel, groups=len(d_parts) // 3),
        grid_spec=pltpu.PrefetchScalarGridSpec(
            num_scalar_prefetch=1,
            grid=(slots // tile,),
            in_specs=[rows(width)] * 2
            + [whole(vec.shape)] * 2
            + [rows(part.shape[1]) for part in d_parts]
            + [ANY] * 8,
            out_specs=[rows(width), whole(vec.shape)],
            scratch_shapes=[
                pltpu.VMEM((3 * width, width), BF),
                pltpu.SemaphoreType.DMA((2 * BLOCKS,)),
            ],
        ),
        out_shape=[
            jax.ShapeDtypeStruct((slots, width), F32),
            jax.ShapeDtypeStruct(vec.shape, F32),
        ],
        compiler_params=params(40),
        cost_estimate=cost(6 * slots * width * width, slots * width * 16),
        name="last",
    )(table, x, d_resid, vec, sums, *d_parts, *blocks)


def fold_kernel(table, *refs):
    terms, outs, turned = refs[:4], refs[4:-1], refs[-1]
    rows = turned.shape[0] // 4
    total = terms[0][...].astype(F32)
    for term in terms[1:]:
        total += term[...].astype(F32)
    turned[...] = total.T

    def plane(k):
        return turned[pl.ds(pl.multiple_of(table[2 * BLOCKS + k] * rows, 8), rows), :]

    if len(outs) == 4:
        for k in range(4):
            outs[k][...] = plane(k).astype(outs[k].dtype)
    else:
        for k in range(4):
            outs[k // 2][k % 2] = plane(PLANES[k]).astype(outs[k // 2].dtype)


def fold(table, terms, paired):
    columns, width = terms[0].shape
    shape = (width // 4, columns)
    if paired:
        out = [jax.ShapeDtypeStruct((2, *shape), dtype) for dtype in (F32, BF)]
    else:
        out = [jax.ShapeDtypeStruct(shape, dtype) for dtype in (F32, BF, BF, BF)]
    return pl.pallas_call(
        fold_kernel,
        grid_spec=pltpu.PrefetchScalarGridSpec(
            num_scalar_prefetch=1,
            grid=(1,),
            in_specs=[whole(terms[0].shape)] * 4,
            out_specs=[whole(o.shape) for o in out],
            scratch_shapes=[pltpu.VMEM((width, columns), F32)],
        ),
        out_shape=out,
        compiler_params=params(16),
        cost_estimate=cost(1e6, columns * width * 12),
        name="fold",
    )(table, *terms)


def swap(values, axis, mask, size):
    return lax.ppermute(values, axis, [(i, i ^ mask) for i in range(size)])


def in_turn(*values):
    return lax.optimization_barrier(values)


def gather_planes(message):
    return [message] + [swap(message, "gx", k, 4) for k in (1, 2, 3)]


def orders(z, g):
    planes, blocks = z ^ jnp.arange(4), g ^ jnp.arange(BLOCKS)
    return jnp.concatenate(
        [
            g ^ jnp.array(MASKS_A),
            g ^ jnp.array(MASKS_B),
            planes,
            planes % 2 * 2 + planes // 2,
            blocks % 2 * 4 + blocks // 2,
        ]
    ).astype(jnp.int32)


def near(first, second):
    return swap(first, "gy", 2, BLOCKS), swap(second, "gy", 4, BLOCKS)


def far(first, second):
    return swap(first, "gy", 4, BLOCKS), swap(second, "gy", 2, BLOCKS)


def join(first, second):
    return jnp.concatenate([first, second], axis=0)


def with_cores(a, b, a_far, b_far):
    a_core, b_core, a_other, b_other = [swap(v, "gy", 1, BLOCKS) for v in (a, b, a_far, b_far)]
    return [a, a_far, a_core, a_other, b, b_far, b_core, b_other]


def add(*terms):
    total = terms[0].astype(F32)
    for term in terms[1:]:
        total = total + term.astype(F32)
    return total


def per_device(
    patches,
    lengths,
    cotangent,
    w_qkv,
    w_out,
    w_up,
    w_down,
    bias_q,
    bias_v,
    bias_o,
    bias_up,
    bias_down,
    gain_one,
    shift_one,
    gain_two,
    shift_two,
    *,
    planes,
    columns,
):
    slots, width = patches.shape
    hidden = w_up.shape[1] * columns
    wide, narrow = hidden // BLOCKS, width // BLOCKS
    tile = slots // 3
    z, g = lax.axis_index("gx"), lax.axis_index("gy")
    fast = planes == 4 and columns == BLOCKS
    vectors = (bias_q, bias_v, bias_o, bias_down, gain_one, shift_one, gain_two, shift_two)
    if fast:
        pos = jnp.stack([z, g]).astype(jnp.int32)
        table = orders(z, g)
        message, own = pack(w_qkv, w_up, w_out, w_down, vectors + (bias_up,))
        pieces = gather_planes(message)
        near_piece = swap(own, "gx", 1, 4)
        block, near_piece = in_turn(arrange_qkv(pos, pieces, width), near_piece)
        edge = own.shape[1] - wide
        up_message = join(own[:, :edge], near_piece[:, :edge])
        down_message = join(own[:, edge:], near_piece[:, edge:])
        qkv_blocks = [block] + [swap(block, "gy", mask, BLOCKS) for mask in MASKS_A[1:4]]
        far_pieces = swap(up_message, "gx", 2, 4)
        far_pieces, *qkv_blocks = in_turn(far_pieces, *qkv_blocks)
        qkv_blocks += [swap(block, "gy", 1, BLOCKS) for block in qkv_blocks]
        ra, rb = arrange_rest(pos, own, near_piece, far_pieces, width, wide + narrow)
        ra, rb, down_message, table = in_turn(ra, rb, down_message, table)
        ra_near, rb_near = near(ra, rb)
        down_far = swap(down_message, "gx", 2, 4)
    else:

        def everything(shard):
            return lax.all_gather(
                lax.all_gather(shard, "gx", axis=0, tiled=True), "gy", axis=1, tiled=True
            ).T

        order = jnp.arange(BLOCKS)
        place = jnp.array(PLANES)
        table = jnp.concatenate([order, order, jnp.arange(4), place, order]).astype(jnp.int32)
        aux = [lax.all_gather(v, AXES, axis=0, tiled=True)[None] for v in vectors]
        aux.append(lax.all_gather(bias_up, AXES, axis=0, tiled=True).reshape(4, width))
        aux.append(jnp.zeros((AUX - 12, width), BF))
        none = jnp.zeros((BLOCKS - 1, AUX, width), BF)
        aux = jnp.concatenate([jnp.concatenate(aux)[None], none])

        def halved(blocks):
            half = blocks.shape[1] // 2
            first, second = blocks[:, :half], blocks[:, half:]
            return list(first.reshape(4, -1, width)) + list(second.reshape(4, -1, width))

        qkv_blocks = list(
            jnp.concatenate([everything(w_qkv).reshape(BLOCKS, -1, width), aux], axis=1)
        )
        up = everything(w_up).reshape(BLOCKS, wide, width)
        out = everything(w_out).reshape(BLOCKS, narrow, width)
        rest_blocks = halved(jnp.concatenate([up, out], axis=1))
        down = everything(w_down).reshape(BLOCKS, narrow, 4, width)
        downs = halved(jnp.transpose(down, (0, 2, 1, 3)).reshape(BLOCKS, wide, width))

    proj, normed, vec = project(table, patches, qkv_blocks)
    if fast:
        ra_near, rb_near, length, proj, down_far = in_turn(
            ra_near, rb_near, lengths, proj, down_far
        )
        ra, rb = join(ra, ra_near), join(rb, rb_near)
        da, db = arrange_down(own, near_piece, down_far)
        length, ra, rb, da, db = in_turn(length, ra, rb, da, db)
        ra_far, rb_far = far(ra, rb)
        da_near, db_near = near(da, db)
        half = HEADS // 4
        mixed, totals = attend(length, proj, 0, half)
        mixed, totals, da_near, db_near = in_turn(mixed, totals, da_near, db_near)
        da, db = join(da, da_near), join(db, db_near)
        length, da, db, mixed, totals = in_turn(length, da, db, mixed, totals)
        da_far, db_far = far(da, db)
        mixed, totals = attend(length, proj, half, half, (mixed, totals))
        mixed, ra, rb, ra_far, rb_far, da, db, da_far, db_far = in_turn(
            mixed, ra, rb, ra_far, rb_far, da, db, da_far, db_far
        )
        rest_blocks = with_cores(ra, rb, ra_far, rb_far)
        downs = with_cores(da, db, da_far, db_far)
    else:
        mixed, totals = attend(lengths, proj)
    out_rows, active, d_inner, normed_two, d_resid, d_branch, d_mixed, sums = middle(
        lengths, table, patches, mixed, cotangent, vec, rest_blocks, downs, hidden, tile
    )
    down_keep, down_send = down_grads(lengths, table, active, cotangent)
    down_keep, down_send, d_inner = in_turn(down_keep, down_send, d_inner)
    up_keep, up_send = up_grads(table, d_inner, normed_two, d_branch, mixed)

    def back(length, first, count):
        return list(
            attend_back(length, proj, d_mixed, mixed, totals, first=first, count=count)
        )

    if fast:
        down_got = swap(down_send, "gy", 1, BLOCKS)
        up_got = swap(up_send, "gy", 1, BLOCKS)
        down_keep, down_got, up_keep = in_turn(down_keep, down_got, up_keep)
        down_next = add(down_keep[2:], down_got[2:]).astype(BF)
        length, down_next = in_turn(lengths, down_next)
        down_near = swap(down_next, "gx", 1, 4)
        d_parts = back(length, 0, 2)
        d_parts[0], up_keep, up_got = in_turn(d_parts[0], up_keep, up_got)
        up_sums = [add(up_keep[r], up_got[r]).astype(BF) for r in range(4)]
        length, *up_sums = in_turn(length, *up_sums)
        up_blocks = [swap(up_sums[r], "gy", MASKS_A[r], BLOCKS) for r in (1, 2, 3)]
        more = back(length, 2, 1)
        more[0], down_near, down_keep = in_turn(more[0], down_near, down_keep)
        d_parts += more
        down_sum = add(down_keep[0], down_got[0], down_near[0])
        down_next = add(down_keep[1], down_got[1], down_near[1]).astype(BF)
        length, down_next, down_sum = in_turn(length, down_next, down_sum)
        down_far = swap(down_next, "gx", 2, 4)
        more = back(length, 3, 3)
        more[0], down_far, *up_blocks = in_turn(more[0], down_far, *up_blocks)
        d_parts += more
        down_sums = [add(down_sum[r], down_far[r]).astype(BF) for r in range(4)]
        up_keep, up_send = fold(table, up_sums[:1] + up_blocks, True)
        table, up_keep, up_send, *down_sums = in_turn(table, up_keep, up_send, *down_sums)
        down_blocks = [swap(down_sums[r], "gy", MASKS_A[r], BLOCKS) for r in (1, 2, 3)]
        up_near = swap(up_send, "gx", 1, 4)
        qkv_keep, qkv_send = qkv_grads(table, d_parts, normed)
        qkv_keep, qkv_send, up_near, *down_blocks = in_turn(
            qkv_keep, qkv_send, up_near, *down_blocks
        )
        qkv_got = swap(qkv_send, "gy", 1, BLOCKS)
        grad_down = add(down_sums[0], *down_blocks).T
        up_sum = add(up_keep[0], up_near[0])
        up_next = add(up_keep[1], up_near[1]).astype(BF)
        qkv_keep, qkv_got, up_next = in_turn(qkv_keep, qkv_got, up_next)
        up_far = swap(up_next, "gx", 2, 4)
        qkv_sums = [add(qkv_keep[r], qkv_got[r]).astype(BF) for r in range(4)]
        table, grad_down, *qkv_sums = in_turn(table, grad_down, *qkv_sums)
        qkv_got = [swap(qkv_sums[r], "gy", MASKS_A[r], BLOCKS) for r in (1, 2, 3)]
        grad_rows, sums = last(table, d_parts, patches, d_resid, vec, sums, qkv_blocks, tile)
        up_far, sums = in_turn(up_far, sums)
        up_sum = add(up_sum, up_far)
        grad_up, grad_out = up_sum[:, :wide], up_sum[:, wide:]
        steps = (("gy", 1, 8), ("gy", 2, 8), ("gy", 4, 8), ("gx", 1, 4), ("gx", 2, 4))
        for axis, mask, size in steps[:3]:
            sums = sums + swap(sums, axis, mask, size)
        table, sums = in_turn(table, sums)
        qkv_pieces = fold(table, qkv_sums[:1] + qkv_got, False)
        sums, *qkv_pieces = in_turn(sums, *qkv_pieces)
        qkv_planes = [swap(qkv_pieces[k], "gx", k, 4) for k in (1, 2, 3)]
        for axis, mask, size in steps[3:]:
            sums = sums + swap(sums, axis, mask, size)
        sums, *qkv_planes = in_turn(sums, *qkv_planes)
        grad_qkv = add(qkv_pieces[0], *qkv_planes)
        device = z * columns + g
        own = lax.dynamic_slice(sums, (0, device * (narrow // 4)), (8, narrow // 4))
        own_up = lax.dynamic_slice(sums, (8 + z, g * narrow), (1, narrow))[0]
        own = [own[j] for j in range(8)]
    else:
        d_parts = back(lengths, 0, 2) + back(lengths, 2, 1) + back(lengths, 3, 3)
        qkv_keep, qkv_send = qkv_grads(table, d_parts, normed)
        grad_rows, sums = last(table, d_parts, patches, d_resid, vec, sums, qkv_blocks, tile)

        def spread(grads):
            part = lax.psum_scatter(grads, "gy", scatter_dimension=0, tiled=True)
            return lax.psum_scatter(part.T, "gx", scatter_dimension=0, tiled=True).astype(F32)

        rest = jnp.concatenate([up_keep, up_send], axis=0)
        grad_up = spread(rest[:, :wide].reshape(hidden, width))
        grad_out = spread(rest[:, wide:].reshape(width, width))
        down = jnp.stack([down_keep, down_send])[:, jnp.array(PLANES)]
        grad_down = spread(jnp.transpose(down, (0, 2, 3, 1, 4)).reshape(width, hidden))
        grad_qkv = spread(jnp.concatenate([qkv_keep, qkv_send]).reshape(3 * width, width))

        def share(vector):
            return lax.psum_scatter(vector, AXES, scatter_dimension=0, tiled=True)

        own = [share(sums[j]) for j in range(8)]
        own_up = share(sums[8:12].reshape(hidden))

    return (
        out_rows,
        grad_rows,
        grad_qkv,
        grad_out,
        grad_up,
        grad_down,
        own[0],
        own[1],
        own[2],
        own_up,
        own[3],
        own[4],
        own[5],
        own[6],
        own[7],
    )


def solution(mesh):
    by_rows = P(AXES, None)
    by_parts = P(AXES)
    matrix = P("gx", "gy")
    in_specs = (by_rows, by_parts, by_rows) + (matrix,) * 4 + (by_parts,) * 9
    out_specs = (by_rows, by_rows) + (matrix,) * 4 + (by_parts,) * 9
    body = functools.partial(per_device, planes=mesh.shape["gx"], columns=mesh.shape["gy"])
    return jax.shard_map(body, mesh=mesh, in_specs=in_specs, out_specs=out_specs, check_vma=False)
```

```python
import functools

import jax
import jax.numpy as jnp
from jax import lax
from jax.experimental import pallas as pl
from jax.experimental.pallas import tpu as pltpu
from jax.sharding import PartitionSpec as P

HEADS = 12
HEAD_DIM = 64
PAIR = 2 * HEAD_DIM
EPSILON = 1e-06
NEG_FILL = -1e30
BF = jnp.bfloat16
F32 = jnp.float32
AXES = ("gx", "gy")
BLOCKS = 8
AUX = 16
MIB = 1 << 20
MASKS_A = (0, 2, 4, 6, 1, 3, 5, 7)
MASKS_B = (0, 4, 2, 6, 1, 5, 3, 7)
PLANES = (0, 2, 1, 3)
PLACE_AT = 2 * BLOCKS + 4
RELATIVE_AT = PLACE_AT + 4
ANY = pl.BlockSpec(memory_space=pl.ANY)


def nt(left, right):
    return lax.dot_general(left, right, (((1,), (1,)), ((), ())), preferred_element_type=F32)


def nn(left, right):
    return lax.dot_general(left, right, (((1,), (0,)), ((), ())), preferred_element_type=F32)


def tn(left, right):
    return lax.dot_general(left, right, (((0,), (0,)), ((), ())), preferred_element_type=F32)


def params(mebibytes):
    return pltpu.CompilerParams(vmem_limit_bytes=mebibytes * MIB)


def cost(flops, bytes_moved, transcendentals=0):
    return pl.CostEstimate(
        flops=int(flops), bytes_accessed=int(bytes_moved), transcendentals=int(transcendentals)
    )


def whole(shape):
    return pl.BlockSpec(shape, lambda *_: (0,) * len(shape))


def normalise(values):
    centre = values - jnp.mean(values, axis=-1, keepdims=True)
    spread = jnp.mean(centre * centre, axis=-1, keepdims=True)
    scale = lax.rsqrt(spread + EPSILON)
    return centre * scale, scale


def norm_back(grads, nhat, scale, gain):
    e = grads * gain
    return scale * (
        e
        - jnp.mean(e, axis=-1, keepdims=True)
        - nhat * jnp.mean(e * nhat, axis=-1, keepdims=True)
    )


def pack_kernel(w_ref, up_ref, out_ref, down_ref, *refs):
    vectors, message_ref, both_ref = refs[:-2], refs[-2], refs[-1]
    rows = w_ref.shape[0]
    message_ref[0:rows, :] = w_ref[...]
    pieces = [ref[...].astype(F32) for ref in vectors]
    message_ref[rows : rows + 8, :] = jnp.broadcast_to(
        jnp.concatenate(pieces, axis=1), (8, message_ref.shape[1])
    ).astype(BF)
    wide, narrow = up_ref.shape[1], out_ref.shape[1]
    edge = both_ref.shape[1] - wide
    both_ref[:, 0:wide] = up_ref[...]
    both_ref[:, wide : wide + narrow] = out_ref[...]
    both_ref[:, wide + narrow : edge] = jnp.zeros(
        (both_ref.shape[0], edge - wide - narrow), BF
    )
    both_ref[0:narrow, edge:] = down_ref[:, 0:wide]
    both_ref[narrow : 2 * narrow, edge:] = down_ref[:, wide : 2 * wide]


def pack(w_qkv, w_up, w_out, w_down, vectors):
    rows, columns = w_qkv.shape
    wide = w_up.shape[1]
    edge = -(-(wide + w_out.shape[1]) // 128) * 128
    return pl.pallas_call(
        pack_kernel,
        out_shape=[
            jax.ShapeDtypeStruct((rows + 8, columns), BF),
            jax.ShapeDtypeStruct((rows, edge + wide), BF),
        ],
        compiler_params=params(63),
        cost_estimate=cost(1e4, rows * (columns + edge + wide) * 4),
        name="pack",
    )(w_qkv, w_up, w_out, w_down.T, *[v[None, :] for v in vectors])


def arrange_qkv_kernel(pos, *refs):
    pieces, out_ref, stacked = refs[:4], refs[4], refs[5]
    width, columns = out_ref.shape[1], pieces[0].shape[1]
    rows = width // 4
    vec_rows = []
    for k in range(4):
        place = pos[0] ^ k
        stacked[pl.ds(pl.multiple_of(place * rows, 8), rows), :] = pieces[k][0:rows, :].astype(F32)
        vec_rows.append(pieces[k][rows : rows + 1, :].astype(F32))
    out_ref[0:columns, :] = stacked[...].T.astype(BF)
    vec = jnp.concatenate(vec_rows, axis=0).astype(BF)
    lane = lax.broadcasted_iota(jnp.int32, (columns, width), 1)
    source = lax.broadcasted_iota(jnp.int32, (columns, width), 0)
    lane4 = lax.broadcasted_iota(jnp.int32, (4, width), 1)
    order = lax.broadcasted_iota(jnp.int32, (4, 1), 0)
    piece = width // (4 * BLOCKS)
    device = (pos[0] ^ order) * BLOCKS + pos[1]
    here = lane4 // piece == device
    base = lane % piece
    rows_out = []
    for j in range(8):
        spread = nn(vec, (source == piece * j + base).astype(BF))
        rows_out.append(jnp.sum(jnp.where(here, spread, 0.0), axis=0, keepdims=True))
    pick = (source == piece * 8 + lane % (4 * piece)).astype(BF)
    spread = jnp.where(lane4 // (4 * piece) == pos[1], nn(vec, pick), 0.0)
    for row in range(4):
        rows_out.append(
            jnp.sum(jnp.where((pos[0] ^ order) == row, spread, 0.0), axis=0, keepdims=True)
        )
    rows_out.append(jnp.zeros((AUX - 12, width), F32))
    out_ref[columns : columns + AUX, :] = jnp.concatenate(rows_out, axis=0).astype(BF)


def arrange_qkv(pos, pieces, width):
    rows, columns = pieces[0].shape
    out = jax.ShapeDtypeStruct((columns + AUX, width), BF)
    return pl.pallas_call(
        arrange_qkv_kernel,
        grid_spec=pltpu.PrefetchScalarGridSpec(
            num_scalar_prefetch=1,
            grid=(1,),
            in_specs=[whole((rows, columns))] * 4,
            out_specs=whole(out.shape),
            scratch_shapes=[pltpu.VMEM((width, columns), F32)],
        ),
        out_shape=out,
        compiler_params=params(16),
        cost_estimate=cost(4e6, 4 * rows * columns * 2 * 2),
        name="arrange_qkv",
    )(pos, *pieces)


def arrange_rest_kernel(pos, own_ref, near_ref, far_ref, first_ref, second_ref, stacked):
    rows = first_ref.shape[1] // 4
    half = first_ref.shape[0]
    edge = far_ref.shape[1]
    pieces = [own_ref[:, 0:edge], near_ref[:, 0:edge], far_ref[0:rows], far_ref[rows : 2 * rows]]
    for k in range(4):
        start = pl.multiple_of((pos[0] ^ k) * rows, 8)
        stacked[pl.ds(start, rows), :] = pieces[k].astype(F32)
    turned = stacked[...].T.astype(BF)
    first_ref[...] = turned[0:half]
    second_ref[...] = turned[half : 2 * half]


def arrange_rest(pos, own, near_piece, far_pieces, width, height):
    out = jax.ShapeDtypeStruct((height // 2, width), BF)
    return pl.pallas_call(
        arrange_rest_kernel,
        grid_spec=pltpu.PrefetchScalarGridSpec(
            num_scalar_prefetch=1,
            grid=(1,),
            in_specs=[whole(own.shape)] * 2 + [whole(far_pieces.shape)],
            out_specs=[whole(out.shape)] * 2,
            scratch_shapes=[pltpu.VMEM((width, far_pieces.shape[1]), F32)],
        ),
        out_shape=[out, out],
        compiler_params=params(16),
        cost_estimate=cost(1e6, out.shape[0] * width * 2 * 4),
        name="arrange_rest",
    )(pos, own, near_piece, far_pieces)


def arrange_down_kernel(own_ref, near_ref, far_ref, first_ref, second_ref):
    wide = far_ref.shape[1]
    rows = own_ref.shape[0]
    narrow = rows // 2
    edge = own_ref.shape[1] - wide
    pieces = [own_ref[:, edge:], near_ref[:, edge:], far_ref[0:rows], far_ref[rows : 2 * rows]]
    for k in range(4):
        target = (first_ref, second_ref)[k // 2]
        at = k % 2 * narrow
        target[at : at + narrow, 0:wide] = pieces[k][0:narrow]
        target[at : at + narrow, wide : 2 * wide] = pieces[k][narrow:rows]


def arrange_down(own, near_piece, far_pieces):
    rows, wide = own.shape[0], far_pieces.shape[1]
    out = jax.ShapeDtypeStruct((rows, 2 * wide), BF)
    return pl.pallas_call(
        arrange_down_kernel,
        out_shape=[out, out],
        compiler_params=params(16),
        cost_estimate=cost(1e4, rows * wide * 2 * 8),
        name="arrange_down",
    )(own, near_piece, far_pieces)


def qkv_copies(table, blocks, weights, sems):
    step = weights.shape[0] // BLOCKS
    return [
        pltpu.make_async_copy(
            blocks[j].at[pl.ds(0, step)],
            weights.at[pl.ds(pl.multiple_of(table[j] * step, 16), step)],
            sems.at[j],
        )
        for j in range(BLOCKS)
    ]


def project_kernel(table, x_ref, *refs):
    blocks, (proj_ref, normed_ref, vec_ref), (weights, aux, sems) = refs[:8], refs[8:11], refs[11:]
    j = pl.program_id(0)
    step = weights.shape[0] // BLOCKS
    tile = proj_ref.shape[1]
    width = x_ref.shape[1]

    @pl.when(j == 0)
    def _():
        small = [
            pltpu.make_async_copy(
                blocks[i].at[pl.ds(step, AUX)], aux.at[i], sems.at[BLOCKS + i]
            )
            for i in range(BLOCKS)
        ]
        large = qkv_copies(table, blocks, weights, sems)
        for copy in small + large:
            copy.start()
        nhat, _ = normalise(x_ref[...].astype(F32))
        for copy in small:
            copy.wait()
        vec_ref[...] = jnp.sum(aux[...].astype(F32), axis=0)
        normed_ref[...] = (nhat * vec_ref[4:5, :] + vec_ref[5:6, :]).astype(BF)
        for copy in large:
            copy.wait()

    per = width // tile
    start = pl.multiple_of(j * tile, tile)
    lanes = pl.ds(pl.multiple_of(lax.rem(j, per) * tile, tile), tile)
    section = j // per
    bias = jnp.where(
        section == 0, vec_ref[0:1, lanes], jnp.where(section == 2, vec_ref[1:2, lanes], 0.0)
    )
    proj_ref[...] = (nt(normed_ref[...], weights[pl.ds(start, tile), :]) + bias).astype(BF)


def project(table, x, blocks, tile=256):
    slots, width = x.shape
    columns = 3 * width
    return pl.pallas_call(
        project_kernel,
        grid_spec=pltpu.PrefetchScalarGridSpec(
            num_scalar_prefetch=1,
            grid=(columns // tile,),
            in_specs=[whole((slots, width))] + [ANY] * 8,
            out_specs=[
                pl.BlockSpec((slots, tile), lambda j, _: (0, j)),
                whole((slots, width)),
                whole((AUX, width)),
            ],
            scratch_shapes=[
                pltpu.VMEM((columns, width), BF),
                pltpu.VMEM((BLOCKS, AUX, width), BF),
                pltpu.SemaphoreType.DMA((3 * BLOCKS,)),
            ],
        ),
        out_shape=[
            jax.ShapeDtypeStruct((slots, columns), BF),
            jax.ShapeDtypeStruct((slots, width), BF),
            jax.ShapeDtypeStruct((AUX, width), F32),
        ],
        compiler_params=params(32),
        cost_estimate=cost(2 * slots * width * columns, slots * width * 10),
        name="project",
    )(table, x, *blocks)


def attend_kernel(len_ref, q_ref, k_ref, v_ref, *refs, slots, padded):
    o_ref, lse_ref, qp = refs[-3:]
    length = len_ref[0]
    lane = lax.broadcasted_iota(jnp.int32, (slots, PAIR), 1)
    row = lax.broadcasted_iota(jnp.int32, (slots, PAIR), 0)
    bias = jnp.where(row < length, 0.0, NEG_FILL)
    keys = k_ref[...].astype(F32)
    values = v_ref[...].astype(F32)
    queries = q_ref[...].astype(F32) * HEAD_DIM**-0.5
    outs = []
    for h in range(2):
        mine = (lane // HEAD_DIM) == h
        spare = (1 - h) * HEAD_DIM
        flag = lane == spare
        key_ext = jnp.where(mine, keys, jnp.where(flag, bias, 0.0)).astype(BF)
        value_ext = jnp.where(mine, values, jnp.where(flag, 1.0, 0.0)).astype(BF)
        qp[h, 0:slots, :] = jnp.where(mine, queries, jnp.where(flag, 1.0, 0.0)).astype(BF)
        if padded > slots:
            qp[h, slots:padded, :] = jnp.zeros((padded - slots, PAIR), BF)
        scores = nt(key_ext, qp[h])
        top = jnp.max(scores, axis=0, keepdims=True)
        weights = jnp.exp(scores - top).astype(BF)
        mixed = nn(value_ext.T, weights)
        total = mixed[spare : spare + 1, :]
        outs.append(mixed[h * HEAD_DIM : (h + 1) * HEAD_DIM, :] / total)
        lse_ref[0, h : h + 1, :] = top + jnp.log(total)
    o_ref[...] = jnp.concatenate(outs, axis=0).T[0:slots].astype(BF)


def attend(length, proj, first=0, count=None, into=()):
    slots = proj.shape[0]
    padded = -(-slots // 128) * 128
    width = proj.shape[1] // 3
    pairs = width // PAIR
    count = pairs if count is None else count

    def spec(off):
        return pl.BlockSpec((slots, PAIR), lambda p, _: (0, off + first + p))

    return pl.pallas_call(
        functools.partial(attend_kernel, slots=slots, padded=padded),
        grid_spec=pltpu.PrefetchScalarGridSpec(
            num_scalar_prefetch=1,
            grid=(count,),
            in_specs=[spec(0), spec(pairs), spec(2 * pairs)] + [ANY] * len(into),
            out_specs=[spec(0), pl.BlockSpec((1, 8, padded), lambda p, _: (first + p, 0, 0))],
            scratch_shapes=[pltpu.VMEM((2, padded, PAIR), BF)],
        ),
        out_shape=[
            jax.ShapeDtypeStruct((slots, width), BF),
            jax.ShapeDtypeStruct((pairs, 8, padded), F32),
        ],
        input_output_aliases={4 + i: i for i in range(len(into))},
        compiler_params=params(63),
        cost_estimate=cost(
            2 * count * 8 * slots * slots * PAIR, slots * width * 8, 2 * count * slots * slots
        ),
        name="attend",
    )(length, proj, proj, proj, *into)


def parts(values):
    high = values.astype(BF).astype(F32)
    rest = values - high
    mid = rest.astype(BF).astype(F32)
    return high, mid, (rest - mid).astype(BF).astype(F32)


def attend_back_kernel(
    len_ref,
    q_ref,
    k_ref,
    v_ref,
    g_ref,
    o_ref,
    lse_ref,
    dq_ref,
    dk_ref,
    dv_ref,
    qp,
    gp,
    *,
    slots,
    padded,
    tile,
):
    length = len_ref[0]
    lane = lax.broadcasted_iota(jnp.int32, (slots, PAIR), 1)
    row = lax.broadcasted_iota(jnp.int32, (slots, PAIR), 0)
    bias = jnp.where(row < length, 0.0, NEG_FILL)
    keys = k_ref[...].astype(F32)
    values = v_ref[...].astype(F32)
    queries = q_ref[...].astype(F32) * HEAD_DIM**-0.5
    grads = g_ref[...].astype(F32)
    products = grads * o_ref[...].astype(F32)
    d_queries, d_keys, d_values = [], [], []
    for h in range(2):
        mine = (lane // HEAD_DIM) == h
        spare = (1 - h) * HEAD_DIM
        flag = lane == spare
        dots = jnp.sum(jnp.where(mine, products, 0.0), axis=1, keepdims=True)
        high, mid, low = parts(-dots)
        ones = (lane >= spare) & (lane < spare + 3)
        value_ext = jnp.where(mine, values, jnp.where(ones, 1.0, 0.0)).astype(BF)
        tail = jnp.where(
            flag, high, jnp.where(lane == spare + 1, mid, jnp.where(lane == spare + 2, low, 0.0))
        )
        gp[h, 0:slots, :] = jnp.where(mine, grads, tail).astype(BF)
        key_ext = jnp.where(mine, keys, jnp.where(flag, bias, 0.0)).astype(BF)
        qp[h, 0:slots, :] = jnp.where(mine, queries, jnp.where(flag, 1.0, 0.0)).astype(BF)
        if padded > slots:
            gp[h, slots:padded, :] = jnp.zeros((padded - slots, PAIR), BF)
            qp[h, slots:padded, :] = jnp.zeros((padded - slots, PAIR), BF)
        keys_turned = key_ext.T[h * HEAD_DIM : (h + 1) * HEAD_DIM]
        d_key = d_value = None
        d_query = []
        for j in range(padded // tile):
            at = slice(j * tile, (j + 1) * tile)
            weights = jnp.exp(nt(key_ext, qp[h, at, :]) - lse_ref[0, h : h + 1, at])
            d_scores = (weights * nt(value_ext, gp[h, at, :])).astype(BF)
            more_value = nn(weights.astype(BF), gp[h, at, :])
            more_key = nn(d_scores, qp[h, at, :])
            d_value = more_value if d_value is None else d_value + more_value
            d_key = more_key if d_key is None else d_key + more_key
            d_query.append(nn(keys_turned, d_scores))
        d_queries.append(jnp.concatenate(d_query, axis=1))
        d_keys.append(d_key)
        d_values.append(d_value)
    turned = jnp.concatenate(d_queries, axis=0) * HEAD_DIM**-0.5
    dq_ref[...] = turned.T[0:slots].astype(BF)
    dk_ref[...] = jnp.where(lane < HEAD_DIM, d_keys[0], d_keys[1]).astype(BF)
    dv_ref[...] = jnp.where(lane < HEAD_DIM, d_values[0], d_values[1]).astype(BF)


def attend_back(length, proj, grads, mixed, totals, tile=256, first=0, count=None):
    slots = proj.shape[0]
    padded = -(-slots // 128) * 128
    width = proj.shape[1] // 3
    pairs = width // PAIR
    count = pairs if count is None else count

    def spec(off):
        return pl.BlockSpec((slots, PAIR), lambda p, _: (0, off + p))

    return pl.pallas_call(
        functools.partial(attend_back_kernel, slots=slots, padded=padded, tile=tile),
        grid_spec=pltpu.PrefetchScalarGridSpec(
            num_scalar_prefetch=1,
            grid=(count,),
            in_specs=[
                spec(first),
                spec(first + pairs),
                spec(first + 2 * pairs),
                spec(first),
                spec(first),
                pl.BlockSpec((1, 8, padded), lambda p, _: (first + p, 0, 0)),
            ],
            out_specs=[spec(0)] * 3,
            scratch_shapes=[pltpu.VMEM((2, padded, PAIR), BF)] * 2,
        ),
        out_shape=[jax.ShapeDtypeStruct((slots, count * PAIR), BF)] * 3,
        compiler_params=params(32),
        cost_estimate=cost(
            2 * count * 20 * slots * slots * PAIR, slots * width * 16, 2 * count * slots * slots
        ),
        name="attend_back",
    )(length, proj, proj, proj, grads, mixed, totals)


def rest_copies(table, halves, downs, w_out, w_up, w_down, sems):
    width = w_out.shape[0]
    narrow = width // BLOCKS
    wide = w_up.shape[0] // BLOCKS
    half = (wide + narrow) // 2
    copies_out, copies_up, copies_down = [], [], []
    for j in range(2 * BLOCKS):
        block = table[j]
        base = j % 2 * half
        size = half if j < BLOCKS else wide - half
        start = block * wide + j // BLOCKS * half
        copies_up.append(
            pltpu.make_async_copy(
                halves[j // 2].at[pl.ds(base, size)],
                w_up.at[pl.ds(pl.multiple_of(start, 16), size)],
                sems.at[j],
            )
        )
        if j >= BLOCKS:
            copies_out.append(
                pltpu.make_async_copy(
                    halves[j // 2].at[pl.ds(base + size, narrow)],
                    w_out.at[pl.ds(pl.multiple_of(block * narrow, 16), narrow)],
                    sems.at[BLOCKS + j],
                )
            )
        for k in range(2):
            plane = table[2 * BLOCKS + j // BLOCKS * 2 + k]
            copies_down.append(
                pltpu.make_async_copy(
                    downs[j // 2].at[pl.ds((j % 2 * 2 + k) * narrow, narrow)],
                    w_down.at[
                        pl.ds(pl.multiple_of(block * narrow, 16), narrow),
                        pl.ds(pl.multiple_of(plane * width, 128), width),
                    ],
                    sems.at[3 * BLOCKS + j * 2 + k],
                )
            )
    return copies_out, copies_up, copies_down


def middle_kernel(len_ref, table, x_ref, mixed_ref, cot_ref, vec_ref, *refs, chunk):
    blocks, downs = refs[:8], refs[8:16]
    (
        out_ref,
        active_ref,
        d_inner_ref,
        normed_ref,
        d_resid_ref,
        d_branch_ref,
        d_mixed_ref,
        sums_ref,
    ) = refs[16:24]
    w_out, w_up, w_down, sems = refs[24:]
    i = pl.program_id(0)
    tile, width = x_ref.shape
    hidden = w_up.shape[0]

    copies_out, copies_up, copies_down = rest_copies(
        table, blocks, downs, w_out, w_up, w_down, sems
    )

    @pl.when(i == 0)
    def _():
        for copy in copies_out + copies_up + copies_down:
            copy.start()
        sums_ref[...] = jnp.zeros_like(sums_ref)
        for copy in copies_out:
            copy.wait()

    residual = x_ref[...].astype(F32) + nt(mixed_ref[...], w_out[...]) + vec_ref[2:3, :]
    nhat, scale = normalise(residual)
    normed = (nhat * vec_ref[6:7, :] + vec_ref[7:8, :]).astype(BF)
    normed_ref[...] = normed
    rows = lax.broadcasted_iota(jnp.int32, (tile, 1), 0) + i * tile
    seed_low = jnp.where(rows < len_ref[0], cot_ref[...], jnp.zeros_like(cot_ref))
    seed = seed_low.astype(F32)
    ones = jnp.ones((8, tile), BF)

    @pl.when(i == 0)
    def _():
        for copy in copies_up + copies_down:
            copy.wait()

    per = width // chunk

    def step(c, carry):
        out_sum, d_normed = carry
        at = pl.ds(pl.multiple_of(c * chunk, chunk), chunk)
        row = pl.ds(8 + c // per, 1)
        lanes = pl.ds(pl.multiple_of(lax.rem(c, per) * chunk, chunk), chunk)
        inner = nt(normed, w_up[at, :]) + vec_ref[row, lanes]
        cdf = 0.5 + 0.5 * lax.erf(inner * 0.5**0.5)
        active = (inner * cdf).astype(BF)
        active_ref[:, at] = active
        d_active = nn(seed_low, w_down[:, at])
        slope = cdf + inner * (jnp.exp(-0.5 * inner * inner) * 0.3989422804014327)
        d_inner = (d_active * slope).astype(BF)
        d_inner_ref[:, at] = d_inner
        sums_ref[row, lanes] += nn(ones, d_inner)[0:1]
        return (out_sum + nt(active, w_down[:, at]), d_normed + nn(d_inner, w_up[at, :]))

    zero = jnp.zeros((tile, width), F32)
    out_sum, d_normed = lax.fori_loop(0, hidden // chunk, step, (zero, zero), unroll=True)
    out_ref[...] = (residual + out_sum + vec_ref[3:4, :]).astype(BF)
    d_resid = seed + norm_back(d_normed, nhat, scale, vec_ref[6:7, :])
    d_resid_ref[...] = d_resid
    d_branch = d_resid.astype(BF)
    d_branch_ref[...] = d_branch
    d_mixed_ref[...] = nn(d_branch, w_out[...]).astype(BF)
    sums_ref[2:3, :] += jnp.sum(d_resid, axis=0, keepdims=True)
    sums_ref[3:4, :] += jnp.sum(seed, axis=0, keepdims=True)
    sums_ref[6:7, :] += jnp.sum(d_normed * nhat, axis=0, keepdims=True)
    sums_ref[7:8, :] += jnp.sum(d_normed, axis=0, keepdims=True)


def middle(length, table, x, mixed, cot, vec, blocks, downs, hidden, tile, chunk=768):
    slots, width = x.shape

    def rows(columns):
        return pl.BlockSpec((tile, columns), lambda i, *_: (i, 0))

    return pl.pallas_call(
        functools.partial(middle_kernel, chunk=chunk),
        grid_spec=pltpu.PrefetchScalarGridSpec(
            num_scalar_prefetch=2,
            grid=(slots // tile,),
            in_specs=[rows(width)] * 3 + [whole(vec.shape)] + [ANY] * 16,
            out_specs=[
                rows(width),
                rows(hidden),
                rows(hidden),
                rows(width),
                rows(width),
                rows(width),
                rows(width),
                whole(vec.shape),
            ],
            scratch_shapes=[
                pltpu.VMEM((width, width), BF),
                pltpu.VMEM((hidden, width), BF),
                pltpu.VMEM((width, hidden), BF),
                pltpu.SemaphoreType.DMA((7 * BLOCKS,)),
            ],
        ),
        out_shape=[
            jax.ShapeDtypeStruct((slots, width), BF),
            jax.ShapeDtypeStruct((slots, hidden), BF),
            jax.ShapeDtypeStruct((slots, hidden), BF),
            jax.ShapeDtypeStruct((slots, width), BF),
            jax.ShapeDtypeStruct((slots, width), F32),
            jax.ShapeDtypeStruct((slots, width), BF),
            jax.ShapeDtypeStruct((slots, width), BF),
            jax.ShapeDtypeStruct(vec.shape, F32),
        ],
        compiler_params=params(63),
        cost_estimate=cost(
            2 * slots * width * (4 * hidden + 2 * width),
            slots * (hidden * 4 + width * 18) + hidden * width * 4,
            2 * slots * hidden,
        ),
        name="middle",
    )(length, table, x, mixed, cot, vec, *blocks, *downs)


def deliver(copies):
    for copy in copies:
        copy.start()


def collect(copies):
    for copy in copies:
        copy.wait()


def down_grads_kernel(
    len_ref, table, active_ref, cot_ref, keep_ref, send_ref, sums, sems
):
    z = pl.program_id(0)
    slots, width = cot_ref.shape
    narrow = width // BLOCKS
    rows = lax.broadcasted_iota(jnp.int32, (slots, 1), 0)
    seed = jnp.where(rows < len_ref[0], cot_ref[...], jnp.zeros_like(cot_ref))
    sums[z] = tn(seed, active_ref[...]).astype(BF)

    def plane(index):
        copies = []
        for j in range(BLOCKS):
            target = keep_ref if j < 4 else send_ref
            at = pl.ds(pl.multiple_of(table[j] * narrow, 16), narrow)
            copies.append(
                pltpu.make_async_copy(
                    sums.at[index, at],
                    target.at[table[PLACE_AT + index], j % 4],
                    sems.at[index * BLOCKS + j],
                )
            )
        return copies

    deliver(plane(z))

    @pl.when(z == pl.num_programs(0) - 1)
    def _():
        for index in range(4):
            collect(plane(index))


def down_grads(length, table, active, cot):
    slots, width = cot.shape
    hidden = active.shape[1]
    out = jax.ShapeDtypeStruct((4, 4, width // BLOCKS, width), BF)
    return pl.pallas_call(
        down_grads_kernel,
        grid_spec=pltpu.PrefetchScalarGridSpec(
            num_scalar_prefetch=2,
            grid=(hidden // width,),
            in_specs=[pl.BlockSpec((slots, width), lambda z, *_: (0, z)), whole((slots, width))],
            out_specs=[ANY] * 2,
            scratch_shapes=[
                pltpu.VMEM((4, width, width), BF),
                pltpu.SemaphoreType.DMA((4 * BLOCKS,)),
            ],
        ),
        out_shape=[out, out],
        compiler_params=params(63),
        cost_estimate=cost(2 * slots * width * hidden, slots * hidden * 2 + out.size * 4),
        name="down_grads",
    )(length, table, active, cot)


def up_grads_kernel(
    table, d_inner_ref, normed_ref, d_branch_ref, mixed_ref, keep_ref, send_ref, sums, sems
):
    z = pl.program_id(0)
    slots, width = normed_ref.shape
    narrow = width // BLOCKS
    wide = sums.shape[1] - narrow
    up = tn(d_inner_ref[...], normed_ref[...]).astype(BF)
    per = width // wide
    for j in range(per):
        sums[z * per + j, 0:wide, :] = up[j * wide : (j + 1) * wide]

    @pl.when(z == 0)
    def _():
        out = tn(d_branch_ref[...], mixed_ref[...]).astype(BF)
        for g in range(BLOCKS):
            sums[g, wide : wide + narrow, :] = out[g * narrow : (g + 1) * narrow]

    def block(g):
        index = table[RELATIVE_AT + g]
        source = sums.at[g]
        return (
            pltpu.make_async_copy(source, keep_ref.at[lax.rem(index, 4)], sems.at[g]),
            pltpu.make_async_copy(source, send_ref.at[lax.rem(index, 4)], sems.at[g]),
            index < 4,
        )

    for j in range(per):
        keep, send, kept = block(z * per + j)

        @pl.when(kept)
        def _():
            keep.start()

        @pl.when(jnp.logical_not(kept))
        def _():
            send.start()

    @pl.when(z == pl.num_programs(0) - 1)
    def _():
        for g in range(BLOCKS):
            block(g)[0].wait()


def up_grads(table, d_inner, normed, d_branch, mixed):
    slots, width = normed.shape
    hidden = d_inner.shape[1]
    rows = hidden // BLOCKS + width // BLOCKS
    out = jax.ShapeDtypeStruct((4, rows, width), BF)
    return pl.pallas_call(
        up_grads_kernel,
        grid_spec=pltpu.PrefetchScalarGridSpec(
            num_scalar_prefetch=1,
            grid=(hidden // width,),
            in_specs=[pl.BlockSpec((slots, width), lambda z, *_: (0, z))]
            + [whole((slots, width))] * 3,
            out_specs=[ANY] * 2,
            scratch_shapes=[
                pltpu.VMEM((BLOCKS, rows, width), BF),
                pltpu.SemaphoreType.DMA((BLOCKS,)),
            ],
        ),
        out_shape=[out, out],
        compiler_params=params(63),
        cost_estimate=cost(
            2 * slots * width * (hidden + width), slots * hidden * 2 + out.size * 4
        ),
        name="up_grads",
    )(table, d_inner, normed, d_branch, mixed)


def qkv_grads_kernel(table, *refs):
    parts_in, normed_ref, (keep_ref, send_ref, sums, sems) = refs[:-5], refs[-5], refs[-4:]
    width = normed_ref.shape[1]
    block = sums.shape[0] // BLOCKS
    groups = len(parts_in) // 3
    for s in range(3):
        start = s * width
        for i in range(groups):
            part = parts_in[i * 3 + s]
            sums[start : start + part.shape[1], :] = tn(part[...], normed_ref[...]).astype(BF)
            start += part.shape[1]
    copies = [
        pltpu.make_async_copy(
            sums.at[pl.ds(pl.multiple_of(table[j] * block, 16), block)],
            (keep_ref if j < 4 else send_ref).at[j % 4],
            sems.at[j],
        )
        for j in range(BLOCKS)
    ]
    deliver(copies)
    collect(copies)


def qkv_grads(table, d_parts, normed):
    slots, width = normed.shape
    out = jax.ShapeDtypeStruct((4, 3 * width // BLOCKS, width), BF)
    return pl.pallas_call(
        qkv_grads_kernel,
        grid_spec=pltpu.PrefetchScalarGridSpec(
            num_scalar_prefetch=1,
            grid=(1,),
            in_specs=[whole(part.shape) for part in d_parts] + [whole((slots, width))],
            out_specs=[ANY] * 2,
            scratch_shapes=[
                pltpu.VMEM((3 * width, width), BF),
                pltpu.SemaphoreType.DMA((BLOCKS,)),
            ],
        ),
        out_shape=[out, out],
        compiler_params=params(40),
        cost_estimate=cost(6 * slots * width * width, slots * width * 8 + out.size * 4),
        name="qkv_grads",
    )(table, *d_parts, normed)


def last_kernel(table, x_ref, d_resid_ref, vec_ref, sums_in, *refs, groups):
    parts_in, blocks = refs[: 3 * groups], refs[3 * groups : 3 * groups + 8]
    grad_ref, sums_ref, weights, sems = refs[3 * groups + 8 :]
    i = pl.program_id(0)
    tile, width = x_ref.shape
    copies = qkv_copies(table, blocks, weights, sems)

    @pl.when(i == 0)
    def _():
        for copy in copies:
            copy.start()
        sums_ref[...] = sums_in[...]
        for copy in copies:
            copy.wait()

    ones = jnp.ones((8, tile), BF)
    d_normed = jnp.zeros((tile, width), F32)
    for s in range(3):
        start = 0
        for j in range(groups):
            ref = parts_in[j * 3 + s]
            end = start + ref.shape[1]
            d_normed += nn(ref[...], weights[s * width + start : s * width + end, :])
            if s != 1:
                row = s // 2
                sums_ref[row : row + 1, start:end] += nn(ones, ref[...])[0:1]
            start = end
    nhat, scale = normalise(x_ref[...].astype(F32))
    grad_ref[...] = d_resid_ref[...] + norm_back(d_normed, nhat, scale, vec_ref[4:5, :])
    sums_ref[4:5, :] += jnp.sum(d_normed * nhat, axis=0, keepdims=True)
    sums_ref[5:6, :] += jnp.sum(d_normed, axis=0, keepdims=True)


def last(table, d_parts, x, d_resid, vec, sums, blocks, tile):
    slots, width = x.shape

    def rows(columns):
        return pl.BlockSpec((tile, columns), lambda i, _: (i, 0))

    return pl.pallas_call(
        functools.partial(last_kernel, groups=len(d_parts) // 3),
        grid_spec=pltpu.PrefetchScalarGridSpec(
            num_scalar_prefetch=1,
            grid=(slots // tile,),
            in_specs=[rows(width)] * 2
            + [whole(vec.shape)] * 2
            + [rows(part.shape[1]) for part in d_parts]
            + [ANY] * 8,
            out_specs=[rows(width), whole(vec.shape)],
            scratch_shapes=[
                pltpu.VMEM((3 * width, width), BF),
                pltpu.SemaphoreType.DMA((2 * BLOCKS,)),
            ],
        ),
        out_shape=[
            jax.ShapeDtypeStruct((slots, width), F32),
            jax.ShapeDtypeStruct(vec.shape, F32),
        ],
        compiler_params=params(24),
        cost_estimate=cost(6 * slots * width * width, slots * width * 16),
        name="last",
    )(table, x, d_resid, vec, sums, *d_parts, *blocks)


def fold_kernel(table, *refs):
    terms, outs, turned = refs[:4], refs[4:-1], refs[-1]
    rows = turned.shape[0] // 4
    total = terms[0][...].astype(F32)
    for term in terms[1:]:
        total += term[...].astype(F32)
    turned[...] = total.T

    def plane(k):
        return turned[pl.ds(pl.multiple_of(table[2 * BLOCKS + k] * rows, 8), rows), :]

    if len(outs) == 4:
        for k in range(4):
            outs[k][...] = plane(k).astype(outs[k].dtype)
    else:
        for k in range(4):
            outs[k // 2][k % 2] = plane(PLANES[k]).astype(outs[k // 2].dtype)


def fold(table, terms, paired):
    columns, width = terms[0].shape
    shape = (width // 4, columns)
    if paired:
        out = [jax.ShapeDtypeStruct((2, *shape), dtype) for dtype in (F32, BF)]
    else:
        out = [jax.ShapeDtypeStruct(shape, dtype) for dtype in (F32, BF, BF, BF)]
    return pl.pallas_call(
        fold_kernel,
        grid_spec=pltpu.PrefetchScalarGridSpec(
            num_scalar_prefetch=1,
            grid=(1,),
            in_specs=[whole(terms[0].shape)] * 4,
            out_specs=[whole(o.shape) for o in out],
            scratch_shapes=[pltpu.VMEM((width, columns), F32)],
        ),
        out_shape=out,
        compiler_params=params(16),
        cost_estimate=cost(1e6, columns * width * 12),
        name="fold",
    )(table, *terms)


def swap(values, axis, mask, size):
    return lax.ppermute(values, axis, [(i, i ^ mask) for i in range(size)])


def in_turn(*values):
    return lax.optimization_barrier(values)


def gather_planes(message):
    return [message] + [swap(message, "gx", k, 4) for k in (1, 2, 3)]


def orders(z, g):
    planes, blocks = z ^ jnp.arange(4), g ^ jnp.arange(BLOCKS)
    return jnp.concatenate(
        [
            g ^ jnp.array(MASKS_A),
            g ^ jnp.array(MASKS_B),
            planes,
            planes % 2 * 2 + planes // 2,
            blocks % 2 * 4 + blocks // 2,
        ]
    ).astype(jnp.int32)


def near(first, second):
    return swap(first, "gy", 2, BLOCKS), swap(second, "gy", 4, BLOCKS)


def far(first, second):
    return swap(first, "gy", 4, BLOCKS), swap(second, "gy", 2, BLOCKS)


def join(first, second):
    return jnp.concatenate([first, second], axis=0)


def with_cores(a, b, a_far, b_far):
    a_core, b_core, a_other, b_other = [swap(v, "gy", 1, BLOCKS) for v in (a, b, a_far, b_far)]
    return [a, a_far, a_core, a_other, b, b_far, b_core, b_other]


def add(*terms):
    total = terms[0].astype(F32)
    for term in terms[1:]:
        total = total + term.astype(F32)
    return total


def per_device(
    patches,
    lengths,
    cotangent,
    w_qkv,
    w_out,
    w_up,
    w_down,
    bias_q,
    bias_v,
    bias_o,
    bias_up,
    bias_down,
    gain_one,
    shift_one,
    gain_two,
    shift_two,
    *,
    planes,
    columns,
):
    slots, width = patches.shape
    hidden = w_up.shape[1] * columns
    wide, narrow = hidden // BLOCKS, width // BLOCKS
    tile = slots // 3
    z, g = lax.axis_index("gx"), lax.axis_index("gy")
    fast = planes == 4 and columns == BLOCKS
    vectors = (bias_q, bias_v, bias_o, bias_down, gain_one, shift_one, gain_two, shift_two)
    if fast:
        pos = jnp.stack([z, g]).astype(jnp.int32)
        table = orders(z, g)
        message, own = pack(w_qkv, w_up, w_out, w_down, vectors + (bias_up,))
        pieces = gather_planes(message)
        near_piece = swap(own, "gx", 1, 4)
        block, near_piece = in_turn(arrange_qkv(pos, pieces, width), near_piece)
        edge = own.shape[1] - wide
        up_message = join(own[:, :edge], near_piece[:, :edge])
        down_message = join(own[:, edge:], near_piece[:, edge:])
        qkv_blocks = [block] + [swap(block, "gy", mask, BLOCKS) for mask in MASKS_A[1:4]]
        far_pieces = swap(up_message, "gx", 2, 4)
        far_pieces, *qkv_blocks = in_turn(far_pieces, *qkv_blocks)
        qkv_blocks += [swap(block, "gy", 1, BLOCKS) for block in qkv_blocks]
        ra, rb = arrange_rest(pos, own, near_piece, far_pieces, width, wide + narrow)
        ra, rb, down_message, table = in_turn(ra, rb, down_message, table)
        ra_near, rb_near = near(ra, rb)
        down_far = swap(down_message, "gx", 2, 4)
    else:

        def everything(shard):
            return lax.all_gather(
                lax.all_gather(shard, "gx", axis=0, tiled=True), "gy", axis=1, tiled=True
            ).T

        order = jnp.arange(BLOCKS)
        place = jnp.array(PLANES)
        table = jnp.concatenate([order, order, jnp.arange(4), place, order]).astype(jnp.int32)
        aux = [lax.all_gather(v, AXES, axis=0, tiled=True)[None] for v in vectors]
        aux.append(lax.all_gather(bias_up, AXES, axis=0, tiled=True).reshape(4, width))
        aux.append(jnp.zeros((AUX - 12, width), BF))
        none = jnp.zeros((BLOCKS - 1, AUX, width), BF)
        aux = jnp.concatenate([jnp.concatenate(aux)[None], none])

        def halved(blocks):
            half = blocks.shape[1] // 2
            first, second = blocks[:, :half], blocks[:, half:]
            return list(first.reshape(4, -1, width)) + list(second.reshape(4, -1, width))

        qkv_blocks = list(
            jnp.concatenate([everything(w_qkv).reshape(BLOCKS, -1, width), aux], axis=1)
        )
        up = everything(w_up).reshape(BLOCKS, wide, width)
        out = everything(w_out).reshape(BLOCKS, narrow, width)
        rest_blocks = halved(jnp.concatenate([up, out], axis=1))
        down = everything(w_down).reshape(BLOCKS, narrow, 4, width)
        downs = halved(jnp.transpose(down, (0, 2, 1, 3)).reshape(BLOCKS, wide, width))

    proj, normed, vec = project(table, patches, qkv_blocks)
    if fast:
        ra_near, rb_near, length, proj, down_far = in_turn(
            ra_near, rb_near, lengths, proj, down_far
        )
        ra, rb = join(ra, ra_near), join(rb, rb_near)
        da, db = arrange_down(own, near_piece, down_far)
        length, ra, rb, da, db = in_turn(length, ra, rb, da, db)
        ra_far, rb_far = far(ra, rb)
        da_near, db_near = near(da, db)
        half = HEADS // 4
        mixed, totals = attend(length, proj, 0, half)
        mixed, totals, da_near, db_near = in_turn(mixed, totals, da_near, db_near)
        da, db = join(da, da_near), join(db, db_near)
        length, da, db, mixed, totals = in_turn(length, da, db, mixed, totals)
        da_far, db_far = far(da, db)
        mixed, totals = attend(length, proj, half, half, (mixed, totals))
        mixed, ra, rb, ra_far, rb_far, da, db, da_far, db_far = in_turn(
            mixed, ra, rb, ra_far, rb_far, da, db, da_far, db_far
        )
        rest_blocks = with_cores(ra, rb, ra_far, rb_far)
        downs = with_cores(da, db, da_far, db_far)
    else:
        mixed, totals = attend(lengths, proj)
    out_rows, active, d_inner, normed_two, d_resid, d_branch, d_mixed, sums = middle(
        lengths, table, patches, mixed, cotangent, vec, rest_blocks, downs, hidden, tile
    )
    down_keep, down_send = down_grads(lengths, table, active, cotangent)
    down_keep, down_send, d_inner = in_turn(down_keep, down_send, d_inner)
    up_keep, up_send = up_grads(table, d_inner, normed_two, d_branch, mixed)

    def back(length, first, count):
        return list(
            attend_back(length, proj, d_mixed, mixed, totals, first=first, count=count)
        )

    if fast:
        down_got = swap(down_send, "gy", 1, BLOCKS)
        up_got = swap(up_send, "gy", 1, BLOCKS)
        down_keep, down_got, up_keep = in_turn(down_keep, down_got, up_keep)
        down_next = add(down_keep[2:], down_got[2:]).astype(BF)
        length, down_next = in_turn(lengths, down_next)
        down_near = swap(down_next, "gx", 1, 4)
        d_parts = back(length, 0, 2)
        d_parts[0], up_keep, up_got = in_turn(d_parts[0], up_keep, up_got)
        up_sums = [add(up_keep[r], up_got[r]).astype(BF) for r in range(4)]
        length, *up_sums = in_turn(length, *up_sums)
        up_blocks = [swap(up_sums[r], "gy", MASKS_A[r], BLOCKS) for r in (1, 2, 3)]
        more = back(length, 2, 1)
        more[0], down_near, down_keep = in_turn(more[0], down_near, down_keep)
        d_parts += more
        down_sum = add(down_keep[0], down_got[0], down_near[0])
        down_next = add(down_keep[1], down_got[1], down_near[1]).astype(BF)
        length, down_next, down_sum = in_turn(length, down_next, down_sum)
        down_far = swap(down_next, "gx", 2, 4)
        more = back(length, 3, 3)
        more[0], down_far, *up_blocks = in_turn(more[0], down_far, *up_blocks)
        d_parts += more
        down_sums = [add(down_sum[r], down_far[r]).astype(BF) for r in range(4)]
        up_keep, up_send = fold(table, up_sums[:1] + up_blocks, True)
        table, up_keep, up_send, *down_sums = in_turn(table, up_keep, up_send, *down_sums)
        down_blocks = [swap(down_sums[r], "gy", MASKS_A[r], BLOCKS) for r in (1, 2, 3)]
        up_near = swap(up_send, "gx", 1, 4)
        qkv_keep, qkv_send = qkv_grads(table, d_parts, normed)
        qkv_keep, qkv_send, up_near, *down_blocks = in_turn(
            qkv_keep, qkv_send, up_near, *down_blocks
        )
        qkv_got = swap(qkv_send, "gy", 1, BLOCKS)
        grad_down = add(down_sums[0], *down_blocks).T
        up_sum = add(up_keep[0], up_near[0])
        up_next = add(up_keep[1], up_near[1]).astype(BF)
        qkv_keep, qkv_got, up_next = in_turn(qkv_keep, qkv_got, up_next)
        up_far = swap(up_next, "gx", 2, 4)
        qkv_sums = [add(qkv_keep[r], qkv_got[r]).astype(BF) for r in range(4)]
        table, grad_down, *qkv_sums = in_turn(table, grad_down, *qkv_sums)
        qkv_got = [swap(qkv_sums[r], "gy", MASKS_A[r], BLOCKS) for r in (1, 2, 3)]
        grad_rows, sums = last(table, d_parts, patches, d_resid, vec, sums, qkv_blocks, tile)
        up_far, sums = in_turn(up_far, sums)
        up_sum = add(up_sum, up_far)
        grad_up, grad_out = up_sum[:, :wide], up_sum[:, wide:]
        steps = (("gy", 1, 8), ("gy", 2, 8), ("gy", 4, 8), ("gx", 1, 4), ("gx", 2, 4))
        for axis, mask, size in steps[:3]:
            sums = sums + swap(sums, axis, mask, size)
        table, sums = in_turn(table, sums)
        qkv_pieces = fold(table, qkv_sums[:1] + qkv_got, False)
        sums, *qkv_pieces = in_turn(sums, *qkv_pieces)
        qkv_planes = [swap(qkv_pieces[k], "gx", k, 4) for k in (1, 2, 3)]
        for axis, mask, size in steps[3:]:
            sums = sums + swap(sums, axis, mask, size)
        sums, *qkv_planes = in_turn(sums, *qkv_planes)
        grad_qkv = add(qkv_pieces[0], *qkv_planes)
        device = z * columns + g
        own = lax.dynamic_slice(sums, (0, device * (narrow // 4)), (8, narrow // 4))
        own_up = lax.dynamic_slice(sums, (8 + z, g * narrow), (1, narrow))[0]
        own = [own[j] for j in range(8)]
    else:
        d_parts = back(lengths, 0, 2) + back(lengths, 2, 1) + back(lengths, 3, 3)
        qkv_keep, qkv_send = qkv_grads(table, d_parts, normed)
        grad_rows, sums = last(table, d_parts, patches, d_resid, vec, sums, qkv_blocks, tile)

        def spread(grads):
            part = lax.psum_scatter(grads, "gy", scatter_dimension=0, tiled=True)
            return lax.psum_scatter(part.T, "gx", scatter_dimension=0, tiled=True).astype(F32)

        rest = jnp.concatenate([up_keep, up_send], axis=0)
        grad_up = spread(rest[:, :wide].reshape(hidden, width))
        grad_out = spread(rest[:, wide:].reshape(width, width))
        down = jnp.stack([down_keep, down_send])[:, jnp.array(PLANES)]
        grad_down = spread(jnp.transpose(down, (0, 2, 3, 1, 4)).reshape(width, hidden))
        grad_qkv = spread(jnp.concatenate([qkv_keep, qkv_send]).reshape(3 * width, width))

        def share(vector):
            return lax.psum_scatter(vector, AXES, scatter_dimension=0, tiled=True)

        own = [share(sums[j]) for j in range(8)]
        own_up = share(sums[8:12].reshape(hidden))

    return (
        out_rows,
        grad_rows,
        grad_qkv,
        grad_out,
        grad_up,
        grad_down,
        own[0],
        own[1],
        own[2],
        own_up,
        own[3],
        own[4],
        own[5],
        own[6],
        own[7],
    )


def solution(mesh):
    by_rows = P(AXES, None)
    by_parts = P(AXES)
    matrix = P("gx", "gy")
    in_specs = (by_rows, by_parts, by_rows) + (matrix,) * 4 + (by_parts,) * 9
    out_specs = (by_rows, by_rows) + (matrix,) * 4 + (by_parts,) * 9
    body = functools.partial(per_device, planes=mesh.shape["gx"], columns=mesh.shape["gy"])
    return jax.shard_map(body, mesh=mesh, in_specs=in_specs, out_specs=out_specs, check_vma=False)
```
